32 devices in a mesh: groups: 2 (over y), shard: 16 (over z, x, core).
Axes of the slice: x: 2, y: 2, z: 4, core: 2. Of those that a mesh axis runs over, the one named last changes fastest.
Arguments:
- grad_out: bfloat16 [4, 4096, 2048], P('groups', 'shard'), parts along dimension 0, may hold values from -6 to 6
- saved_input: bfloat16 [4, 4096, 2048], P('groups', 'shard'), parts along dimension 0, may hold values from -6 to 6
- lengths: int32 [4], P('groups'), parts along dimension 0, may hold values from 1024 to 4096, as said below
- kernel: float32 [31, 2048], replicated, may hold values from -1 to 1
- gain: float32 [2048], replicated, may hold values from 0.1 to 1.9
- bias: float32 [2048], replicated, may hold values from -4 to 4
- proj_weight: bfloat16 [2048, 2048], P('shard'), may hold values from -0.125 to 0.125
Outputs:
- input_grad: bfloat16 [4, 4096, 2048], P('groups', 'shard'), parts along dimension 0
- proj_grad: float32 [4096, 2048], P(('groups', 'shard')), parts along dimension 0
- kernel_grad: float32 [62, 2048], P('groups', 'shard'), parts along dimension 0
- norm_grads: float32 [4, 2048], P('groups', 'shard'), parts along dimension 0
The draws below stay inside these ranges and needn't reach their ends.
There are 2 independent parts, one for each index of `groups`. The reference program is written for one: setup_inputs(seed, part) draws one part's arguments, and reference() takes and returns one part's arrays. A program takes and returns all parts, laid end to end along the dimension named above; an argument that names none is the same for every part. Nothing has to cross between parts.
Inputs may be any that keep to these rules, and one draw needn't show every extreme that they name: `lengths`: one utterance of every microbatch is live over all 4096 frames.
All inputs are finite; a program needn't handle non-finite values.
Results may differ from the reference program's by a relative error of at most 0.0051.
Values may be sent and summed in bfloat16 or wider, within the bound.
No kernel may reach another device: no remote copies, remote signals or barrier semaphores. Data moves between devices by JAX's collectives and lax.ppermute only.
A program may use at most 128 MiB of HBM per device.

```python
import jax
import jax.numpy as jnp
from jax import lax

D = 2048
KTAPS = 31
MICRO = 2
FRAMES = 4096
HALO = 15


def draw_lengths(key, part):
    first_key, second_key = jax.random.split(jax.random.fold_in(key, 7))
    shorter = jax.random.randint(first_key, (), FRAMES // 4, FRAMES + 1).astype(jnp.int32)
    which = jax.random.randint(second_key, (), 0, 2)
    full = jnp.full((), FRAMES, jnp.int32)
    return jnp.where(which == 0, jnp.stack([full, shorter]), jnp.stack([shorter, full])).astype(jnp.int32)


def shard_levels(stream_key, extent, cuts, smallest, largest):
    def one(dim, parts):
        draws = jax.random.uniform(jax.random.fold_in(jax.random.fold_in(stream_key, 6), dim), (parts,), jnp.float32, smallest / len(cuts), largest / len(cuts))
        return jnp.repeat(jnp.exp(draws), extent[dim] // parts).reshape((-1,) + (1,) * (len(extent) - dim - 1))

    level = one(*cuts[0])
    for cut in cuts[1:]:
        level = level * one(*cut)
    return level


def noise(rng, dims, spread, limit, shards=(), kind=jnp.bfloat16):
    level = shard_levels(rng, dims, shards, -0.22, 0.18) if shards else 1.0
    array = jax.random.normal(rng, dims, jnp.float32) * spread * level
    return jnp.minimum(jnp.maximum(array, -limit), limit).astype(kind)


def setup_inputs(seed: int = 0, part: int = 0) -> dict:
    key_of = jax.random.split(jax.random.key(seed), 8)
    part_keys = jax.random.split(jax.random.fold_in(key_of[7], part), 8)
    grad_out = noise(part_keys[0], (MICRO, FRAMES, D), 1.0, 6.0, ((1, 16),))
    saved_input = noise(part_keys[1], (MICRO, FRAMES, D), 1.0, 6.0, ((1, 16),))
    lengths = draw_lengths(jax.random.fold_in(jax.random.fold_in(key_of[7], part), 71), part)
    kernel = noise(key_of[3], (KTAPS, D), KTAPS ** -0.5, 1.0, (), jnp.float32)
    gain = jnp.clip(1.0 + 0.18 * jax.random.normal(key_of[4], (D,), jnp.float32), 0.1, 1.9)
    bias = noise(key_of[5], (D,), 1.0, 4.0, (), jnp.float32)
    proj_weight = noise(key_of[6], (D, D), D ** -0.5, 0.125, ((0, 16),))
    return dict(grad_out=grad_out, saved_input=saved_input, lengths=lengths, kernel=kernel, gain=gain, bias=bias, proj_weight=proj_weight)


def reference(grad_out, saved_input, lengths, kernel, gain, bias, proj_weight):
    live_frames = jnp.sum(lengths).astype(jnp.float32)
    norm_scale = lax.rsqrt(live_frames)
    position = jnp.arange(FRAMES, dtype=jnp.int32)
    proj_total = jnp.zeros((D, D), jnp.float32)
    kernel_total = jnp.zeros((KTAPS, D), jnp.float32)
    gain_total = jnp.zeros((D,), jnp.float32)
    bias_total = jnp.zeros((D,), jnp.float32)
    grads_in = []
    for batch in range(MICRO):
        live_mask = (position < lengths[batch])[:, None]
        masked_in = jnp.where(live_mask, saved_input[batch], jnp.zeros_like(saved_input[batch]))
        masked_grad = jnp.where(live_mask, grad_out[batch], jnp.zeros_like(grad_out[batch]))
        padded_in = jnp.pad(masked_in, ((HALO, HALO), (0, 0)))
        conv = jnp.zeros((FRAMES, D), jnp.float32)
        for index_tap in range(KTAPS):
            conv = conv + kernel[index_tap] * padded_in[index_tap:index_tap + FRAMES].astype(jnp.float32)
        pre_act = gain * conv + bias
        gate_sig = jax.nn.sigmoid(pre_act)
        activated = (pre_act * gate_sig).astype(jnp.bfloat16)
        act_grad = lax.dot_general(masked_grad, proj_weight, (((1,), (1,)), ((), ())), preferred_element_type=jnp.float32)
        pre_grad = act_grad * gate_sig * (1.0 + pre_act * (1.0 - gate_sig))
        conv_grad = (pre_grad * gain).astype(jnp.bfloat16)
        padded_grad = jnp.pad(conv_grad, ((HALO, HALO), (0, 0)))
        back_sum = jnp.zeros((FRAMES, D), jnp.float32)
        for index_tap in range(KTAPS):
            begin = 2 * HALO - index_tap
            back_sum = back_sum + kernel[index_tap] * padded_grad[begin:begin + FRAMES].astype(jnp.float32)
        grads_in.append(jnp.where(live_mask, back_sum, jnp.zeros_like(back_sum)).astype(jnp.bfloat16))
        proj_total = proj_total + lax.dot_general(activated, masked_grad, (((0,), (0,)), ((), ())), preferred_element_type=jnp.float32)
        grad_wide = conv_grad.astype(jnp.float32)
        tap_rows = []
        for index_tap in range(KTAPS):
            tap_rows.append(lax.optimization_barrier(jnp.sum(padded_in[index_tap:index_tap + FRAMES].astype(jnp.float32) * grad_wide, axis=0)))
        kernel_total = kernel_total + jnp.stack(tap_rows, 0)
        gain_total = gain_total + lax.optimization_barrier(jnp.sum(pre_grad * conv, axis=0))
        bias_total = bias_total + lax.optimization_barrier(jnp.sum(pre_grad, axis=0))
    input_grad = jnp.stack(grads_in, 0)
    norm_grads = jnp.stack([gain_total, bias_total], 0) * norm_scale
    return (input_grad, proj_total * norm_scale, kernel_total * norm_scale, norm_grads)
```

```python
import functools

import jax
import jax.numpy as jnp
from jax import lax
from jax.experimental import pallas as pl
from jax.experimental.pallas import tpu as pltpu
from jax.sharding import PartitionSpec as P

LANES = 128
CORES = 2
VMEM_LIMIT = 56 * 1024 * 1024


def extended(block, width):
    count = lax.axis_size("shard")
    forward = [(i, i + 1) for i in range(count - 1)]
    backward = [(target, source) for source, target in forward]
    low = lax.ppermute(block[:, block.shape[1] - width :], "shard", forward)
    high = lax.ppermute(block[:, :width], "shard", backward)
    return jnp.concatenate([low, block, high], axis=1)


def frame_mask(lengths, offset, count):
    position = offset + jnp.arange(count, dtype=jnp.int32)
    return (position[None, :] < lengths[:, None])[:, :, None]


def plain_shards(grad_out, saved_input, lengths, kernel, gain, bias, proj_weight):
    batches, frames, model_width = grad_out.shape
    tap_count = kernel.shape[0]
    half_span = (tap_count - 1) // 2
    offset = lax.axis_index("shard") * frames
    norm_scale = lax.rsqrt(jnp.sum(lengths).astype(jnp.float32))
    own_mask = frame_mask(lengths, offset, frames)
    masked_in = jnp.where(own_mask, saved_input, jnp.zeros_like(saved_input))
    masked_grad = jnp.where(own_mask, grad_out, jnp.zeros_like(grad_out))
    in_ext = extended(masked_in, half_span)
    conv = jnp.zeros(grad_out.shape, jnp.float32)
    for tap in range(tap_count):
        conv = conv + kernel[tap] * in_ext[:, tap : tap + frames].astype(jnp.float32)
    pre_act = gain * conv + bias
    gate_sig = jax.nn.sigmoid(pre_act)
    activated = (pre_act * gate_sig).astype(jnp.bfloat16)
    rows = masked_grad.reshape(batches * frames, model_width)
    weight = lax.all_gather(proj_weight, "shard", axis=0, tiled=True)
    act_grad = lax.dot_general(
        rows, weight, (((1,), (1,)), ((), ())), preferred_element_type=jnp.float32
    ).reshape(batches, frames, model_width)
    pre_grad = act_grad * gate_sig * (1.0 + pre_act * (1.0 - gate_sig))
    conv_grad = (pre_grad * gain).astype(jnp.bfloat16)
    grad_ext = extended(conv_grad, half_span)
    back_sum = jnp.zeros(grad_out.shape, jnp.float32)
    grad_float = conv_grad.astype(jnp.float32)
    tap_rows = []
    for tap in range(tap_count):
        begin = 2 * half_span - tap
        back_sum = back_sum + kernel[tap] * grad_ext[:, begin : begin + frames].astype(jnp.float32)
        tap_rows.append(
            jnp.sum(in_ext[:, tap : tap + frames].astype(jnp.float32) * grad_float, axis=(0, 1))
        )
    input_grad = jnp.where(own_mask, back_sum, 0.0).astype(jnp.bfloat16)
    tap_rows.append(jnp.sum(pre_grad * conv, axis=(0, 1)))
    tap_rows.append(jnp.sum(pre_grad, axis=(0, 1)))
    stats = jnp.stack(tap_rows, 0) * norm_scale
    summed = lax.psum_scatter(stats, "shard", scatter_dimension=1, tiled=True)
    product = lax.dot_general(
        activated.reshape(batches * frames, model_width),
        rows,
        (((0,), (0,)), ((), ())),
        preferred_element_type=jnp.float32,
    )
    proj_grad = lax.psum_scatter(product * norm_scale, "shard", scatter_dimension=0, tiled=True)
    return (input_grad, proj_grad, summed[:tap_count], summed[tap_count:])


class Plan:
    def __init__(self, count, batches, frames, model_width, tap_count):
        self.count = count
        self.chips = count // CORES
        self.rounds = self.chips // 2
        self.batches = batches
        self.frames = frames
        self.chip_frames = CORES * frames
        self.width = model_width
        self.block = model_width // count
        self.taps = tap_count
        self.half = (tap_count - 1) // 2
        self.ghalo = -(-self.half // 16) * 16
        self.xhalo = 2 * self.ghalo
        self.ext = self.chip_frames + 2 * self.ghalo
        self.xext = self.chip_frames + 2 * self.xhalo
        self.stat_rows = -(-(tap_count + 2) // 8) * 8
        vregs = self.ext // 8
        self.conv_rows = 8 * max(d for d in range(1, 18) if vregs % d == 0)

    def usable(self):
        return (
            self.count % (2 * CORES) == 0
            and self.block == LANES
            and self.block * self.count == self.width
            and self.frames % 128 == 0
            and self.frames >= self.xhalo
            and self.taps % 2 == 1
            and self.chips <= 16
        )

    def chip_at(self, position):
        half = self.chips // 2
        return jnp.where(position < half, 2 * position, 2 * (self.chips - 1 - position) + 1)

    def position_of(self, chip):
        return jnp.where(chip % 2 == 0, chip // 2, self.chips - 1 - chip // 2)

    def ring(self):
        half = self.chips // 2
        order = [2 * i for i in range(half)] + [2 * i + 1 for i in reversed(range(half))]
        forward = []
        for core in range(CORES):
            for i in range(self.chips):
                source, target = order[i], order[(i + 1) % self.chips]
                forward.append((CORES * source + core, CORES * target + core))
        return forward, [(t, s) for s, t in forward]

    def edges(self):
        pairs = []
        for chip in range(self.chips - 1):
            last, first = CORES * chip + 1, CORES * (chip + 1)
            pairs += [(last, first), (first, last)]
        return pairs

    def partners(self):
        return [(s, s ^ 1) for s in range(self.count)]


def sigmoid(value):
    return 0.5 * jnp.tanh(0.5 * value) + 0.5


def conv_body(plan, blk, info, x_ref, xp_ref, ha_ref, hb_ref, k_ref, gain_ref, bias_ref,
              conv_ref, act_ref, xs):
    core, offset = info[0], info[1]
    f, xh, gh = plan.frames, plan.xhalo, plan.ghalo

    def put(row, value, b):
        rows = value.shape[0]
        position = offset - xh + row + lax.broadcasted_iota(jnp.int32, (rows, LANES), 0)
        xs[b, row : row + rows, :] = jnp.where(
            position < info[2 + b], value.astype(jnp.float32), 0.0
        )

    for b in range(plan.batches):

        @pl.when(core == 0)
        def _():
            put(0, ha_ref[b, :xh], b)
            put(xh, x_ref[b], b)
            put(xh + f, xp_ref[b], b)
            put(xh + 2 * f, hb_ref[b, :xh], b)

        @pl.when(core != 0)
        def _():
            put(0, hb_ref[b, :xh], b)
            put(xh, xp_ref[b], b)
            put(xh + f, x_ref[b], b)
            put(xh + 2 * f, ha_ref[b, :xh], b)

    rows = plan.conv_rows
    shift = xh - gh - plan.half
    for b in range(plan.batches):

        def tile(i, carry):
            base = pl.multiple_of(i * rows, 8)
            total = jnp.zeros((rows, LANES), jnp.float32)
            for tap in range(plan.taps):
                total = total + k_ref[tap : tap + 1, :] * xs[b, pl.ds(base + (shift + tap), rows), :]
            conv_ref[0, b, pl.ds(base, rows), :] = total
            return carry

        lax.fori_loop(0, plan.ext // rows, tile, 0)

    for b in range(plan.batches):
        for i in range(plan.chip_frames // LANES):
            conv = conv_ref[0, b, gh + i * LANES : gh + (i + 1) * LANES, :]
            pre = gain_ref[...] * conv + bias_ref[...]
            act = (pre * sigmoid(pre)).T
            begin = b * plan.chip_frames + i * LANES
            act_ref[0, :, begin : begin + LANES] = act.astype(jnp.bfloat16)


def conv_call(plan, blk, info, x, xp, ha, hb, kernel, gain, bias):
    bt = plan.batches
    halo_rows = plan.xhalo + plan.ghalo
    by_block = lambda g, blk, info: (0, 0, blk[g])
    flat = lambda g, blk, info: (0, blk[g])
    return pl.pallas_call(
        functools.partial(conv_body, plan),
        grid_spec=pltpu.PrefetchScalarGridSpec(
            num_scalar_prefetch=2,
            grid=(2,),
            in_specs=[
                pl.BlockSpec((bt, plan.frames, LANES), by_block),
                pl.BlockSpec((bt, plan.frames, LANES), by_block),
                pl.BlockSpec((bt, halo_rows, LANES), by_block),
                pl.BlockSpec((bt, halo_rows, LANES), by_block),
                pl.BlockSpec((plan.taps, LANES), flat),
                pl.BlockSpec((1, LANES), flat),
                pl.BlockSpec((1, LANES), flat),
            ],
            out_specs=[
                pl.BlockSpec((1, bt, plan.ext, LANES), lambda g, blk, info: (g, 0, 0, 0)),
                pl.BlockSpec((1, LANES, bt * plan.chip_frames), lambda g, blk, info: (g, 0, 0)),
            ],
            scratch_shapes=[pltpu.VMEM((bt, plan.xext, LANES), jnp.float32)],
        ),
        out_shape=[
            jax.ShapeDtypeStruct((2, bt, plan.ext, LANES), jnp.float32),
            jax.ShapeDtypeStruct((2, LANES, bt * plan.chip_frames), jnp.bfloat16),
        ],
        compiler_params=pltpu.CompilerParams(vmem_limit_bytes=VMEM_LIMIT),
        name="conv",
    )(blk, info, x, xp, ha, hb, kernel, gain, bias)


def proj_body(plan, first, last, *refs):
    act_ref, mg_ref = refs[:2]
    recv = None if first else refs[2:4]
    out_f, out_b = refs[-2:]
    gh, cf = plan.ghalo, plan.chip_frames
    act = act_ref[...].reshape(2 * LANES, plan.batches * cf)
    total = None
    for b in range(plan.batches):
        part = jnp.dot(
            act[:, b * cf : (b + 1) * cf],
            mg_ref[b, gh : gh + cf, :],
            preferred_element_type=jnp.float32,
        )
        total = part if total is None else total + part
    for half, out in enumerate((out_f, out_b)):
        value = total[half * LANES : (half + 1) * LANES]
        if recv is not None:
            value = value + recv[half][...].astype(jnp.float32)
        out[...] = value.astype(out.dtype)


def proj_call(plan, act, mg, recv, last):
    columns = plan.width // 4
    wide = pl.BlockSpec((LANES, columns), lambda j: (0, j))
    shape = lambda kind: jax.ShapeDtypeStruct((LANES, plan.width), kind)
    return pl.pallas_call(
        functools.partial(proj_body, plan, recv is None, last),
        grid=(4,),
        in_specs=[
            pl.BlockSpec((2, LANES, plan.batches * plan.chip_frames), lambda j: (0, 0, 0)),
            pl.BlockSpec((plan.batches, plan.ext, columns), lambda j: (0, 0, j)),
        ]
        + [wide] * (0 if recv is None else 2),
        out_specs=[wide, wide],
        out_shape=[shape(jnp.bfloat16), shape(jnp.float32 if last else jnp.bfloat16)],
        compiler_params=pltpu.CompilerParams(vmem_limit_bytes=VMEM_LIMIT),
        name="proj",
    )(act, mg, *(() if recv is None else recv))


def back_body(plan, aliased, blk, info, *refs):
    mg_ref, wa_ref, wb_ref, conv_ref, x_ref, xp_ref, k_ref, gain_ref, bias_ref = refs[:9]
    own_ref, send_ref, stat_ref, ag, gs, xs, os, acc = refs[-8:]
    core, offset = info[0], info[1]
    f, gh, cf, ext = plan.frames, plan.ghalo, plan.chip_frames, plan.ext
    g = pl.program_id(0)

    @pl.when(g == 0)
    def _():
        weight = jnp.concatenate([wa_ref[...], wb_ref[...]], axis=0)
        for b in range(plan.batches):
            value = lax.dot_general(
                mg_ref[b], weight, (((1,), (1,)), ((), ())), preferred_element_type=jnp.float32
            )
            for half in range(2):
                ag[half, b] = value[:, half * LANES : (half + 1) * LANES]

    for b in range(plan.batches):
        def put(row, value, b=b):
            rows = value.shape[0]
            position = offset + row + lax.broadcasted_iota(jnp.int32, (rows, LANES), 0)
            xs[b, row : row + rows, :] = jnp.where(
                position < info[2 + b], value.astype(jnp.float32), 0.0
            )

        @pl.when(core == 0)
        def _():
            put(0, x_ref[b])
            put(f, xp_ref[b])

        @pl.when(core != 0)
        def _():
            put(0, xp_ref[b])
            put(f, x_ref[b])

    gain, bias = gain_ref[...], bias_ref[...]

    def pre_grad(b, begin, rows):
        conv = conv_ref[0, b, begin : begin + rows, :]
        pre = gain * conv + bias
        sig = sigmoid(pre)
        value = ag[g, b, begin : begin + rows, :] * sig * (1.0 + pre * (1.0 - sig))
        gs[b, begin : begin + rows, :] = (value * gain).astype(jnp.bfloat16).astype(jnp.float32)
        return value, conv

    gain_sum = jnp.zeros((8, LANES), jnp.float32)
    bias_sum = jnp.zeros((8, LANES), jnp.float32)
    for b in range(plan.batches):
        pre_grad(b, 0, gh)
        pre_grad(b, gh + cf, gh)
        step = 64
        for i in range(cf // step):
            value, conv = pre_grad(b, gh + i * step, step)
            gain_sum = gain_sum + jnp.sum((value * conv).reshape(step // 8, 8, LANES), axis=0)
            bias_sum = bias_sum + jnp.sum(value.reshape(step // 8, 8, LANES), axis=0)

    acc[...] = jnp.zeros_like(acc)
    rows = 64
    for b in range(plan.batches):

        def tile(i, carry):
            base = pl.multiple_of(i * rows, rows)
            x = xs[b, pl.ds(base, rows), :]
            total = jnp.zeros((rows, LANES), jnp.float32)
            for tap in range(plan.taps):
                shifted = gs[b, pl.ds(base + (gh + plan.half - tap), rows), :]
                total = total + k_ref[tap : tap + 1, :] * shifted
                acc[tap] += jnp.sum((x * shifted).reshape(rows // 8, 8, LANES), axis=0)
            position = offset + base + lax.broadcasted_iota(jnp.int32, (rows, LANES), 0)
            os[b, pl.ds(base, rows), :] = jnp.where(position < info[2 + b], total, 0.0).astype(
                jnp.bfloat16
            )
            return carry

        lax.fori_loop(0, cf // rows, tile, 0)

    @pl.when(core == 0)
    def _():
        own_ref[...] = os[:, :f]
        send_ref[0] = os[:, f:]

    @pl.when(core != 0)
    def _():
        own_ref[...] = os[:, f:]
        send_ref[0] = os[:, :f]

    for tap in range(plan.taps):
        stat_ref[0, tap : tap + 1, :] = jnp.sum(acc[tap], axis=0, keepdims=True)
    stat_ref[0, plan.taps : plan.taps + 1, :] = jnp.sum(gain_sum, axis=0, keepdims=True)
    stat_ref[0, plan.taps + 1 : plan.taps + 2, :] = jnp.sum(bias_sum, axis=0, keepdims=True)
    if plan.stat_rows > plan.taps + 2:
        stat_ref[0, plan.taps + 2 :, :] = jnp.zeros(
            (plan.stat_rows - plan.taps - 2, LANES), jnp.float32
        )


def back_call(plan, blk, info, mg, wa, wb, conv, x, xp, kernel, gain, bias, full):
    bt = plan.batches
    by_block = lambda g, blk, info: (0, 0, blk[g])
    flat = lambda g, blk, info: (0, blk[g])
    fixed2 = lambda g, blk, info: (0, 0)
    one = pl.Buffered(1)
    in_specs = [
        pl.BlockSpec((bt, plan.ext, plan.width), lambda g, blk, info: (0, 0, 0), pipeline_mode=one),
        pl.BlockSpec((LANES, plan.width), fixed2, pipeline_mode=one),
        pl.BlockSpec((LANES, plan.width), fixed2, pipeline_mode=one),
        pl.BlockSpec((1, bt, plan.ext, LANES), lambda g, blk, info: (g, 0, 0, 0)),
        pl.BlockSpec((bt, plan.frames, LANES), by_block),
        pl.BlockSpec((bt, plan.frames, LANES), by_block),
        pl.BlockSpec((plan.taps, LANES), flat),
        pl.BlockSpec((1, LANES), flat),
        pl.BlockSpec((1, LANES), flat),
    ]
    operands = [mg, wa, wb, conv, x, xp, kernel, gain, bias]
    aliases = {}
    if full is not None:
        in_specs.append(pl.BlockSpec(memory_space=pl.ANY))
        operands.append(full)
        aliases = {2 + len(operands) - 1: 0}
    return pl.pallas_call(
        functools.partial(back_body, plan, full is not None),
        grid_spec=pltpu.PrefetchScalarGridSpec(
            num_scalar_prefetch=2,
            grid=(2,),
            in_specs=in_specs,
            out_specs=[
                pl.BlockSpec((bt, plan.frames, LANES), by_block),
                pl.BlockSpec((1, bt, plan.frames, LANES), lambda g, blk, info: (g, 0, 0, 0)),
                pl.BlockSpec((1, plan.stat_rows, LANES), lambda g, blk, info: (g, 0, 0)),
            ],
            scratch_shapes=[
                pltpu.VMEM((2, bt, plan.ext, LANES), jnp.float32),
                pltpu.VMEM((bt, plan.ext, LANES), jnp.float32),
                pltpu.VMEM((bt, plan.chip_frames, LANES), jnp.float32),
                pltpu.VMEM((bt, plan.chip_frames, LANES), jnp.bfloat16),
                pltpu.VMEM((plan.taps, 8, LANES), jnp.float32),
            ],
        ),
        out_shape=[
            jax.ShapeDtypeStruct((bt, plan.frames, plan.width), jnp.bfloat16),
            jax.ShapeDtypeStruct((2, bt, plan.frames, LANES), jnp.bfloat16),
            jax.ShapeDtypeStruct((2, plan.stat_rows, LANES), jnp.float32),
        ],
        input_output_aliases=aliases,
        compiler_params=pltpu.CompilerParams(vmem_limit_bytes=VMEM_LIMIT),
        name="back",
    )(blk, info, *operands)


def place_body(blk, recv_ref, full_ref, out_ref):
    out_ref[...] = recv_ref[0]


def place_call(plan, blk, recv, full):
    count = recv.shape[0]
    bt = plan.batches
    return pl.pallas_call(
        place_body,
        grid_spec=pltpu.PrefetchScalarGridSpec(
            num_scalar_prefetch=1,
            grid=(count,),
            in_specs=[
                pl.BlockSpec((1, bt, plan.frames, LANES), lambda g, blk: (g, 0, 0, 0)),
                pl.BlockSpec(memory_space=pl.ANY),
            ],
            out_specs=pl.BlockSpec((bt, plan.frames, LANES), lambda g, blk: (0, 0, blk[g])),
        ),
        out_shape=jax.ShapeDtypeStruct(full.shape, full.dtype),
        input_output_aliases={2: 0},
        name="place",
    )(blk, recv, full)


def ring_shards(plan, grad_out, saved_input, lengths, kernel, gain, bias, proj_weight):
    f, xh, gh = plan.frames, plan.xhalo, plan.ghalo
    index = lax.axis_index("shard")
    core = index % CORES
    chip = index // CORES
    place = plan.position_of(chip)
    forward, backward = plan.ring()
    offset = chip * plan.chip_frames
    scale = lax.rsqrt(jnp.sum(lengths).astype(jnp.float32))
    info = jnp.concatenate([jnp.stack([core, offset]), lengths]).astype(jnp.int32)
    gain2, bias2 = gain.reshape(1, -1), bias.reshape(1, -1)

    edge = jnp.concatenate(
        [
            jnp.where(core == 1, saved_input[:, f - xh :], saved_input[:, :xh]),
            jnp.where(core == 1, grad_out[:, f - gh :], grad_out[:, :gh]),
        ],
        axis=1,
    )
    xp = lax.ppermute(saved_input, "shard", plan.partners())
    ha = lax.ppermute(edge, "shard", plan.edges())
    mgp = lax.ppermute(grad_out, "shard", plan.partners())
    hb = lax.ppermute(ha, "shard", plan.partners())

    weights = {0: proj_weight}
    going_f = going_b = proj_weight
    for step in range(1, plan.rounds + 1):
        going_f = lax.ppermute(going_f, "shard", forward)
        weights[-step] = going_f
        if step < plan.rounds:
            going_b = lax.ppermute(going_b, "shard", backward)
            weights[step] = going_b
    weights[plan.rounds] = weights.pop(-plan.rounds)

    first = core == 0
    low, high = jnp.where(first, ha, hb), jnp.where(first, hb, ha)
    mg = jnp.concatenate(
        [
            low[:, xh:],
            jnp.where(first, grad_out, mgp),
            jnp.where(first, mgp, grad_out),
            high[:, xh:],
        ],
        axis=1,
    )
    mg = jnp.where(frame_mask(lengths, offset - gh, plan.ext), mg, jnp.zeros_like(mg))

    def blocks(pair, owner):
        chips = [plan.chip_at((place + d) % plan.chips) for d in pair]
        return jnp.stack([CORES * c + owner for c in chips]).astype(jnp.int32)

    pairs = [(h, 1 - h) for h in range(plan.rounds, 0, -1)]
    convs, acts = [], []
    for pair in pairs:
        conv, act = conv_call(
            plan, blocks(pair, core), info, saved_input, xp, ha, hb, kernel, gain2, bias2
        )
        convs.append(conv)
        acts.append(act)

    recv = None
    for step, pair in enumerate(pairs):
        last = step == plan.rounds - 1
        send_f, send_b = proj_call(plan, acts[step], mg, recv, last)
        recv_f = lax.ppermute(send_f, "shard", forward)
        if not last:
            recv = (recv_f, lax.ppermute(send_b, "shard", backward))
    proj_grad = (send_b + recv_f.astype(jnp.float32)) * scale

    full, sends, stats = None, [], {}
    for step in reversed(range(plan.rounds)):
        pair = pairs[step]
        full, send, stat = back_call(
            plan, blocks(pair, core), info, mg, weights[pair[0]], weights[pair[1]],
            convs[step], saved_input, xp, kernel, gain2, bias2, full,
        )
        sends.append((pair, send))
        for half, d in enumerate(pair):
            stats[d % plan.chips] = stat[half]
    for pair, send in sends:
        full = place_call(
            plan, blocks(pair, 1 - core), lax.ppermute(send, "shard", plan.partners()), full
        )

    stacked = jnp.stack([stats[d] for d in range(plan.chips)], 0)
    order = (plan.position_of(jnp.arange(plan.chips)) - place) % plan.chips
    stacked = jnp.take(stacked, order, axis=0)
    groups = [[CORES * p + c for p in range(plan.chips)] for c in range(CORES)]
    parts = lax.all_to_all(stacked, "shard", 0, 0, axis_index_groups=groups)
    summed = jnp.sum(parts, axis=0) * scale
    return (full, proj_grad, summed[: plan.taps], summed[plan.taps : plan.taps + 2])


def shards(count, grad_out, saved_input, lengths, kernel, gain, bias, proj_weight):
    batches, frames, model_width = grad_out.shape
    plan = Plan(count, batches, frames, model_width, kernel.shape[0])
    args = (grad_out, saved_input, lengths, kernel, gain, bias, proj_weight)
    return ring_shards(plan, *args) if plan.usable() else plain_shards(*args)


def solution(mesh):
    placed = (
        P("groups", "shard", None),
        P("groups", "shard", None),
        P("groups"),
        P(),
        P(),
        P(),
        P("shard", None),
    )
    return jax.shard_map(
        functools.partial(shards, mesh.shape["shard"]),
        mesh=mesh,
        in_specs=placed,
        out_specs=(
            P("groups", "shard", None),
            P(("groups", "shard"), None),
            P("groups", "shard"),
            P("groups", "shard"),
        ),
        check_vma=False,
    )
```

```python
import functools

import jax
import jax.numpy as jnp
import numpy as np
from jax import lax
from jax.experimental import pallas as pl
from jax.experimental.pallas import tpu as pltpu
from jax.sharding import PartitionSpec as P

LANES = 128
CORES = 2
VMEM_LIMIT = 56 * 1024 * 1024
POINTS = 256


def cost(micros):
    return pl.CostEstimate(flops=0, transcendentals=0, bytes_accessed=int(micros * 3.6e6))


def extended(block, width):
    count = lax.axis_size("shard")
    forward = [(i, i + 1) for i in range(count - 1)]
    backward = [(target, source) for source, target in forward]
    low = lax.ppermute(block[:, block.shape[1] - width :], "shard", forward)
    high = lax.ppermute(block[:, :width], "shard", backward)
    return jnp.concatenate([low, block, high], axis=1)


def frame_mask(lengths, offset, count):
    position = offset + jnp.arange(count, dtype=jnp.int32)
    return (position[None, :] < lengths[:, None])[:, :, None]


def plain_shards(grad_out, saved_input, lengths, kernel, gain, bias, proj_weight):
    batches, frames, model_width = grad_out.shape
    tap_count = kernel.shape[0]
    half_span = (tap_count - 1) // 2
    offset = lax.axis_index("shard") * frames
    norm_scale = lax.rsqrt(jnp.sum(lengths).astype(jnp.float32))
    own_mask = frame_mask(lengths, offset, frames)
    masked_in = jnp.where(own_mask, saved_input, jnp.zeros_like(saved_input))
    masked_grad = jnp.where(own_mask, grad_out, jnp.zeros_like(grad_out))
    in_ext = extended(masked_in, half_span)
    conv = jnp.zeros(grad_out.shape, jnp.float32)
    for tap in range(tap_count):
        conv = conv + kernel[tap] * in_ext[:, tap : tap + frames].astype(jnp.float32)
    pre_act = gain * conv + bias
    gate_sig = jax.nn.sigmoid(pre_act)
    activated = (pre_act * gate_sig).astype(jnp.bfloat16)
    rows = masked_grad.reshape(batches * frames, model_width)
    weight = lax.all_gather(proj_weight, "shard", axis=0, tiled=True)
    act_grad = lax.dot_general(
        rows, weight, (((1,), (1,)), ((), ())), preferred_element_type=jnp.float32
    ).reshape(batches, frames, model_width)
    pre_grad = act_grad * gate_sig * (1.0 + pre_act * (1.0 - gate_sig))
    conv_grad = (pre_grad * gain).astype(jnp.bfloat16)
    grad_ext = extended(conv_grad, half_span)
    back_sum = jnp.zeros(grad_out.shape, jnp.float32)
    grad_float = conv_grad.astype(jnp.float32)
    tap_rows = []
    for tap in range(tap_count):
        begin = 2 * half_span - tap
        back_sum = back_sum + kernel[tap] * grad_ext[:, begin : begin + frames].astype(jnp.float32)
        tap_rows.append(
            jnp.sum(in_ext[:, tap : tap + frames].astype(jnp.float32) * grad_float, axis=(0, 1))
        )
    input_grad = jnp.where(own_mask, back_sum, 0.0).astype(jnp.bfloat16)
    tap_rows.append(jnp.sum(pre_grad * conv, axis=(0, 1)))
    tap_rows.append(jnp.sum(pre_grad, axis=(0, 1)))
    stats = jnp.stack(tap_rows, 0) * norm_scale
    summed = lax.psum_scatter(stats, "shard", scatter_dimension=1, tiled=True)
    product = lax.dot_general(
        activated.reshape(batches * frames, model_width),
        rows,
        (((0,), (0,)), ((), ())),
        preferred_element_type=jnp.float32,
    )
    proj_grad = lax.psum_scatter(product * norm_scale, "shard", scatter_dimension=0, tiled=True)
    return (input_grad, proj_grad, summed[:tap_count], summed[tap_count:])


class Plan:
    def __init__(self, count, batches, frames, model_width, tap_count):
        self.count = count
        self.chips = count // CORES
        self.rounds = self.chips // 2
        self.batches = batches
        self.frames = frames
        self.chip_frames = CORES * frames
        self.width = model_width
        self.block = model_width // count
        self.taps = tap_count
        self.half = (tap_count - 1) // 2
        self.ghalo = -(-self.half // 16) * 16
        self.xhalo = 2 * self.ghalo
        self.ext = self.chip_frames + 2 * self.ghalo
        self.xext = self.chip_frames + 2 * self.xhalo
        self.tap_rows = -(-tap_count // 16) * 16
        self.stat_rows = self.tap_rows + 8

    def usable(self):
        return (
            self.count % (2 * CORES) == 0
            and self.block == LANES
            and self.block * self.count == self.width
            and self.frames % 128 == 0
            and self.frames >= self.xhalo
            and self.taps % 2 == 1
            and 4 * self.ghalo <= POINTS // 2
            and self.ext >= POINTS
            and self.chips <= 16
        )

    def chip_at(self, position):
        half = self.chips // 2
        return jnp.where(position < half, 2 * position, 2 * (self.chips - 1 - position) + 1)

    def position_of(self, chip):
        return jnp.where(chip % 2 == 0, chip // 2, self.chips - 1 - chip // 2)

    def ring(self):
        half = self.chips // 2
        order = [2 * i for i in range(half)] + [2 * i + 1 for i in reversed(range(half))]
        forward = []
        for core in range(CORES):
            for i in range(self.chips):
                source, target = order[i], order[(i + 1) % self.chips]
                forward.append((CORES * source + core, CORES * target + core))
        return forward, [(t, s) for s, t in forward]

    def edges(self):
        pairs = []
        for chip in range(self.chips - 1):
            last, first = CORES * chip + 1, CORES * (chip + 1)
            pairs += [(last, first), (first, last)]
        return pairs

    def partners(self):
        return [(s, s ^ 1) for s in range(self.count)]


def sigmoid(value):
    return 0.5 * jnp.tanh(0.5 * value) + 0.5


def split(value):
    high = value.astype(jnp.bfloat16)
    return high, (value - high.astype(jnp.float32)).astype(jnp.bfloat16)


def split_matrix(matrix):
    high = matrix.astype(jnp.bfloat16)
    return high, (matrix - high.astype(np.float64)).astype(jnp.bfloat16)


def transforms(plan):
    time = np.arange(POINTS)
    theta = np.pi * (2 * np.arange(POINTS // 2) + 1) / POINTS
    angle = theta[:, None] * time[None, :]
    direct = np.concatenate([np.cos(angle), -np.sin(angle)], 0)
    inverse = direct.T * (2.0 / POINTS)

    def spectrum(lags):
        phase = theta[:, None] * lags[None, :]
        matrix = np.concatenate([np.cos(phase), np.sin(phase)], 0)
        return np.pad(matrix, ((0, 0), (0, plan.tap_rows - plan.taps)))

    taps = np.arange(plan.taps)
    back_lags = plan.ghalo + plan.half - taps
    lag_rows = np.pad(inverse[back_lags], ((0, plan.tap_rows - plan.taps), (0, 0)))
    double = lambda m: np.concatenate(split_matrix(m), 1)

    def triple(m):
        high, low = split_matrix(m)
        return np.concatenate([high, low, high], 1)

    conv_lags = plan.xhalo - plan.ghalo - plan.half + taps
    return (
        double(direct),
        triple(inverse),
        np.stack(split_matrix(spectrum(conv_lags))),
        np.stack(split_matrix(spectrum(back_lags))),
        triple(lag_rows),
    )


def taps_spectrum(t_ref, k_ref):
    high, low = split(jnp.concatenate([k_ref[0][...], k_ref[1][...]], axis=1))
    dot = functools.partial(jnp.dot, preferred_element_type=jnp.float32)
    return dot(t_ref[0], high) + dot(t_ref[1], high) + dot(t_ref[0], low)


def to_spectrum(direct_ref, window):
    return jnp.dot(
        direct_ref[...], jnp.concatenate([window, window], 0), preferred_element_type=jnp.float32
    )


def from_spectrum(inverse_ref, rows, parts):
    return jnp.dot(inverse_ref[rows, :], parts[...], preferred_element_type=jnp.float32)


def store_parts(parts, row, value):
    high, low = split(value)
    rows = value.shape[0]
    parts[row : row + rows, :] = high
    parts[POINTS + row : POINTS + row + rows, :] = high
    parts[2 * POINTS + row : 2 * POINTS + row + rows, :] = low


def windows(rows_in, rows_out, reach):
    count = -(-rows_out // ((POINTS - reach) // 16 * 16))
    each = -(-rows_out // count // 16) * 16
    found = []
    for begin in range(0, rows_out, each):
        start = min(begin, rows_in - POINTS)
        found.append((start, begin, min(each, rows_out - begin), begin - start))
    return found


STEP = 16
HALF = POINTS // 2


def conv_body(plan, blk, info, *refs):
    x_ref, xp_ref, ha_ref, hb_ref, k_ref, gain_ref, bias_ref = (
        refs[2 * i : 2 * i + 2] for i in range(7)
    )
    direct, inverse, t_ref, conv_ref, act_ref, xs, spec, taps, parts = refs[14:]
    core, offset = info[0], info[1]
    f, xh, gh = plan.frames, plan.xhalo, plan.ghalo
    live = info[2 + pl.program_id(0)]

    def put(row, ref, rows):
        position = offset - xh + row + lax.broadcasted_iota(jnp.int32, (rows, LANES), 0)
        for side in range(2):
            value = jnp.where(position < live, ref[side][0, :rows].astype(jnp.float32), 0.0)
            xs[row : row + rows, side * LANES : (side + 1) * LANES] = value.astype(jnp.bfloat16)

    @pl.when(core == 0)
    def _():
        put(0, ha_ref, xh)
        put(xh, x_ref, f)
        put(xh + f, xp_ref, f)
        put(xh + 2 * f, hb_ref, xh)

    @pl.when(core != 0)
    def _():
        put(0, hb_ref, xh)
        put(xh, xp_ref, f)
        put(xh + f, x_ref, f)
        put(xh + 2 * f, ha_ref, xh)

    taps[...] = taps_spectrum(t_ref, k_ref)
    reach = xh - gh - plan.half + plan.taps
    for start, begin, count, first in windows(plan.xext, plan.ext, reach):
        spec[...] = to_spectrum(direct, xs[start : start + POINTS, :])
        for row in range(0, HALF, STEP):
            re, im = spec[row : row + STEP, :], spec[HALF + row : HALF + row + STEP, :]
            kr, ks = taps[row : row + STEP, :], taps[HALF + row : HALF + row + STEP, :]
            store_parts(parts, row, re * kr - im * ks)
            store_parts(parts, HALF + row, re * ks + im * kr)
        conv_ref[0, begin : begin + count, :] = from_spectrum(
            inverse, slice(first, first + count), parts
        )

    for i in range(plan.chip_frames // LANES):
        for side in range(2):
            lanes = slice(side * LANES, (side + 1) * LANES)
            conv = conv_ref[0, gh + i * LANES : gh + (i + 1) * LANES, lanes]
            pre = gain_ref[side][...] * conv + bias_ref[side][...]
            act_ref[lanes, i * LANES : (i + 1) * LANES] = (pre * sigmoid(pre)).T.astype(
                jnp.bfloat16
            )


def pair_specs(shape, index):
    return [
        pl.BlockSpec(shape, lambda b, blk, info, side=side: index(b, blk[side]))
        for side in range(2)
    ]


def whole(array):
    return pl.BlockSpec(
        array.shape, lambda *_: (0,) * array.ndim, pipeline_mode=pl.Buffered(1)
    )


def conv_call(plan, blk, info, x, xp, ha, hb, kernel, gain, bias, consts):
    bt = plan.batches
    halo_rows = plan.xhalo + plan.ghalo
    by_batch = lambda b, block: (b, 0, block)
    flat = lambda b, block: (0, block)
    frames, halo = (1, plan.frames, LANES), (1, halo_rows, LANES)
    direct, inverse, t_conv = consts[:3]
    return pl.pallas_call(
        functools.partial(conv_body, plan),
        grid_spec=pltpu.PrefetchScalarGridSpec(
            num_scalar_prefetch=2,
            grid=(bt,),
            in_specs=pair_specs(frames, by_batch)
            + pair_specs(frames, by_batch)
            + pair_specs(halo, by_batch)
            + pair_specs(halo, by_batch)
            + pair_specs((plan.tap_rows, LANES), flat)
            + pair_specs((1, LANES), flat)
            + pair_specs((1, LANES), flat)
            + [whole(direct), whole(inverse), whole(t_conv)],
            out_specs=[
                pl.BlockSpec((1, plan.ext, 2 * LANES), lambda b, blk, info: (b, 0, 0)),
                pl.BlockSpec((2 * LANES, plan.chip_frames), lambda b, blk, info: (0, b)),
            ],
            scratch_shapes=[
                pltpu.VMEM((plan.xext, 2 * LANES), jnp.bfloat16),
                pltpu.VMEM((POINTS, 2 * LANES), jnp.float32),
                pltpu.VMEM((POINTS, 2 * LANES), jnp.float32),
                pltpu.VMEM((3 * POINTS, 2 * LANES), jnp.bfloat16),
            ],
        ),
        out_shape=[
            jax.ShapeDtypeStruct((bt, plan.ext, 2 * LANES), jnp.float32),
            jax.ShapeDtypeStruct((2 * LANES, bt * plan.chip_frames), jnp.bfloat16),
        ],
        compiler_params=pltpu.CompilerParams(vmem_limit_bytes=VMEM_LIMIT),
        cost_estimate=cost(3.0),
        name="conv",
    )(blk, info, x, x, xp, xp, ha, ha, hb, hb, kernel, kernel, gain, gain, bias, bias,
      direct, inverse, t_conv)


def proj_body(plan, first, last, *refs):
    act_ref, mg_ref = refs[:2]
    recv = None if first else refs[2:4]
    out_f, out_b = refs[-2:]
    gh, cf = plan.ghalo, plan.chip_frames
    act = act_ref[...]
    total = None
    for b in range(plan.batches):
        part = jnp.dot(
            act[:, b * cf : (b + 1) * cf],
            mg_ref[b, gh : gh + cf, :],
            preferred_element_type=jnp.float32,
        )
        total = part if total is None else total + part
    for half, out in enumerate((out_f, out_b)):
        value = total[half * LANES : (half + 1) * LANES]
        if recv is not None:
            value = value + recv[half][...].astype(jnp.float32)
        out[...] = value.astype(out.dtype)


def proj_call(plan, act, mg, recv, last):
    columns = plan.width // 4
    wide = pl.BlockSpec((LANES, columns), lambda j: (0, j))
    shape = lambda kind: jax.ShapeDtypeStruct((LANES, plan.width), kind)
    return pl.pallas_call(
        functools.partial(proj_body, plan, recv is None, last),
        grid=(4,),
        in_specs=[
            whole(act),
            pl.BlockSpec((plan.batches, plan.ext, columns), lambda j: (0, 0, j)),
        ]
        + [wide] * (0 if recv is None else 2),
        out_specs=[wide, wide],
        out_shape=[shape(jnp.bfloat16), shape(jnp.float32 if last else jnp.bfloat16)],
        compiler_params=pltpu.CompilerParams(vmem_limit_bytes=VMEM_LIMIT),
        cost_estimate=cost(5.0),
        name="proj",
    )(act, mg, *(() if recv is None else recv))


def back_body(plan, blk, info, *refs):
    x_ref, xp_ref, k_ref, gain_ref, bias_ref, w_ref = (refs[2 * i : 2 * i + 2] for i in range(6))
    mg_ref, conv_ref, direct, inverse, t_ref, lag_ref = refs[12:18]
    own_ref, send_ref, stat_ref, ag, gs, xs, spec, xspec, taps, cross, parts, os, sums = refs[18:]
    core, offset = info[0], info[1]
    f, gh, cf, ext = plan.frames, plan.ghalo, plan.chip_frames, plan.ext
    b = pl.program_id(0)
    live = info[2 + b]

    @pl.when(b == 0)
    def _():
        taps[...] = taps_spectrum(t_ref, k_ref)
        cross[...] = jnp.zeros_like(cross)
        sums[...] = jnp.zeros_like(sums)

    weight = jnp.concatenate([w_ref[0][...], w_ref[1][...]], axis=0)
    ag[...] = lax.dot_general(
        mg_ref[0], weight, (((1,), (1,)), ((), ())), preferred_element_type=jnp.float32
    )
    gain = jnp.concatenate([gain_ref[0][...], gain_ref[1][...]], axis=1)
    bias = jnp.concatenate([bias_ref[0][...], bias_ref[1][...]], axis=1)

    gain_sum = jnp.zeros((8, 2 * LANES), jnp.float32)
    bias_sum = jnp.zeros((8, 2 * LANES), jnp.float32)
    for row in range(0, ext, STEP):
        conv = conv_ref[0, row : row + STEP, :]
        pre = gain * conv + bias
        sig = sigmoid(pre)
        value = ag[row : row + STEP, :] * sig * (1.0 + pre * (1.0 - sig))
        gs[row : row + STEP, :] = (value * gain).astype(jnp.bfloat16)
        if gh <= row < gh + cf:
            fold = lambda v: jnp.sum(v.reshape(STEP // 8, 8, 2 * LANES), axis=0)
            gain_sum = gain_sum + fold(value * conv)
            bias_sum = bias_sum + fold(value)
    sums[0] += gain_sum
    sums[1] += bias_sum

    spans = windows(ext, cf, gh + plan.half + 1)
    xs[...] = jnp.zeros_like(xs)

    def put(row, ref):
        for j, (start, begin, count, first) in enumerate(spans):
            low, high = max(begin, row), min(begin + count, row + f)
            if low >= high:
                continue
            rows = high - low
            position = offset + low + lax.broadcasted_iota(jnp.int32, (rows, LANES), 0)
            for side in range(2):
                value = ref[side][0, low - row : high - row].astype(jnp.float32)
                value = jnp.where(position < live, value, 0.0).astype(jnp.bfloat16)
                lanes = slice(side * LANES, (side + 1) * LANES)
                xs[j, low - start : high - start, lanes] = value

    @pl.when(core == 0)
    def _():
        put(0, x_ref)
        put(f, xp_ref)

    @pl.when(core != 0)
    def _():
        put(0, xp_ref)
        put(f, x_ref)

    for j, (start, begin, count, first) in enumerate(spans):
        spec[...] = to_spectrum(direct, gs[start : start + POINTS, :])
        xspec[...] = to_spectrum(direct, xs[j])
        for row in range(0, HALF, STEP):
            up, down = slice(row, row + STEP), slice(HALF + row, HALF + row + STEP)
            re, im, kr, ks = spec[up, :], spec[down, :], taps[up, :], taps[down, :]
            store_parts(parts, row, re * kr - im * ks)
            store_parts(parts, HALF + row, re * ks + im * kr)
            xr, xi = xspec[up, :], xspec[down, :]
            cross[up, :] += re * xr + im * xi
            cross[down, :] += im * xr - re * xi
        value = from_spectrum(inverse, slice(first, first + count), parts)
        position = offset + begin + lax.broadcasted_iota(jnp.int32, value.shape, 0)
        os[begin : begin + count, :] = jnp.where(position < live, value, 0.0).astype(jnp.bfloat16)

    @pl.when(core == 0)
    def _():
        own_ref[0] = os[:f]
        send_ref[0] = os[f:]

    @pl.when(core != 0)
    def _():
        own_ref[0] = os[f:]
        send_ref[0] = os[:f]

    @pl.when(b == plan.batches - 1)
    def _():
        for row in range(0, POINTS, STEP):
            store_parts(parts, row, cross[row : row + STEP, :])
        stat_ref[: plan.tap_rows] = from_spectrum(lag_ref, slice(0, plan.tap_rows), parts)
        total = [jnp.sum(sums[i], axis=0, keepdims=True) for i in range(2)]
        pad = jnp.zeros((plan.stat_rows - plan.tap_rows - 2, 2 * LANES), jnp.float32)
        stat_ref[plan.tap_rows :] = jnp.concatenate(total + [pad], axis=0)


def back_call(plan, blk, info, mg, wa, wb, conv, x, xp, kernel, gain, bias, consts):
    bt = plan.batches
    by_batch = lambda b, block: (b, 0, block)
    flat = lambda b, block: (0, block)
    batch = lambda b, blk, info: (b, 0, 0)
    frames = (1, plan.frames, LANES)
    direct, inverse, _, t_back, lags = consts
    pair = (1, plan.frames, 2 * LANES)
    wide = 2 * LANES
    return pl.pallas_call(
        functools.partial(back_body, plan),
        grid_spec=pltpu.PrefetchScalarGridSpec(
            num_scalar_prefetch=2,
            grid=(bt,),
            in_specs=pair_specs(frames, by_batch)
            + pair_specs(frames, by_batch)
            + pair_specs((plan.tap_rows, LANES), flat)
            + pair_specs((1, LANES), flat)
            + pair_specs((1, LANES), flat)
            + [whole(wa), whole(wb)]
            + [pl.BlockSpec((1, plan.ext, plan.width), batch)]
            + [pl.BlockSpec((1, plan.ext, wide), batch)]
            + [whole(direct), whole(inverse), whole(t_back), whole(lags)],
            out_specs=[
                pl.BlockSpec(pair, batch),
                pl.BlockSpec(pair, batch),
                pl.BlockSpec((plan.stat_rows, wide), lambda b, blk, info: (0, 0)),
            ],
            scratch_shapes=[
                pltpu.VMEM((plan.ext, wide), jnp.float32),
                pltpu.VMEM((plan.ext, wide), jnp.bfloat16),
                pltpu.VMEM(
                    (len(windows(plan.ext, plan.chip_frames, plan.ghalo + plan.half + 1)),
                     POINTS, wide), jnp.bfloat16),
                pltpu.VMEM((POINTS, wide), jnp.float32),
                pltpu.VMEM((POINTS, wide), jnp.float32),
                pltpu.VMEM((POINTS, wide), jnp.float32),
                pltpu.VMEM((POINTS, wide), jnp.float32),
                pltpu.VMEM((3 * POINTS, wide), jnp.bfloat16),
                pltpu.VMEM((plan.chip_frames, wide), jnp.bfloat16),
                pltpu.VMEM((2, 8, wide), jnp.float32),
            ],
        ),
        out_shape=[
            jax.ShapeDtypeStruct((bt, plan.frames, wide), jnp.bfloat16),
            jax.ShapeDtypeStruct((bt, plan.frames, wide), jnp.bfloat16),
            jax.ShapeDtypeStruct((plan.stat_rows, wide), jnp.float32),
        ],
        compiler_params=pltpu.CompilerParams(vmem_limit_bytes=VMEM_LIMIT),
        cost_estimate=cost(5.0),
        name="back",
    )(blk, info, x, x, xp, xp, kernel, kernel, gain, gain, bias, bias, wa, wb, mg, conv,
      direct, inverse, t_back, lags)


def place_body(plan, blk, *refs):
    out_ref, sem = refs[-2:]
    copies = []
    for i, ref in enumerate(refs[:-2]):
        for side in range(2):
            column = pl.multiple_of(blk[2 * i + side] * LANES, LANES)
            copies.append(
                pltpu.make_async_copy(
                    ref.at[:, :, pl.ds(side * LANES, LANES)],
                    out_ref.at[:, :, pl.ds(column, LANES)],
                    sem.at[2 * i + side],
                )
            )
    for copy in copies:
        copy.start()
    for copy in copies:
        copy.wait()


def place_call(plan, blk, arrays):
    any_space = pl.BlockSpec(memory_space=pl.ANY)
    return pl.pallas_call(
        functools.partial(place_body, plan),
        grid_spec=pltpu.PrefetchScalarGridSpec(
            num_scalar_prefetch=1,
            grid=(1,),
            in_specs=[any_space] * len(arrays),
            out_specs=any_space,
            scratch_shapes=[pltpu.SemaphoreType.DMA((2 * len(arrays),))],
        ),
        out_shape=jax.ShapeDtypeStruct((plan.batches, plan.frames, plan.width), jnp.bfloat16),
        cost_estimate=cost(2.0),
        name="place",
    )(blk, *arrays)


def ring_shards(plan, grad_out, saved_input, lengths, kernel, gain, bias, proj_weight):
    f, xh, gh = plan.frames, plan.xhalo, plan.ghalo
    index = lax.axis_index("shard")
    core = index % CORES
    chip = index // CORES
    place = plan.position_of(chip)
    forward, backward = plan.ring()
    offset = chip * plan.chip_frames
    scale = lax.rsqrt(jnp.sum(lengths).astype(jnp.float32))
    info = jnp.concatenate([jnp.stack([core, offset]), lengths]).astype(jnp.int32)
    gain2, bias2 = gain.reshape(1, -1), bias.reshape(1, -1)
    taps = jnp.pad(kernel, ((0, plan.tap_rows - plan.taps), (0, 0)))
    consts = [jnp.asarray(c) for c in transforms(plan)]

    edge = jnp.concatenate(
        [
            jnp.where(core == 1, saved_input[:, f - xh :], saved_input[:, :xh]),
            jnp.where(core == 1, grad_out[:, f - gh :], grad_out[:, :gh]),
        ],
        axis=1,
    )
    xp = lax.ppermute(saved_input, "shard", plan.partners())
    ha = lax.ppermute(edge, "shard", plan.edges())
    mgp = lax.ppermute(grad_out, "shard", plan.partners())
    hb = lax.ppermute(ha, "shard", plan.partners())

    weights = {0: proj_weight}
    going_f = going_b = proj_weight
    for step in range(1, plan.rounds + 1):
        going_f = lax.ppermute(going_f, "shard", forward)
        weights[-step] = going_f
        if step < plan.rounds:
            going_b = lax.ppermute(going_b, "shard", backward)
            weights[step] = going_b
    weights[plan.rounds] = weights.pop(-plan.rounds)

    first = core == 0
    low, high = jnp.where(first, ha, hb), jnp.where(first, hb, ha)
    mg = jnp.concatenate(
        [
            low[:, xh:],
            jnp.where(first, grad_out, mgp),
            jnp.where(first, mgp, grad_out),
            high[:, xh:],
        ],
        axis=1,
    )
    mg = jnp.where(frame_mask(lengths, offset - gh, plan.ext), mg, jnp.zeros_like(mg))

    def blocks(pair, owner):
        chips = [plan.chip_at((place + d) % plan.chips) for d in pair]
        return jnp.stack([CORES * c + owner for c in chips]).astype(jnp.int32)

    pairs = [(h, 1 - h) for h in range(plan.rounds, 0, -1)]
    convs, acts = [], []
    for pair in pairs:
        conv, act = conv_call(
            plan, blocks(pair, core), info, saved_input, xp, ha, hb, taps, gain2, bias2, consts
        )
        convs.append(conv)
        acts.append(act)

    recv = None
    for step, pair in enumerate(pairs):
        last = step == plan.rounds - 1
        send_f, send_b = proj_call(plan, acts[step], mg, recv, last)
        recv_f = lax.ppermute(send_f, "shard", forward)
        if not last:
            recv = (recv_f, lax.ppermute(send_b, "shard", backward))
    proj_grad = (send_b + recv_f.astype(jnp.float32)) * scale

    pieces, columns, stats = [], [], {}
    for step in reversed(range(plan.rounds)):
        pair = pairs[step]
        own, send, stat = back_call(
            plan, blocks(pair, core), info, mg, weights[pair[0]], weights[pair[1]],
            convs[step], saved_input, xp, taps, gain2, bias2, consts,
        )
        pieces += [own, lax.ppermute(send, "shard", plan.partners())]
        columns += [blocks(pair, core), blocks(pair, 1 - core)]
        for half, d in enumerate(pair):
            stats[d % plan.chips] = stat[:, half * LANES : (half + 1) * LANES]
    full = place_call(plan, jnp.concatenate(columns), pieces)

    stacked = jnp.stack([stats[d] for d in range(plan.chips)], 0)
    order = (plan.position_of(jnp.arange(plan.chips)) - place) % plan.chips
    stacked = jnp.take(stacked, order, axis=0)
    groups = [[CORES * p + c for p in range(plan.chips)] for c in range(CORES)]
    parts = lax.all_to_all(stacked, "shard", 0, 0, axis_index_groups=groups)
    summed = jnp.sum(parts, axis=0) * scale
    return (
        full, proj_grad, summed[: plan.taps], summed[plan.tap_rows : plan.tap_rows + 2]
    )


def shards(count, grad_out, saved_input, lengths, kernel, gain, bias, proj_weight):
    batches, frames, model_width = grad_out.shape
    plan = Plan(count, batches, frames, model_width, kernel.shape[0])
    args = (grad_out, saved_input, lengths, kernel, gain, bias, proj_weight)
    return ring_shards(plan, *args) if plan.usable() else plain_shards(*args)


def solution(mesh):
    placed = (
        P("groups", "shard", None),
        P("groups", "shard", None),
        P("groups"),
        P(),
        P(),
        P(),
        P("shard", None),
    )
    return jax.shard_map(
        functools.partial(shards, mesh.shape["shard"]),
        mesh=mesh,
        in_specs=placed,
        out_specs=(
            P("groups", "shard", None),
            P(("groups", "shard"), None),
            P("groups", "shard"),
            P("groups", "shard"),
        ),
        check_vma=False,
    )
```

```python
import functools

import jax
import jax.numpy as jnp
import numpy as np
from jax import lax
from jax.experimental import pallas as pl
from jax.experimental.pallas import tpu as pltpu
from jax.sharding import PartitionSpec as P

LANES = 128
CORES = 2
VMEM_LIMIT = 56 * 1024 * 1024
POINTS = 256


def cost(micros):
    return pl.CostEstimate(flops=0, transcendentals=0, bytes_accessed=int(micros * 3.6e6))


def extended(block, width):
    count = lax.axis_size("shard")
    forward = [(i, i + 1) for i in range(count - 1)]
    backward = [(target, source) for source, target in forward]
    low = lax.ppermute(block[:, block.shape[1] - width :], "shard", forward)
    high = lax.ppermute(block[:, :width], "shard", backward)
    return jnp.concatenate([low, block, high], axis=1)


def frame_mask(lengths, offset, count):
    position = offset + jnp.arange(count, dtype=jnp.int32)
    return (position[None, :] < lengths[:, None])[:, :, None]


def plain_shards(grad_out, saved_input, lengths, kernel, gain, bias, proj_weight):
    batches, frames, model_width = grad_out.shape
    tap_count = kernel.shape[0]
    half_span = (tap_count - 1) // 2
    offset = lax.axis_index("shard") * frames
    norm_scale = lax.rsqrt(jnp.sum(lengths).astype(jnp.float32))
    own_mask = frame_mask(lengths, offset, frames)
    masked_in = jnp.where(own_mask, saved_input, jnp.zeros_like(saved_input))
    masked_grad = jnp.where(own_mask, grad_out, jnp.zeros_like(grad_out))
    in_ext = extended(masked_in, half_span)
    conv = jnp.zeros(grad_out.shape, jnp.float32)
    for tap in range(tap_count):
        conv = conv + kernel[tap] * in_ext[:, tap : tap + frames].astype(jnp.float32)
    pre_act = gain * conv + bias
    gate_sig = jax.nn.sigmoid(pre_act)
    activated = (pre_act * gate_sig).astype(jnp.bfloat16)
    rows = masked_grad.reshape(batches * frames, model_width)
    weight = lax.all_gather(proj_weight, "shard", axis=0, tiled=True)
    act_grad = lax.dot_general(
        rows, weight, (((1,), (1,)), ((), ())), preferred_element_type=jnp.float32
    ).reshape(batches, frames, model_width)
    pre_grad = act_grad * gate_sig * (1.0 + pre_act * (1.0 - gate_sig))
    conv_grad = (pre_grad * gain).astype(jnp.bfloat16)
    grad_ext = extended(conv_grad, half_span)
    back_sum = jnp.zeros(grad_out.shape, jnp.float32)
    grad_float = conv_grad.astype(jnp.float32)
    tap_rows = []
    for tap in range(tap_count):
        begin = 2 * half_span - tap
        back_sum = back_sum + kernel[tap] * grad_ext[:, begin : begin + frames].astype(jnp.float32)
        tap_rows.append(
            jnp.sum(in_ext[:, tap : tap + frames].astype(jnp.float32) * grad_float, axis=(0, 1))
        )
    input_grad = jnp.where(own_mask, back_sum, 0.0).astype(jnp.bfloat16)
    tap_rows.append(jnp.sum(pre_grad * conv, axis=(0, 1)))
    tap_rows.append(jnp.sum(pre_grad, axis=(0, 1)))
    stats = jnp.stack(tap_rows, 0) * norm_scale
    summed = lax.psum_scatter(stats, "shard", scatter_dimension=1, tiled=True)
    product = lax.dot_general(
        activated.reshape(batches * frames, model_width),
        rows,
        (((0,), (0,)), ((), ())),
        preferred_element_type=jnp.float32,
    )
    proj_grad = lax.psum_scatter(product * norm_scale, "shard", scatter_dimension=0, tiled=True)
    return (input_grad, proj_grad, summed[:tap_count], summed[tap_count:])


class Plan:
    def __init__(self, count, groups, batches, frames, model_width, tap_count):
        self.count = count
        self.chips = count // CORES
        self.rounds = self.chips // 2
        self.batches = batches
        self.frames = frames
        self.chip_frames = CORES * frames
        self.width = model_width
        self.block = model_width // count
        self.taps = tap_count
        self.half = (tap_count - 1) // 2
        self.ghalo = -(-self.half // 16) * 16
        self.xhalo = 2 * self.ghalo
        self.ext = self.chip_frames + 2 * self.ghalo
        self.xext = self.chip_frames + 2 * self.xhalo
        self.tap_rows = -(-tap_count // 16) * 16
        self.stat_rows = self.tap_rows + 8
        self.weight_parts = 2 if groups == 2 else 1
        self.pairs = [(h, 1 - h) for h in range(self.rounds, 0, -1)]
        self.conv_windows = windows(self.ext, self.xhalo - self.ghalo - self.half + tap_count)
        self.back_windows = windows(self.chip_frames, self.ghalo + self.half + 1)

    def window_rows(self, found):
        return found[0] * (found[1] - 1) + POINTS

    def block_slot(self, step, side):
        return 3 + self.batches + 2 * step + side

    def usable(self):
        return (
            self.count % (2 * CORES) == 0
            and self.block == LANES
            and self.block * self.count == self.width
            and self.frames % 128 == 0
            and self.frames >= self.xhalo
            and self.taps % 2 == 1
            and 4 * self.ghalo <= POINTS // 2
            and self.window_rows(self.conv_windows) >= self.xext
            and self.window_rows(self.back_windows) >= self.ext
            and self.window_rows(self.conv_windows)
            >= self.xhalo + self.window_rows(self.back_windows) - self.back_windows[0]
            and self.chips <= 16
        )

    def chip_at(self, position):
        half = self.chips // 2
        return jnp.where(position < half, 2 * position, 2 * (self.chips - 1 - position) + 1)

    def position_of(self, chip):
        return jnp.where(chip % 2 == 0, chip // 2, self.chips - 1 - chip // 2)

    def ring(self):
        half = self.chips // 2
        order = [2 * i for i in range(half)] + [2 * i + 1 for i in reversed(range(half))]
        forward = []
        for core in range(CORES):
            for i in range(self.chips):
                source, target = order[i], order[(i + 1) % self.chips]
                forward.append((CORES * source + core, CORES * target + core))
        return forward, [(t, s) for s, t in forward]

    def edges(self):
        pairs = []
        for chip in range(self.chips - 1):
            last, first = CORES * chip + 1, CORES * (chip + 1)
            pairs += [(last, first), (first, last)]
        return pairs

    def partners(self):
        return [(s, s ^ 1) for s in range(self.count)]


def sigmoid(value):
    return 0.5 * jnp.tanh(0.5 * value) + 0.5


def split(value):
    high = value.astype(jnp.bfloat16)
    return high, (value - high.astype(jnp.float32)).astype(jnp.bfloat16)


def split_matrix(matrix):
    high = matrix.astype(jnp.bfloat16)
    return high, (matrix - high.astype(np.float64)).astype(jnp.bfloat16)


def transforms(plan):
    time = np.arange(POINTS)
    theta = np.pi * (2 * np.arange(POINTS // 2) + 1) / POINTS
    angle = theta[:, None] * time[None, :]
    direct = np.concatenate([np.cos(angle), -np.sin(angle)], 0)
    inverse = direct.T * (2.0 / POINTS)

    def spectrum(lags):
        phase = theta[:, None] * lags[None, :]
        matrix = np.concatenate([np.cos(phase), np.sin(phase)], 0)
        return np.pad(matrix, ((0, 0), (0, plan.tap_rows - plan.taps)))

    taps = np.arange(plan.taps)
    back_lags = plan.ghalo + plan.half - taps
    lag_rows = np.pad(inverse[back_lags], ((0, plan.tap_rows - plan.taps), (0, 0)))
    double = lambda m: np.concatenate(split_matrix(m), 1)

    def triple(m):
        high, low = split_matrix(m)
        return np.concatenate([high, low, high], 1)

    conv_lags = plan.xhalo - plan.ghalo - plan.half + taps
    return (
        double(direct),
        triple(inverse),
        np.stack(split_matrix(spectrum(conv_lags))),
        np.stack(split_matrix(spectrum(back_lags))),
        triple(lag_rows),
        double(direct * (time < plan.back_windows[0])),
    )


def taps_spectrum(t_ref, k_ref):
    high, low = split(jnp.concatenate([k_ref[0][...], k_ref[1][...]], axis=1))
    dot = functools.partial(jnp.dot, preferred_element_type=jnp.float32)
    return dot(t_ref[0], high) + dot(t_ref[1], high) + dot(t_ref[0], low)


def to_spectrum(direct_ref, window):
    return jnp.dot(
        direct_ref[...], jnp.concatenate([window, window], 0), preferred_element_type=jnp.float32
    )


def from_spectrum(inverse_ref, rows, parts, slot):
    return jnp.dot(inverse_ref[:rows, :], parts[slot], preferred_element_type=jnp.float32)


def store_parts(parts, slot, row, value):
    high, low = split(value)
    rows = value.shape[0]
    parts[slot, row : row + rows, :] = high
    parts[slot, POINTS + row : POINTS + row + rows, :] = high
    parts[slot, 2 * POINTS + row : 2 * POINTS + row + rows, :] = low


def windows(rows_out, reach):
    count = -(-rows_out // ((POINTS - reach) // 16 * 16))
    return -(-rows_out // count // 16) * 16, count


STEP = 16
HALF = POINTS // 2


def spectral_product(spec, taps, parts, slot):
    for row in range(0, HALF, STEP):
        up, down = slice(row, row + STEP), slice(HALF + row, HALF + row + STEP)
        re, im, kr, ks = spec[slot, up, :], spec[slot, down, :], taps[up, :], taps[down, :]
        store_parts(parts, slot, row, re * kr - im * ks)
        store_parts(parts, slot, HALF + row, re * ks + im * kr)


def conv_body(plan, info, *refs):
    x_ref, k_ref, gain_ref, bias_ref = (refs[2 * i : 2 * i + 2] for i in range(4))
    direct, inverse, t_ref, conv_ref, act_ref, spec, taps, parts = refs[8:]
    each, count = plan.conv_windows

    @pl.when(pl.program_id(0) == 0)
    def _():
        taps[...] = taps_spectrum(t_ref, k_ref)

    for j in range(count):
        window = [ref[0, j * each : j * each + POINTS, :] for ref in x_ref]
        spec[j] = to_spectrum(direct, jnp.concatenate(window, axis=1))
    for j in range(count):
        spectral_product(spec, taps, parts, j)
        rows = min(each, plan.ext - j * each)
        conv_ref[0, j * each : j * each + rows, :] = from_spectrum(inverse, rows, parts, j)

    for i in range(plan.chip_frames // LANES):
        for side in range(2):
            lanes = slice(side * LANES, (side + 1) * LANES)
            begin = plan.ghalo + i * LANES
            conv = conv_ref[0, begin : begin + LANES, lanes]
            pre = gain_ref[side][...] * conv + bias_ref[side][...]
            act_ref[lanes, i * LANES : (i + 1) * LANES] = (pre * sigmoid(pre)).T.astype(
                jnp.bfloat16
            )


def pair_specs(plan, step, shape, index):
    return [
        pl.BlockSpec(
            shape, lambda b, info, at=plan.block_slot(step, side): index(b, info[at])
        )
        for side in range(2)
    ]


def whole(array):
    return pl.BlockSpec(
        array.shape, lambda *_: (0,) * array.ndim, pipeline_mode=pl.Buffered(1)
    )


def conv_call(plan, step, info, x, kernel, gain, bias, consts):
    bt = plan.batches
    flat = lambda b, block: (0, block)
    direct, inverse, t_conv = consts[:3]
    wide = 2 * LANES
    slots = plan.conv_windows[1]
    specs = functools.partial(pair_specs, plan, step)
    return pl.pallas_call(
        functools.partial(conv_body, plan),
        grid_spec=pltpu.PrefetchScalarGridSpec(
            num_scalar_prefetch=1,
            grid=(bt,),
            in_specs=specs((1, x.shape[1], LANES), lambda b, block: (b, 0, block))
            + specs((plan.tap_rows, LANES), flat)
            + specs((1, LANES), flat)
            + specs((1, LANES), flat)
            + [whole(direct), whole(inverse), whole(t_conv)],
            out_specs=[
                pl.BlockSpec((1, plan.ext, wide), lambda b, info: (b, 0, 0)),
                pl.BlockSpec((wide, plan.chip_frames), lambda b, info: (0, b)),
            ],
            scratch_shapes=[
                pltpu.VMEM((slots, POINTS, wide), jnp.float32),
                pltpu.VMEM((POINTS, wide), jnp.float32),
                pltpu.VMEM((slots, 3 * POINTS, wide), jnp.bfloat16),
            ],
        ),
        out_shape=[
            jax.ShapeDtypeStruct((bt, plan.ext, wide), jnp.float32),
            jax.ShapeDtypeStruct((wide, bt * plan.chip_frames), jnp.bfloat16),
        ],
        compiler_params=pltpu.CompilerParams(vmem_limit_bytes=VMEM_LIMIT),
        cost_estimate=cost(4.0),
        name="conv",
    )(info, x, x, kernel, kernel, gain, gain, bias, bias, direct, inverse, t_conv)


def proj_body(plan, act_ref, mg_ref, out_f, out_b):
    gh, cf = plan.ghalo, plan.chip_frames
    total = None
    for b in range(plan.batches):
        part = jnp.dot(
            act_ref[:, b * cf : (b + 1) * cf],
            mg_ref[b, gh : gh + cf, :],
            preferred_element_type=jnp.float32,
        )
        total = part if total is None else total + part
    out_f[...] = total[:LANES].astype(out_f.dtype)
    out_b[...] = total[LANES:].astype(out_b.dtype)


def proj_call(plan, act, mg, kinds):
    tiles = 2
    columns = plan.width // tiles
    wide = pl.BlockSpec((LANES, columns), lambda j: (0, j))
    return pl.pallas_call(
        functools.partial(proj_body, plan),
        grid=(tiles,),
        in_specs=[
            whole(act),
            pl.BlockSpec((plan.batches, plan.ext, columns), lambda j: (0, 0, j)),
        ],
        out_specs=[wide, wide],
        out_shape=[jax.ShapeDtypeStruct((LANES, plan.width), kind) for kind in kinds],
        compiler_params=pltpu.CompilerParams(vmem_limit_bytes=VMEM_LIMIT),
        cost_estimate=cost(4.0),
        name="proj",
    )(act, mg)


def back_body(plan, info, *refs):
    x_ref, k_ref, gain_ref, bias_ref = (refs[2 * i : 2 * i + 2] for i in range(4))
    halves = plan.weight_parts
    w_ref = refs[8 : 8 + 2 * halves]
    mg_ref, conv_ref, direct, segment, inverse, t_ref, lag_ref = refs[8 + 2 * halves :][:7]
    (own_ref, send_ref, stat_ref, weight, ag, gs, tail, spec, xspec, taps, cross, parts, os,
     sums) = refs[15 + 2 * halves :]
    core, offset, side_y = info[0], info[1], info[2]
    f, xh, gh, cf, ext = plan.frames, plan.xhalo, plan.ghalo, plan.chip_frames, plan.ext
    each, count = plan.back_windows
    b = pl.program_id(0)
    live = info[3 + b]
    piece = LANES // halves

    @pl.when(b == 0)
    def _():
        taps[...] = taps_spectrum(t_ref, k_ref)
        cross[...] = jnp.zeros_like(cross)
        sums[...] = jnp.zeros_like(sums)
        for block in range(2):
            for part in range(halves):
                at = (side_y + part) % halves * piece if halves > 1 else 0
                begin = pl.multiple_of(block * LANES + at, piece)
                weight[pl.ds(begin, piece), :] = w_ref[block * halves + part][...]
        gs[ext:, :] = jnp.zeros((gs.shape[0] - ext, 2 * LANES), jnp.bfloat16)
        tail[...] = jnp.zeros_like(tail)

    ag[...] = lax.dot_general(
        mg_ref[0], weight[...], (((1,), (1,)), ((), ())), preferred_element_type=jnp.float32
    )
    last_rows = cf - (count - 1) * each
    for j in range(count):
        begin = xh + j * each
        if j < count - 1:
            window = [ref[0, begin : begin + POINTS, :] for ref in x_ref]
            window = jnp.concatenate(window, axis=1)
        else:
            for side in range(2):
                lanes = slice(side * LANES, (side + 1) * LANES)
                tail[:last_rows, lanes] = x_ref[side][0, begin : begin + last_rows, :]
            window = tail[...]
        xspec[j] = to_spectrum(segment, window)
    gain = jnp.concatenate([gain_ref[0][...], gain_ref[1][...]], axis=1)
    bias = jnp.concatenate([bias_ref[0][...], bias_ref[1][...]], axis=1)

    gain_sum = jnp.zeros((8, 2 * LANES), jnp.float32)
    bias_sum = jnp.zeros((8, 2 * LANES), jnp.float32)
    for row in range(0, ext, STEP):
        conv = conv_ref[0, row : row + STEP, :]
        pre = gain * conv + bias
        sig = sigmoid(pre)
        value = ag[row : row + STEP, :] * sig * (1.0 + pre * (1.0 - sig))
        gs[row : row + STEP, :] = (value * gain).astype(jnp.bfloat16)
        if gh <= row < gh + cf:
            fold = lambda v: jnp.sum(v.reshape(STEP // 8, 8, 2 * LANES), axis=0)
            gain_sum = gain_sum + fold(value * conv)
            bias_sum = bias_sum + fold(value)
    sums[0] += gain_sum
    sums[1] += bias_sum

    for j in range(count):
        spec[j] = to_spectrum(direct, gs[j * each : j * each + POINTS, :])
    for j in range(count):
        spectral_product(spec, taps, parts, j)
        rows = min(each, cf - j * each)
        value = from_spectrum(inverse, rows, parts, j)
        position = offset + j * each + lax.broadcasted_iota(jnp.int32, value.shape, 0)
        os[j * each : j * each + rows, :] = jnp.where(position < live, value, 0.0).astype(
            jnp.bfloat16
        )
    for row in range(0, HALF, STEP):
        up, down = slice(row, row + STEP), slice(HALF + row, HALF + row + STEP)
        total_r, total_i = cross[up, :], cross[down, :]
        for j in range(count):
            re, im, xr, xi = spec[j, up, :], spec[j, down, :], xspec[j, up, :], xspec[j, down, :]
            total_r = total_r + re * xr + im * xi
            total_i = total_i + im * xr - re * xi
        cross[up, :] = total_r
        cross[down, :] = total_i

    @pl.when(core == 0)
    def _():
        own_ref[0] = os[:f]
        send_ref[0] = os[f:]

    @pl.when(core != 0)
    def _():
        own_ref[0] = os[f:]
        send_ref[0] = os[:f]

    @pl.when(b == plan.batches - 1)
    def _():
        for row in range(0, POINTS, STEP):
            store_parts(parts, 0, row, cross[row : row + STEP, :])
        stat_ref[: plan.tap_rows] = from_spectrum(lag_ref, plan.tap_rows, parts, 0)
        total = [jnp.sum(sums[i], axis=0, keepdims=True) for i in range(2)]
        pad = jnp.zeros((plan.stat_rows - plan.tap_rows - 2, 2 * LANES), jnp.float32)
        stat_ref[plan.tap_rows :] = jnp.concatenate(total + [pad], axis=0)


def back_call(plan, step, info, mg, weights, conv, x, kernel, gain, bias, consts):
    bt = plan.batches
    flat = lambda b, block: (0, block)
    batch = lambda b, info: (b, 0, 0)
    direct, inverse, _, t_back, lags, segment = consts
    pair = (1, plan.frames, 2 * LANES)
    wide = 2 * LANES
    slots = plan.back_windows[1]
    specs = functools.partial(pair_specs, plan, step)
    piece = LANES // plan.weight_parts
    one = pl.Buffered(1)
    w_specs, w_arrays = [], []
    for array, part in weights:
        if part is None:
            index = lambda b, info: (0, 0)
        else:
            index = lambda b, info, part=part: ((info[2] + part) % plan.weight_parts, 0)
        w_specs.append(pl.BlockSpec((piece, plan.width), index, pipeline_mode=one))
        w_arrays.append(array)
    return pl.pallas_call(
        functools.partial(back_body, plan),
        grid_spec=pltpu.PrefetchScalarGridSpec(
            num_scalar_prefetch=1,
            grid=(bt,),
            in_specs=specs((1, x.shape[1], LANES), lambda b, block: (b, 0, block))
            + specs((plan.tap_rows, LANES), flat)
            + specs((1, LANES), flat)
            + specs((1, LANES), flat)
            + w_specs
            + [pl.BlockSpec((1, plan.ext, plan.width), batch)]
            + [pl.BlockSpec((1, plan.ext, wide), batch)]
            + [whole(c) for c in (direct, segment, inverse, t_back, lags)],
            out_specs=[
                pl.BlockSpec(pair, batch),
                pl.BlockSpec(pair, batch),
                pl.BlockSpec((plan.stat_rows, wide), lambda b, info: (0, 0)),
            ],
            scratch_shapes=[
                pltpu.VMEM((wide, plan.width), jnp.bfloat16),
                pltpu.VMEM((plan.ext, wide), jnp.float32),
                pltpu.VMEM((plan.window_rows(plan.back_windows), wide), jnp.bfloat16),
                pltpu.VMEM((POINTS, wide), jnp.bfloat16),
                pltpu.VMEM((slots, POINTS, wide), jnp.float32),
                pltpu.VMEM((slots, POINTS, wide), jnp.float32),
                pltpu.VMEM((POINTS, wide), jnp.float32),
                pltpu.VMEM((POINTS, wide), jnp.float32),
                pltpu.VMEM((slots, 3 * POINTS, wide), jnp.bfloat16),
                pltpu.VMEM((plan.chip_frames, wide), jnp.bfloat16),
                pltpu.VMEM((2, 8, wide), jnp.float32),
            ],
        ),
        out_shape=[
            jax.ShapeDtypeStruct((bt, plan.frames, wide), jnp.bfloat16),
            jax.ShapeDtypeStruct((bt, plan.frames, wide), jnp.bfloat16),
            jax.ShapeDtypeStruct((plan.stat_rows, wide), jnp.float32),
        ],
        compiler_params=pltpu.CompilerParams(vmem_limit_bytes=VMEM_LIMIT),
        cost_estimate=cost(8.0),
        name="back",
    )(info, x, x, kernel, kernel, gain, gain, bias, bias, *w_arrays, mg, conv,
      direct, segment, inverse, t_back, lags)


def place_body(plan, info, *refs):
    out_ref = refs[-1]
    for i, ref in enumerate(refs[:-1]):
        step, partner = divmod(i, 2)
        for side in range(2):
            block = info[plan.block_slot(step, side)]
            if partner:
                block = block + 1 - 2 * info[0]
            column = pl.multiple_of(block * LANES, LANES)
            out_ref[:, :, pl.ds(column, LANES)] = ref[:, :, side * LANES : (side + 1) * LANES]


def place_call(plan, info, arrays):
    shape = (plan.batches, plan.frames, plan.width)
    return pl.pallas_call(
        functools.partial(place_body, plan),
        grid_spec=pltpu.PrefetchScalarGridSpec(
            num_scalar_prefetch=1,
            grid=(1,),
            in_specs=[whole(array) for array in arrays],
            out_specs=pl.BlockSpec(shape, lambda g, info: (0, 0, 0)),
        ),
        out_shape=jax.ShapeDtypeStruct(shape, jnp.bfloat16),
        compiler_params=pltpu.CompilerParams(vmem_limit_bytes=VMEM_LIMIT),
        cost_estimate=cost(3.0),
        name="place",
    )(info, *arrays)


def deal_body(plan, info, *refs):
    out_ref = refs[-1]
    for step, ref in enumerate(refs[:-1]):
        for side in range(2):
            chip = info[plan.block_slot(step, side)] // CORES
            out_ref[chip] = ref[:, side * LANES : (side + 1) * LANES]


def deal_call(plan, info, arrays):
    shape = (plan.chips, plan.stat_rows, LANES)
    return pl.pallas_call(
        functools.partial(deal_body, plan),
        grid_spec=pltpu.PrefetchScalarGridSpec(
            num_scalar_prefetch=1,
            grid=(1,),
            in_specs=[whole(array) for array in arrays],
            out_specs=pl.BlockSpec(shape, lambda g, info: (0, 0, 0)),
        ),
        out_shape=jax.ShapeDtypeStruct(shape, jnp.float32),
        cost_estimate=cost(1.0),
        name="deal",
    )(info, *arrays)


def after(value, *others):
    return lax.optimization_barrier((value, *others))[0]


def ring_shards(plan, grad_out, saved_input, lengths, kernel, gain, bias, proj_weight):
    f, xh, gh = plan.frames, plan.xhalo, plan.ghalo
    index = lax.axis_index("shard")
    group = lax.axis_index("groups")
    core, chip = index % CORES, index // CORES
    place = plan.position_of(chip)
    forward, backward = plan.ring()
    offset = chip * plan.chip_frames
    scale = lax.rsqrt(jnp.sum(lengths).astype(jnp.float32))
    pairs = plan.pairs
    far = jnp.asarray([d for pair in pairs for d in pair], jnp.int32)
    owned = CORES * plan.chip_at((place + far + plan.chips) % plan.chips) + core
    info = jnp.concatenate([jnp.stack([core, offset, group]), lengths, owned]).astype(jnp.int32)
    gain2, bias2 = gain.reshape(1, -1), bias.reshape(1, -1)
    taps = jnp.pad(kernel, ((0, plan.tap_rows - plan.taps), (0, 0)))
    consts = [jnp.asarray(c) for c in transforms(plan)]

    edge = jnp.concatenate(
        [
            jnp.where(core == 1, saved_input[:, f - xh :], saved_input[:, :xh]),
            jnp.where(core == 1, grad_out[:, f - gh :], grad_out[:, :gh]),
        ],
        axis=1,
    )
    xp = lax.ppermute(saved_input, "shard", plan.partners())
    ha = lax.ppermute(edge, "shard", plan.edges())
    mgp = lax.ppermute(grad_out, "shard", plan.partners())
    hb = lax.ppermute(ha, "shard", plan.partners())

    parts = plan.weight_parts
    piece = LANES // parts
    if parts > 1:
        start = lax.dynamic_slice_in_dim(after(proj_weight, ha), group * piece, piece, 0)
    else:
        start = after(proj_weight, ha)
    swap = [
        (g * plan.count + s, (1 - g) * plan.count + s)
        for g in range(parts) for s in range(plan.count)
    ]

    def both(half):
        if parts == 1:
            return [(half, None)]
        return [(half, None), (lax.ppermute(half, ("groups", "shard"), swap), None)]

    weights = {0: [(proj_weight, part) for part in range(parts)]}
    going_f = going_b = start
    arrivals = []
    for step in range(1, plan.rounds + 1):
        going_f = lax.ppermute(going_f, "shard", forward)
        weights[-step] = both(going_f)
        if step < plan.rounds:
            going_b = lax.ppermute(going_b, "shard", backward)
            weights[step] = both(going_b)
        arrivals.append(going_f)
    weights[plan.rounds] = weights.pop(-plan.rounds)

    first = core == 0
    low, high = jnp.where(first, ha, hb), jnp.where(first, hb, ha)

    def assembled(low, own, other, high, rows):
        halo = low.shape[1]
        pieces = [low, jnp.where(first, own, other), jnp.where(first, other, own), high]
        value = jnp.concatenate(pieces, axis=1)
        value = jnp.where(
            frame_mask(lengths, offset - halo, value.shape[1]), value, jnp.zeros_like(value)
        )
        return jnp.pad(value, ((0, 0), (0, rows - value.shape[1]), (0, 0)))

    x = assembled(low[:, :xh], saved_input, xp, high[:, :xh], plan.window_rows(plan.conv_windows))
    mg = assembled(low[:, xh:], grad_out, mgp, high[:, xh:], plan.ext)

    convs, products = [], []
    order = info
    for step in range(plan.rounds):
        conv, act = conv_call(plan, step, order, x, taps, gain2, bias2, consts)
        convs.append(conv)
        last = step == plan.rounds - 1
        kinds = [jnp.bfloat16 if step == 0 else jnp.float32] * 2
        products.append(proj_call(plan, act, mg, kinds))
        order = after(info, products[-1][0])

    def added(product, received):
        return product + received.astype(jnp.float32)

    sends = []
    send_f, send_b = products[0]
    for step in range(plan.rounds):
        recv_f = lax.ppermute(send_f, "shard", forward)
        if step < plan.rounds - 1:
            recv_b = lax.ppermute(send_b, "shard", backward)
            product_f, product_b = products[step + 1]
            send_f = added(product_f, recv_f).astype(jnp.bfloat16)
            send_b = added(product_b, recv_b)
            if step < plan.rounds - 2:
                send_b = send_b.astype(jnp.bfloat16)
            sends.append(send_f)
    proj_grad = added(send_b, recv_f) * scale

    pieces, stats = {}, {}
    for turn, step in enumerate(reversed(range(plan.rounds))):
        pair = pairs[step]
        order = after(info, sends[min(turn, len(sends) - 1)], products[-1][0])
        own, send, stats[step] = back_call(
            plan, step, order, mg, weights[pair[0]] + weights[pair[1]],
            convs[step], x, taps, gain2, bias2, consts,
        )
        pieces[step] = [own, lax.ppermute(send, "shard", plan.partners())]
    full = place_call(plan, info, [a for step in range(plan.rounds) for a in pieces[step]])

    dealt = deal_call(plan, info, [stats[step] for step in range(plan.rounds)])
    groups = [[CORES * p + c for p in range(plan.chips)] for c in range(CORES)]
    summed = jnp.sum(
        lax.all_to_all(dealt, "shard", 0, 0, axis_index_groups=groups), axis=0
    ) * scale
    return (
        full, proj_grad, summed[: plan.taps], summed[plan.tap_rows : plan.tap_rows + 2]
    )


def shards(count, group_count, grad_out, saved_input, lengths, kernel, gain, bias, proj_weight):
    batches, frames, model_width = grad_out.shape
    plan = Plan(count, group_count, batches, frames, model_width, kernel.shape[0])
    args = (grad_out, saved_input, lengths, kernel, gain, bias, proj_weight)
    return ring_shards(plan, *args) if plan.usable() else plain_shards(*args)


def solution(mesh):
    placed = (
        P("groups", "shard", None),
        P("groups", "shard", None),
        P("groups"),
        P(),
        P(),
        P(),
        P("shard", None),
    )
    return jax.shard_map(
        functools.partial(shards, mesh.shape["shard"], mesh.shape["groups"]),
        mesh=mesh,
        in_specs=placed,
        out_specs=(
            P("groups", "shard", None),
            P(("groups", "shard"), None),
            P("groups", "shard"),
            P("groups", "shard"),
        ),
        check_vma=False,
    )
```

```python
import functools

import jax
import jax.numpy as jnp
import numpy as np
from jax import lax
from jax.experimental import pallas as pl
from jax.experimental.pallas import tpu as pltpu
from jax.sharding import PartitionSpec as P

LANES = 128
CORES = 2
VMEM_LIMIT = 56 * 1024 * 1024
POINTS = 256


def cost(micros):
    return pl.CostEstimate(flops=0, transcendentals=0, bytes_accessed=int(micros * 3.6e6))


def extended(block, width):
    count = lax.axis_size("shard")
    forward = [(i, i + 1) for i in range(count - 1)]
    backward = [(target, source) for source, target in forward]
    low = lax.ppermute(block[:, block.shape[1] - width :], "shard", forward)
    high = lax.ppermute(block[:, :width], "shard", backward)
    return jnp.concatenate([low, block, high], axis=1)


def frame_mask(lengths, offset, count):
    position = offset + jnp.arange(count, dtype=jnp.int32)
    return (position[None, :] < lengths[:, None])[:, :, None]


def plain_shards(grad_out, saved_input, lengths, kernel, gain, bias, proj_weight):
    batches, frames, model_width = grad_out.shape
    tap_count = kernel.shape[0]
    half_span = (tap_count - 1) // 2
    offset = lax.axis_index("shard") * frames
    norm_scale = lax.rsqrt(jnp.sum(lengths).astype(jnp.float32))
    own_mask = frame_mask(lengths, offset, frames)
    masked_in = jnp.where(own_mask, saved_input, jnp.zeros_like(saved_input))
    masked_grad = jnp.where(own_mask, grad_out, jnp.zeros_like(grad_out))
    in_ext = extended(masked_in, half_span)
    conv = jnp.zeros(grad_out.shape, jnp.float32)
    for tap in range(tap_count):
        conv = conv + kernel[tap] * in_ext[:, tap : tap + frames].astype(jnp.float32)
    pre_act = gain * conv + bias
    gate_sig = jax.nn.sigmoid(pre_act)
    activated = (pre_act * gate_sig).astype(jnp.bfloat16)
    rows = masked_grad.reshape(batches * frames, model_width)
    weight = lax.all_gather(proj_weight, "shard", axis=0, tiled=True)
    act_grad = lax.dot_general(
        rows, weight, (((1,), (1,)), ((), ())), preferred_element_type=jnp.float32
    ).reshape(batches, frames, model_width)
    pre_grad = act_grad * gate_sig * (1.0 + pre_act * (1.0 - gate_sig))
    conv_grad = (pre_grad * gain).astype(jnp.bfloat16)
    grad_ext = extended(conv_grad, half_span)
    back_sum = jnp.zeros(grad_out.shape, jnp.float32)
    grad_float = conv_grad.astype(jnp.float32)
    tap_rows = []
    for tap in range(tap_count):
        begin = 2 * half_span - tap
        back_sum = back_sum + kernel[tap] * grad_ext[:, begin : begin + frames].astype(jnp.float32)
        tap_rows.append(
            jnp.sum(in_ext[:, tap : tap + frames].astype(jnp.float32) * grad_float, axis=(0, 1))
        )
    input_grad = jnp.where(own_mask, back_sum, 0.0).astype(jnp.bfloat16)
    tap_rows.append(jnp.sum(pre_grad * conv, axis=(0, 1)))
    tap_rows.append(jnp.sum(pre_grad, axis=(0, 1)))
    stats = jnp.stack(tap_rows, 0) * norm_scale
    summed = lax.psum_scatter(stats, "shard", scatter_dimension=1, tiled=True)
    product = lax.dot_general(
        activated.reshape(batches * frames, model_width),
        rows,
        (((0,), (0,)), ((), ())),
        preferred_element_type=jnp.float32,
    )
    proj_grad = lax.psum_scatter(product * norm_scale, "shard", scatter_dimension=0, tiled=True)
    return (input_grad, proj_grad, summed[:tap_count], summed[tap_count:])


class Plan:
    def __init__(self, count, groups, batches, frames, model_width, tap_count):
        self.count = count
        self.chips = count // CORES
        self.rounds = self.chips // 2
        self.batches = batches
        self.frames = frames
        self.chip_frames = CORES * frames
        self.width = model_width
        self.block = model_width // count
        self.taps = tap_count
        self.half = (tap_count - 1) // 2
        self.ghalo = -(-self.half // 16) * 16
        self.xhalo = 2 * self.ghalo
        self.ext = self.chip_frames + 2 * self.ghalo
        self.xext = self.chip_frames + 2 * self.xhalo
        self.tap_rows = -(-tap_count // 16) * 16
        self.stat_rows = self.tap_rows + 8
        self.weight_parts = 2 if groups == 2 else 1
        self.pairs = [(h, 1 - h) for h in range(self.rounds, 0, -1)]
        self.conv_windows = windows(self.ext, self.xhalo - self.ghalo - self.half + tap_count)
        self.back_windows = windows(self.chip_frames, self.ghalo + self.half + 1)

    def window_rows(self, found):
        return found[0] * (found[1] - 1) + POINTS

    def block_slot(self, step, side):
        return 3 + self.batches + 2 * step + side

    def usable(self):
        return (
            self.count % (2 * CORES) == 0
            and self.block == LANES
            and self.block * self.count == self.width
            and self.frames % 128 == 0
            and self.frames >= self.xhalo
            and self.taps % 2 == 1
            and 4 * self.ghalo <= POINTS // 2
            and self.window_rows(self.conv_windows) >= self.xext
            and self.window_rows(self.back_windows) >= self.ext
            and self.window_rows(self.conv_windows)
            >= self.xhalo + self.window_rows(self.back_windows) - self.back_windows[0]
            and self.chips <= 16
        )

    def chip_at(self, position):
        half = self.chips // 2
        return jnp.where(position < half, 2 * position, 2 * (self.chips - 1 - position) + 1)

    def position_of(self, chip):
        return jnp.where(chip % 2 == 0, chip // 2, self.chips - 1 - chip // 2)

    def ring(self):
        half = self.chips // 2
        order = [2 * i for i in range(half)] + [2 * i + 1 for i in reversed(range(half))]
        forward = []
        for core in range(CORES):
            for i in range(self.chips):
                source, target = order[i], order[(i + 1) % self.chips]
                forward.append((CORES * source + core, CORES * target + core))
        return forward, [(t, s) for s, t in forward]

    def edges(self):
        pairs = []
        for chip in range(self.chips - 1):
            last, first = CORES * chip + 1, CORES * (chip + 1)
            pairs += [(last, first), (first, last)]
        return pairs

    def partners(self):
        return [(s, s ^ 1) for s in range(self.count)]


def sigmoid(value):
    return 0.5 * jnp.tanh(0.5 * value) + 0.5


def split(value):
    high = value.astype(jnp.bfloat16)
    return high, (value - high.astype(jnp.float32)).astype(jnp.bfloat16)


def split_matrix(matrix):
    high = matrix.astype(jnp.bfloat16)
    return high, (matrix - high.astype(np.float64)).astype(jnp.bfloat16)


def transforms(plan):
    time = np.arange(POINTS)
    theta = np.pi * (2 * np.arange(POINTS // 2) + 1) / POINTS
    angle = theta[:, None] * time[None, :]
    direct = np.concatenate([np.cos(angle), -np.sin(angle)], 0)
    inverse = direct.T * (2.0 / POINTS)

    def spectrum(lags):
        phase = theta[:, None] * lags[None, :]
        matrix = np.concatenate([np.cos(phase), np.sin(phase)], 0)
        return np.pad(matrix, ((0, 0), (0, plan.tap_rows - plan.taps)))

    taps = np.arange(plan.taps)
    back_lags = plan.ghalo + plan.half - taps
    lag_rows = np.pad(inverse[back_lags], ((0, plan.tap_rows - plan.taps), (0, 0)))
    half = lambda m: m.astype(jnp.bfloat16)
    conv_lags = plan.xhalo - plan.ghalo - plan.half + taps
    return (
        half(direct),
        half(inverse),
        np.stack(split_matrix(spectrum(conv_lags))),
        np.stack(split_matrix(spectrum(back_lags))),
        half(lag_rows),
        half(direct * (time < plan.back_windows[0])),
    )


def taps_spectrum(t_ref, k_ref):
    high, low = split(jnp.concatenate([k_ref[0][...], k_ref[1][...]], axis=1))
    dot = functools.partial(jnp.dot, preferred_element_type=jnp.float32)
    return dot(t_ref[0], high) + dot(t_ref[1], high) + dot(t_ref[0], low)


def to_spectrum(direct_ref, window):
    return jnp.dot(direct_ref[...], window, preferred_element_type=jnp.float32)


def from_spectrum(inverse_ref, rows, parts, slot):
    return jnp.dot(inverse_ref[:rows, :], parts[slot], preferred_element_type=jnp.float32)


def windows(rows_out, reach):
    count = -(-rows_out // ((POINTS - reach) // 16 * 16))
    return -(-rows_out // count // 16) * 16, count


STEP = 16
HALF = POINTS // 2


def spectral_product(spec, taps, parts, slot):
    for row in range(0, HALF, STEP):
        up, down = slice(row, row + STEP), slice(HALF + row, HALF + row + STEP)
        re, im, kr, ks = spec[slot, up, :], spec[slot, down, :], taps[up, :], taps[down, :]
        parts[slot, up, :] = (re * kr - im * ks).astype(jnp.bfloat16)
        parts[slot, down, :] = (re * ks + im * kr).astype(jnp.bfloat16)


def conv_body(plan, info, *refs):
    x_ref = refs[0]
    k_ref, gain_ref, bias_ref = (refs[2 * i + 1 : 2 * i + 3] for i in range(3))
    direct, inverse, t_ref, conv_ref, act_ref, spec, taps, parts = refs[7:]
    each, count = plan.conv_windows

    @pl.when(pl.program_id(0) == 0)
    def _():
        taps[...] = taps_spectrum(t_ref, k_ref)

    for j in range(count):
        spec[j] = to_spectrum(direct, x_ref[0, j * each : j * each + POINTS, :])
    for j in range(count):
        spectral_product(spec, taps, parts, j)
        rows = min(each, plan.ext - j * each)
        conv_ref[0, j * each : j * each + rows, :] = from_spectrum(inverse, rows, parts, j)

    for i in range(plan.chip_frames // LANES):
        for side in range(2):
            lanes = slice(side * LANES, (side + 1) * LANES)
            begin = plan.ghalo + i * LANES
            conv = conv_ref[0, begin : begin + LANES, lanes]
            pre = gain_ref[side][...] * conv + bias_ref[side][...]
            act_ref[lanes, i * LANES : (i + 1) * LANES] = (pre * sigmoid(pre)).T.astype(
                jnp.bfloat16
            )


def pair_specs(plan, step, shape, index):
    return [
        pl.BlockSpec(
            shape, lambda b, info, at=plan.block_slot(step, side): index(b, info[at])
        )
        for side in range(2)
    ]


def whole(array):
    return pl.BlockSpec(
        array.shape, lambda *_: (0,) * array.ndim, pipeline_mode=pl.Buffered(1)
    )


def conv_call(plan, step, info, x, kernel, gain, bias, consts):
    bt = plan.batches
    flat = lambda b, block: (0, block)
    direct, inverse, t_conv = consts[:3]
    wide = 2 * LANES
    slots = plan.conv_windows[1]
    specs = functools.partial(pair_specs, plan, step)
    return pl.pallas_call(
        functools.partial(conv_body, plan),
        grid_spec=pltpu.PrefetchScalarGridSpec(
            num_scalar_prefetch=1,
            grid=(bt,),
            in_specs=[pl.BlockSpec((1, x.shape[1], wide), lambda b, info: (b, 0, step))]
            + specs((plan.tap_rows, LANES), flat)
            + specs((1, LANES), flat)
            + specs((1, LANES), flat)
            + [whole(direct), whole(inverse), whole(t_conv)],
            out_specs=[
                pl.BlockSpec((1, plan.ext, wide), lambda b, info: (b, 0, 0)),
                pl.BlockSpec((wide, plan.chip_frames), lambda b, info: (0, b)),
            ],
            scratch_shapes=[
                pltpu.VMEM((slots, POINTS, wide), jnp.float32),
                pltpu.VMEM((POINTS, wide), jnp.float32),
                pltpu.VMEM((slots, POINTS, wide), jnp.bfloat16),
            ],
        ),
        out_shape=[
            jax.ShapeDtypeStruct((bt, plan.ext, wide), jnp.float32),
            jax.ShapeDtypeStruct((wide, bt * plan.chip_frames), jnp.bfloat16),
        ],
        compiler_params=pltpu.CompilerParams(vmem_limit_bytes=VMEM_LIMIT),
        cost_estimate=cost(4.0),
        name="conv",
    )(info, x, kernel, kernel, gain, gain, bias, bias, direct, inverse, t_conv)


def proj_body(plan, act_ref, mg_ref, out_f, out_b):
    gh, cf = plan.ghalo, plan.chip_frames
    total = None
    for b in range(plan.batches):
        part = jnp.dot(
            act_ref[:, b * cf : (b + 1) * cf],
            mg_ref[b, gh : gh + cf, :],
            preferred_element_type=jnp.float32,
        )
        total = part if total is None else total + part
    out_f[...] = total[:LANES].astype(out_f.dtype)
    out_b[...] = total[LANES:].astype(out_b.dtype)


def proj_call(plan, act, mg, kinds):
    tiles = 2
    columns = plan.width // tiles
    wide = pl.BlockSpec((LANES, columns), lambda j: (0, j))
    return pl.pallas_call(
        functools.partial(proj_body, plan),
        grid=(tiles,),
        in_specs=[
            whole(act),
            pl.BlockSpec((plan.batches, plan.ext, columns), lambda j: (0, 0, j)),
        ],
        out_specs=[wide, wide],
        out_shape=[jax.ShapeDtypeStruct((LANES, plan.width), kind) for kind in kinds],
        compiler_params=pltpu.CompilerParams(vmem_limit_bytes=VMEM_LIMIT),
        cost_estimate=cost(4.0),
        name="proj",
    )(act, mg)


def back_body(plan, info, *refs):
    x_ref = refs[0]
    k_ref, gain_ref, bias_ref = (refs[2 * i + 1 : 2 * i + 3] for i in range(3))
    halves = plan.weight_parts
    w_ref = refs[7 : 7 + 2 * halves]
    mg_ref, conv_ref, direct, segment, inverse, t_ref, lag_ref = refs[7 + 2 * halves :][:7]
    (own_ref, send_ref, stat_ref, weight, ag, gs, tail, spec, xspec, taps, cross, parts, os,
     sums) = refs[14 + 2 * halves :]
    core, offset, side_y = info[0], info[1], info[2]
    f, xh, gh, cf, ext = plan.frames, plan.xhalo, plan.ghalo, plan.chip_frames, plan.ext
    each, count = plan.back_windows
    b = pl.program_id(0)
    live = info[3 + b]
    piece = LANES // halves

    @pl.when(b == 0)
    def _():
        taps[...] = taps_spectrum(t_ref, k_ref)
        cross[...] = jnp.zeros_like(cross)
        sums[...] = jnp.zeros_like(sums)
        for block in range(2):
            for part in range(halves):
                at = (side_y + part) % halves * piece if halves > 1 else 0
                begin = pl.multiple_of(block * LANES + at, piece)
                weight[pl.ds(begin, piece), :] = w_ref[block * halves + part][...]
        gs[ext:, :] = jnp.zeros((gs.shape[0] - ext, 2 * LANES), jnp.bfloat16)
        tail[...] = jnp.zeros_like(tail)

    ag[...] = lax.dot_general(
        mg_ref[0], weight[...], (((1,), (1,)), ((), ())), preferred_element_type=jnp.float32
    )
    last_rows = cf - (count - 1) * each
    for j in range(count):
        begin = xh + j * each
        if j < count - 1:
            window = x_ref[0, begin : begin + POINTS, :]
        else:
            tail[:last_rows, :] = x_ref[0, begin : begin + last_rows, :]
            window = tail[...]
        xspec[j] = to_spectrum(segment, window)
    gain = jnp.concatenate([gain_ref[0][...], gain_ref[1][...]], axis=1)
    bias = jnp.concatenate([bias_ref[0][...], bias_ref[1][...]], axis=1)

    gain_sum = jnp.zeros((8, 2 * LANES), jnp.float32)
    bias_sum = jnp.zeros((8, 2 * LANES), jnp.float32)
    for row in range(0, ext, STEP):
        conv = conv_ref[0, row : row + STEP, :]
        pre = gain * conv + bias
        sig = sigmoid(pre)
        value = ag[row : row + STEP, :] * sig * (1.0 + pre * (1.0 - sig))
        gs[row : row + STEP, :] = (value * gain).astype(jnp.bfloat16)
        if gh <= row < gh + cf:
            fold = lambda v: jnp.sum(v.reshape(STEP // 8, 8, 2 * LANES), axis=0)
            gain_sum = gain_sum + fold(value * conv)
            bias_sum = bias_sum + fold(value)
    sums[0] += gain_sum
    sums[1] += bias_sum

    for j in range(count):
        spec[j] = to_spectrum(direct, gs[j * each : j * each + POINTS, :])
    for j in range(count):
        spectral_product(spec, taps, parts, j)
        rows = min(each, cf - j * each)
        value = from_spectrum(inverse, rows, parts, j)
        position = offset + j * each + lax.broadcasted_iota(jnp.int32, value.shape, 0)
        os[j * each : j * each + rows, :] = jnp.where(position < live, value, 0.0).astype(
            jnp.bfloat16
        )
    for row in range(0, HALF, STEP):
        up, down = slice(row, row + STEP), slice(HALF + row, HALF + row + STEP)
        total_r, total_i = cross[up, :], cross[down, :]
        for j in range(count):
            re, im, xr, xi = spec[j, up, :], spec[j, down, :], xspec[j, up, :], xspec[j, down, :]
            total_r = total_r + re * xr + im * xi
            total_i = total_i + im * xr - re * xi
        cross[up, :] = total_r
        cross[down, :] = total_i

    @pl.when(core == 0)
    def _():
        own_ref[0] = os[:f]
        send_ref[0] = os[f:]

    @pl.when(core != 0)
    def _():
        own_ref[0] = os[f:]
        send_ref[0] = os[:f]

    @pl.when(b == plan.batches - 1)
    def _():
        for row in range(0, POINTS, STEP):
            parts[0, row : row + STEP, :] = cross[row : row + STEP, :].astype(jnp.bfloat16)
        stat_ref[: plan.tap_rows] = from_spectrum(lag_ref, plan.tap_rows, parts, 0)
        total = [jnp.sum(sums[i], axis=0, keepdims=True) for i in range(2)]
        pad = jnp.zeros((plan.stat_rows - plan.tap_rows - 2, 2 * LANES), jnp.float32)
        stat_ref[plan.tap_rows :] = jnp.concatenate(total + [pad], axis=0)


def back_call(plan, step, info, mg, weights, conv, x, kernel, gain, bias, consts):
    bt = plan.batches
    flat = lambda b, block: (0, block)
    batch = lambda b, info: (b, 0, 0)
    direct, inverse, _, t_back, lags, segment = consts
    pair = (1, plan.frames, 2 * LANES)
    wide = 2 * LANES
    slots = plan.back_windows[1]
    specs = functools.partial(pair_specs, plan, step)
    piece = LANES // plan.weight_parts
    one = pl.Buffered(1)
    w_specs, w_arrays = [], []
    for array, part in weights:
        if part is None:
            index = lambda b, info: (0, 0)
        else:
            index = lambda b, info, part=part: ((info[2] + part) % plan.weight_parts, 0)
        w_specs.append(pl.BlockSpec((piece, plan.width), index, pipeline_mode=one))
        w_arrays.append(array)
    return pl.pallas_call(
        functools.partial(back_body, plan),
        grid_spec=pltpu.PrefetchScalarGridSpec(
            num_scalar_prefetch=1,
            grid=(bt,),
            in_specs=[pl.BlockSpec((1, x.shape[1], wide), lambda b, info: (b, 0, step))]
            + specs((plan.tap_rows, LANES), flat)
            + specs((1, LANES), flat)
            + specs((1, LANES), flat)
            + w_specs
            + [pl.BlockSpec((1, plan.ext, plan.width), batch)]
            + [pl.BlockSpec((1, plan.ext, wide), batch)]
            + [whole(c) for c in (direct, segment, inverse, t_back, lags)],
            out_specs=[
                pl.BlockSpec(pair, batch),
                pl.BlockSpec(pair, batch),
                pl.BlockSpec((plan.stat_rows, wide), lambda b, info: (0, 0)),
            ],
            scratch_shapes=[
                pltpu.VMEM((wide, plan.width), jnp.bfloat16),
                pltpu.VMEM((plan.ext, wide), jnp.float32),
                pltpu.VMEM((plan.window_rows(plan.back_windows), wide), jnp.bfloat16),
                pltpu.VMEM((POINTS, wide), jnp.bfloat16),
                pltpu.VMEM((slots, POINTS, wide), jnp.float32),
                pltpu.VMEM((slots, POINTS, wide), jnp.float32),
                pltpu.VMEM((POINTS, wide), jnp.float32),
                pltpu.VMEM((POINTS, wide), jnp.float32),
                pltpu.VMEM((slots, POINTS, wide), jnp.bfloat16),
                pltpu.VMEM((plan.chip_frames, wide), jnp.bfloat16),
                pltpu.VMEM((2, 8, wide), jnp.float32),
            ],
        ),
        out_shape=[
            jax.ShapeDtypeStruct((bt, plan.frames, wide), jnp.bfloat16),
            jax.ShapeDtypeStruct((bt, plan.frames, wide), jnp.bfloat16),
            jax.ShapeDtypeStruct((plan.stat_rows, wide), jnp.float32),
        ],
        compiler_params=pltpu.CompilerParams(vmem_limit_bytes=VMEM_LIMIT),
        cost_estimate=cost(8.0),
        name="back",
    )(info, x, kernel, kernel, gain, gain, bias, bias, *w_arrays, mg, conv,
      direct, segment, inverse, t_back, lags)


def place_body(plan, info, *refs):
    out_ref = refs[-1]
    for i, ref in enumerate(refs[:-1]):
        step, partner = divmod(i, 2)
        for side in range(2):
            block = info[plan.block_slot(step, side)]
            if partner:
                block = block + 1 - 2 * info[0]
            column = pl.multiple_of(block * LANES, LANES)
            out_ref[:, :, pl.ds(column, LANES)] = ref[:, :, side * LANES : (side + 1) * LANES]


def place_call(plan, info, arrays):
    shape = (plan.batches, plan.frames, plan.width)
    return pl.pallas_call(
        functools.partial(place_body, plan),
        grid_spec=pltpu.PrefetchScalarGridSpec(
            num_scalar_prefetch=1,
            grid=(1,),
            in_specs=[whole(array) for array in arrays],
            out_specs=pl.BlockSpec(shape, lambda g, info: (0, 0, 0)),
        ),
        out_shape=jax.ShapeDtypeStruct(shape, jnp.bfloat16),
        compiler_params=pltpu.CompilerParams(vmem_limit_bytes=VMEM_LIMIT),
        cost_estimate=cost(3.0),
        name="place",
    )(info, *arrays)


def deal_body(plan, info, *refs):
    out_ref = refs[-1]
    for step, ref in enumerate(refs[:-1]):
        for side in range(2):
            chip = info[plan.block_slot(step, side)] // CORES
            out_ref[chip] = ref[:, side * LANES : (side + 1) * LANES]


def deal_call(plan, info, arrays):
    shape = (plan.chips, plan.stat_rows, LANES)
    return pl.pallas_call(
        functools.partial(deal_body, plan),
        grid_spec=pltpu.PrefetchScalarGridSpec(
            num_scalar_prefetch=1,
            grid=(1,),
            in_specs=[whole(array) for array in arrays],
            out_specs=pl.BlockSpec(shape, lambda g, info: (0, 0, 0)),
        ),
        out_shape=jax.ShapeDtypeStruct(shape, jnp.float32),
        cost_estimate=cost(1.0),
        name="deal",
    )(info, *arrays)


def edge_body(plan, info, x_ref, g_ref, xe_ref, ge_ref):
    xe_ref[...] = x_ref[...]
    ge_ref[...] = g_ref[...]


def edge_call(plan, info, x, g):
    def spec(rows):
        shape = (plan.batches, rows, plan.width)
        last = plan.frames // rows - 1
        return (
            pl.BlockSpec(shape, lambda i, info: (0, info[0] * last, 0)),
            pl.BlockSpec(shape, lambda i, info: (0, 0, 0)),
            jax.ShapeDtypeStruct(shape, jnp.bfloat16),
        )

    xs, gs = spec(plan.xhalo), spec(plan.ghalo)
    return pl.pallas_call(
        functools.partial(edge_body, plan),
        grid_spec=pltpu.PrefetchScalarGridSpec(
            num_scalar_prefetch=1, grid=(1,), in_specs=[xs[0], gs[0]], out_specs=[xs[1], gs[1]]
        ),
        out_shape=[xs[2], gs[2]],
        cost_estimate=cost(1.0),
        name="edge",
    )(info, x, g)


def assemble_body(plan, halo, picked, info, own_ref, other_ref, near_ref, far_ref, out_ref):
    core, offset, live = info[0], info[1], info[3 + pl.program_id(0)]
    f = plan.frames

    def put(row, ref):
        rows = ref.shape[1]
        for part in range(0, rows, STEP):
            position = lax.broadcasted_iota(jnp.int32, (STEP, LANES), 0) + (
                offset - halo + row + part
            )
            keep = jnp.where(position < live, 1.0, 0.0).astype(jnp.bfloat16)
            for i in range(plan.chips if picked else plan.count):
                if picked:
                    column = pl.multiple_of(info[plan.block_slot(0, i)] * LANES, LANES)
                else:
                    column = i * LANES
                out_ref[0, row + part : row + part + STEP, i * LANES : (i + 1) * LANES] = (
                    ref[0, part : part + STEP, pl.ds(column, LANES)] * keep
                )

    @pl.when(core == 0)
    def _():
        put(0, near_ref)
        put(halo, own_ref)
        put(halo + f, other_ref)
        put(halo + 2 * f, far_ref)

    @pl.when(core != 0)
    def _():
        put(0, far_ref)
        put(halo, other_ref)
        put(halo + f, own_ref)
        put(halo + 2 * f, near_ref)

    total = 2 * (halo + f)
    if out_ref.shape[1] > total:
        out_ref[0, total:, :] = jnp.zeros(
            (out_ref.shape[1] - total, out_ref.shape[2]), jnp.bfloat16
        )


def assemble_call(plan, info, own, other, near, far, rows, picked):
    halo = near.shape[1]
    width = plan.width // CORES if picked else plan.width
    spec = lambda n: pl.BlockSpec((1, n, plan.width), lambda b, info: (b, 0, 0))
    return pl.pallas_call(
        functools.partial(assemble_body, plan, halo, picked),
        grid_spec=pltpu.PrefetchScalarGridSpec(
            num_scalar_prefetch=1,
            grid=(plan.batches,),
            in_specs=[spec(plan.frames), spec(plan.frames), spec(halo), spec(halo)],
            out_specs=pl.BlockSpec((1, rows, width), lambda b, info: (b, 0, 0)),
        ),
        out_shape=jax.ShapeDtypeStruct((plan.batches, rows, width), jnp.bfloat16),
        compiler_params=pltpu.CompilerParams(vmem_limit_bytes=VMEM_LIMIT),
        cost_estimate=cost(3.0),
        name="assemble",
    )(info, own, other, near, far)


def after(value, *others):
    return lax.optimization_barrier((value, *others))[0]


def ring_shards(plan, grad_out, saved_input, lengths, kernel, gain, bias, proj_weight):
    f, xh, gh = plan.frames, plan.xhalo, plan.ghalo
    index = lax.axis_index("shard")
    group = lax.axis_index("groups")
    core, chip = index % CORES, index // CORES
    place = plan.position_of(chip)
    forward, backward = plan.ring()
    offset = chip * plan.chip_frames
    scale = lax.rsqrt(jnp.sum(lengths).astype(jnp.float32))
    pairs = plan.pairs
    far = jnp.asarray([d for pair in pairs for d in pair], jnp.int32)
    owned = CORES * plan.chip_at((place + far + plan.chips) % plan.chips) + core
    info = jnp.concatenate([jnp.stack([core, offset, group]), lengths, owned]).astype(jnp.int32)
    gain2, bias2 = gain.reshape(1, -1), bias.reshape(1, -1)
    taps = jnp.pad(kernel, ((0, plan.tap_rows - plan.taps), (0, 0)))
    consts = [jnp.asarray(c) for c in transforms(plan)]

    x_edge, g_edge = edge_call(plan, info, saved_input, grad_out)
    xa = lax.ppermute(x_edge, "shard", plan.edges())
    xp = lax.ppermute(saved_input, "shard", plan.partners())
    xb = lax.ppermute(xa, "shard", plan.partners())
    mgp = lax.ppermute(grad_out, "shard", plan.partners())
    ga = lax.ppermute(after(g_edge, xa), "shard", plan.edges())
    gb = lax.ppermute(ga, "shard", plan.partners())
    x = assemble_call(
        plan, info, saved_input, xp, xa, xb, plan.window_rows(plan.conv_windows), True
    )
    mg = assemble_call(plan, info, grad_out, mgp, ga, gb, plan.ext, False)

    convs, products = [], []
    order = info
    for step in range(plan.rounds):
        conv, act = conv_call(plan, step, order, x, taps, gain2, bias2, consts)
        convs.append(conv)
        kinds = [jnp.bfloat16 if step == 0 else jnp.float32] * 2
        products.append(proj_call(plan, act, mg, kinds))
        order = after(info, products[-1][0])

    parts = plan.weight_parts
    piece = LANES // parts
    if parts > 1:
        start = lax.dynamic_slice_in_dim(after(proj_weight, xa), group * piece, piece, 0)
    else:
        start = after(proj_weight, xa)
    swap = [
        (g * plan.count + s, (1 - g) * plan.count + s)
        for g in range(parts) for s in range(plan.count)
    ]

    def both(half):
        if parts == 1:
            return [(half, None)]
        return [(half, None), (lax.ppermute(half, ("groups", "shard"), swap), None)]

    weights = {0: [(proj_weight, part) for part in range(parts)]}
    going_f = going_b = start
    for step in range(1, plan.rounds + 1):
        if step > 1:
            going_f, going_b, _ = lax.optimization_barrier(
                (going_f, going_b, products[step - 1][0])
            )
        going_f = lax.ppermute(going_f, "shard", forward)
        weights[-step] = both(going_f)
        if step < plan.rounds:
            going_b = lax.ppermute(going_b, "shard", backward)
            weights[step] = both(going_b)
    weights[plan.rounds] = weights.pop(-plan.rounds)

    def added(product, received):
        return product + received.astype(jnp.float32)

    sends = []
    send_f, send_b = products[0]
    for step in range(plan.rounds):
        recv_f = lax.ppermute(send_f, "shard", forward)
        if step < plan.rounds - 1:
            recv_b = lax.ppermute(send_b, "shard", backward)
            product_f, product_b = products[step + 1]
            send_f = added(product_f, recv_f).astype(jnp.bfloat16)
            send_b = added(product_b, recv_b)
            if step < plan.rounds - 2:
                send_b = send_b.astype(jnp.bfloat16)
            sends.append(send_f)
    proj_grad = added(send_b, recv_f) * scale

    pieces, stats = {}, {}
    for turn, step in enumerate(reversed(range(plan.rounds))):
        pair = pairs[step]
        behind = turn if turn < 2 else turn - 1
        order = after(info, sends[min(behind, len(sends) - 1)], products[-1][0])
        own, send, stats[step] = back_call(
            plan, step, order, mg, weights[pair[0]] + weights[pair[1]],
            convs[step], x, taps, gain2, bias2, consts,
        )
        pieces[step] = [own, lax.ppermute(send, "shard", plan.partners())]
    full = place_call(plan, info, [a for step in range(plan.rounds) for a in pieces[step]])

    dealt = deal_call(plan, info, [stats[step] for step in range(plan.rounds)])
    groups = [[CORES * p + c for p in range(plan.chips)] for c in range(CORES)]
    summed = jnp.sum(
        lax.all_to_all(dealt, "shard", 0, 0, axis_index_groups=groups), axis=0
    ) * scale
    return (
        full, proj_grad, summed[: plan.taps], summed[plan.tap_rows : plan.tap_rows + 2]
    )


def shards(count, group_count, grad_out, saved_input, lengths, kernel, gain, bias, proj_weight):
    batches, frames, model_width = grad_out.shape
    plan = Plan(count, group_count, batches, frames, model_width, kernel.shape[0])
    args = (grad_out, saved_input, lengths, kernel, gain, bias, proj_weight)
    return ring_shards(plan, *args) if plan.usable() else plain_shards(*args)


def solution(mesh):
    placed = (
        P("groups", "shard", None),
        P("groups", "shard", None),
        P("groups"),
        P(),
        P(),
        P(),
        P("shard", None),
    )
    return jax.shard_map(
        functools.partial(shards, mesh.shape["shard"], mesh.shape["groups"]),
        mesh=mesh,
        in_specs=placed,
        out_specs=(
            P("groups", "shard", None),
            P(("groups", "shard"), None),
            P("groups", "shard"),
            P("groups", "shard"),
        ),
        check_vma=False,
    )
```

```python
import functools

import jax
import jax.numpy as jnp
import numpy as np
from jax import lax
from jax.experimental import pallas as pl
from jax.experimental.pallas import tpu as pltpu
from jax.sharding import PartitionSpec as P

LANES = 128
CORES = 2
VMEM_LIMIT = 56 * 1024 * 1024
POINTS = 256


def cost(micros):
    return pl.CostEstimate(flops=0, transcendentals=0, bytes_accessed=int(micros * 3.6e6))


def extended(block, width):
    count = lax.axis_size("shard")
    forward = [(i, i + 1) for i in range(count - 1)]
    backward = [(target, source) for source, target in forward]
    low = lax.ppermute(block[:, block.shape[1] - width :], "shard", forward)
    high = lax.ppermute(block[:, :width], "shard", backward)
    return jnp.concatenate([low, block, high], axis=1)


def frame_mask(lengths, offset, count):
    position = offset + jnp.arange(count, dtype=jnp.int32)
    return (position[None, :] < lengths[:, None])[:, :, None]


def plain_shards(grad_out, saved_input, lengths, kernel, gain, bias, proj_weight):
    batches, frames, model_width = grad_out.shape
    tap_count = kernel.shape[0]
    half_span = (tap_count - 1) // 2
    offset = lax.axis_index("shard") * frames
    norm_scale = lax.rsqrt(jnp.sum(lengths).astype(jnp.float32))
    own_mask = frame_mask(lengths, offset, frames)
    masked_in = jnp.where(own_mask, saved_input, jnp.zeros_like(saved_input))
    masked_grad = jnp.where(own_mask, grad_out, jnp.zeros_like(grad_out))
    in_ext = extended(masked_in, half_span)
    conv = jnp.zeros(grad_out.shape, jnp.float32)
    for tap in range(tap_count):
        conv = conv + kernel[tap] * in_ext[:, tap : tap + frames].astype(jnp.float32)
    pre_act = gain * conv + bias
    gate_sig = jax.nn.sigmoid(pre_act)
    activated = (pre_act * gate_sig).astype(jnp.bfloat16)
    rows = masked_grad.reshape(batches * frames, model_width)
    weight = lax.all_gather(proj_weight, "shard", axis=0, tiled=True)
    act_grad = lax.dot_general(
        rows, weight, (((1,), (1,)), ((), ())), preferred_element_type=jnp.float32
    ).reshape(batches, frames, model_width)
    pre_grad = act_grad * gate_sig * (1.0 + pre_act * (1.0 - gate_sig))
    conv_grad = (pre_grad * gain).astype(jnp.bfloat16)
    grad_ext = extended(conv_grad, half_span)
    back_sum = jnp.zeros(grad_out.shape, jnp.float32)
    grad_float = conv_grad.astype(jnp.float32)
    tap_rows = []
    for tap in range(tap_count):
        begin = 2 * half_span - tap
        back_sum = back_sum + kernel[tap] * grad_ext[:, begin : begin + frames].astype(jnp.float32)
        tap_rows.append(
            jnp.sum(in_ext[:, tap : tap + frames].astype(jnp.float32) * grad_float, axis=(0, 1))
        )
    input_grad = jnp.where(own_mask, back_sum, 0.0).astype(jnp.bfloat16)
    tap_rows.append(jnp.sum(pre_grad * conv, axis=(0, 1)))
    tap_rows.append(jnp.sum(pre_grad, axis=(0, 1)))
    stats = jnp.stack(tap_rows, 0) * norm_scale
    summed = lax.psum_scatter(stats, "shard", scatter_dimension=1, tiled=True)
    product = lax.dot_general(
        activated.reshape(batches * frames, model_width),
        rows,
        (((0,), (0,)), ((), ())),
        preferred_element_type=jnp.float32,
    )
    proj_grad = lax.psum_scatter(product * norm_scale, "shard", scatter_dimension=0, tiled=True)
    return (input_grad, proj_grad, summed[:tap_count], summed[tap_count:])


class Plan:
    def __init__(self, count, groups, batches, frames, model_width, tap_count):
        self.count = count
        self.chips = count // CORES
        self.rounds = self.chips // 2
        self.batches = batches
        self.frames = frames
        self.chip_frames = CORES * frames
        self.width = model_width
        self.block = model_width // count
        self.taps = tap_count
        self.half = (tap_count - 1) // 2
        self.ghalo = -(-self.half // 16) * 16
        self.xhalo = 2 * self.ghalo
        self.ext = self.chip_frames + 2 * self.ghalo
        self.xext = self.chip_frames + 2 * self.xhalo
        self.tap_rows = -(-tap_count // 16) * 16
        self.stat_rows = self.tap_rows + 8
        self.weight_parts = 2 if groups == 2 else 1
        self.pairs = [(h, 1 - h) for h in range(self.rounds, 0, -1)]
        self.conv_windows = windows(self.ext, self.xhalo - self.ghalo - self.half + tap_count)
        self.back_windows = windows(self.chip_frames, self.ghalo + self.half + 1)

    def window_rows(self, found):
        return found[0] * (found[1] - 1) + POINTS

    def block_slot(self, step, side):
        return 3 + self.batches + 2 * step + side

    def usable(self):
        return (
            self.count % (2 * CORES) == 0
            and self.block == LANES
            and self.block * self.count == self.width
            and self.frames % 128 == 0
            and self.frames >= self.xhalo
            and self.taps % 2 == 1
            and 4 * self.ghalo <= POINTS // 2
            and self.window_rows(self.conv_windows) >= self.xext
            and self.window_rows(self.back_windows) >= self.ext
            and self.window_rows(self.conv_windows)
            >= self.xhalo + self.window_rows(self.back_windows) - self.back_windows[0]
            and self.chips == 8
            and self.batches == 2
        )

    def chip_at(self, position):
        half = self.chips // 2
        return jnp.where(position < half, 2 * position, 2 * (self.chips - 1 - position) + 1)

    def position_of(self, chip):
        return jnp.where(chip % 2 == 0, chip // 2, self.chips - 1 - chip // 2)

    def ring(self):
        half = self.chips // 2
        order = [2 * i for i in range(half)] + [2 * i + 1 for i in reversed(range(half))]
        forward = []
        for core in range(CORES):
            for i in range(self.chips):
                source, target = order[i], order[(i + 1) % self.chips]
                forward.append((CORES * source + core, CORES * target + core))
        return forward, [(t, s) for s, t in forward]

    def edges(self):
        pairs = []
        for chip in range(self.chips - 1):
            last, first = CORES * chip + 1, CORES * (chip + 1)
            pairs += [(last, first), (first, last)]
        return pairs

    def edges_like(self):
        pairs = []
        for chip in range(self.chips - 1):
            pairs.append((CORES * chip + 1, CORES * (chip + 1) + 1))
            pairs.append((CORES * (chip + 1), CORES * chip))
        return pairs

    def partners(self):
        return [(s, s ^ 1) for s in range(self.count)]


def sigmoid(value):
    return 0.5 * jnp.tanh(0.5 * value) + 0.5


def split(value):
    high = value.astype(jnp.bfloat16)
    return high, (value - high.astype(jnp.float32)).astype(jnp.bfloat16)


def split_matrix(matrix):
    high = matrix.astype(jnp.bfloat16)
    return high, (matrix - high.astype(np.float64)).astype(jnp.bfloat16)


def transforms(plan):
    time = np.arange(POINTS)
    theta = np.pi * (2 * np.arange(POINTS // 2) + 1) / POINTS
    angle = theta[:, None] * time[None, :]
    direct = np.concatenate([np.cos(angle), -np.sin(angle)], 0)
    inverse = direct.T * (2.0 / POINTS)

    def spectrum(lags):
        phase = theta[:, None] * lags[None, :]
        matrix = np.concatenate([np.cos(phase), np.sin(phase)], 0)
        return np.pad(matrix, ((0, 0), (0, plan.tap_rows - plan.taps)))

    taps = np.arange(plan.taps)
    back_lags = plan.ghalo + plan.half - taps
    lag_rows = np.pad(inverse[back_lags], ((0, plan.tap_rows - plan.taps), (0, 0)))
    half = lambda m: m.astype(jnp.bfloat16)
    conv_lags = plan.xhalo - plan.ghalo - plan.half + taps
    return (
        half(direct),
        half(inverse),
        np.stack(split_matrix(spectrum(conv_lags))),
        np.stack(split_matrix(spectrum(back_lags))),
        np.stack(split_matrix(lag_rows)),
        half(direct * (time < plan.back_windows[0])),
    )


def taps_spectrum(t_ref, k_ref):
    high, low = split(jnp.concatenate([k_ref[0][...], k_ref[1][...]], axis=1))
    dot = functools.partial(jnp.dot, preferred_element_type=jnp.float32)
    return dot(t_ref[0], high) + dot(t_ref[1], high) + dot(t_ref[0], low)


def to_spectrum(direct_ref, window):
    return jnp.dot(direct_ref[...], window, preferred_element_type=jnp.float32)


def from_spectrum(inverse_ref, rows, parts, slot):
    return jnp.dot(inverse_ref[:rows, :], parts[slot], preferred_element_type=jnp.float32)


def windows(rows_out, reach):
    count = -(-rows_out // ((POINTS - reach) // 16 * 16))
    return -(-rows_out // count // 16) * 16, count


STEP = 16
HALF = POINTS // 2


def spectral_product(spec, taps, parts, slot):
    for row in range(0, HALF, STEP):
        up, down = slice(row, row + STEP), slice(HALF + row, HALF + row + STEP)
        re, im, kr, ks = spec[slot, up, :], spec[slot, down, :], taps[up, :], taps[down, :]
        parts[slot, up, :] = (re * kr - im * ks).astype(jnp.bfloat16)
        parts[slot, down, :] = (re * ks + im * kr).astype(jnp.bfloat16)


def conv_body(plan, info, *refs):
    x_ref = refs[0]
    k_ref, gain_ref, bias_ref = (refs[2 * i + 1 : 2 * i + 3] for i in range(3))
    direct, inverse, t_ref, mg_ref = refs[7:11]
    conv_ref, out_f, out_b, spec, taps, parts, act, acc = refs[11:]
    each, count = plan.conv_windows
    gh, cf = plan.ghalo, plan.chip_frames
    b = pl.program_id(0)

    @pl.when(b == 0)
    def _():
        taps[...] = taps_spectrum(t_ref, k_ref)

    for j in range(count):
        spec[j] = to_spectrum(direct, x_ref[0, j * each : j * each + POINTS, :])
    for j in range(count):
        spectral_product(spec, taps, parts, j)
        rows = min(each, plan.ext - j * each)
        conv_ref[0, j * each : j * each + rows, :] = from_spectrum(inverse, rows, parts, j)

    for i in range(cf // LANES):
        for side in range(2):
            lanes = slice(side * LANES, (side + 1) * LANES)
            begin = gh + i * LANES
            conv = conv_ref[0, begin : begin + LANES, lanes]
            pre = gain_ref[side][...] * conv + bias_ref[side][...]
            act[lanes, i * LANES : (i + 1) * LANES] = (pre * sigmoid(pre)).T.astype(jnp.bfloat16)

    def product(columns):
        return jnp.dot(
            act[...], mg_ref[0, gh : gh + cf, columns], preferred_element_type=jnp.float32
        )

    tiles = [slice(c, c + 2 * LANES) for c in range(0, plan.width, 2 * LANES)]

    @pl.when(b == 0)
    def _():
        for columns in tiles:
            acc[:, columns] = product(columns)

    @pl.when(b != 0)
    def _():
        for columns in tiles:
            total = acc[:, columns] + product(columns)
            if plan.batches > 2:
                acc[:, columns] = total
            out_f[:, columns] = total[:LANES].astype(out_f.dtype)
            out_b[:, columns] = total[LANES:].astype(out_b.dtype)


def pair_specs(plan, step, shape, index):
    return [
        pl.BlockSpec(
            shape, lambda b, info, at=plan.block_slot(step, side): index(b, info[at])
        )
        for side in range(2)
    ]


def whole(array):
    return pl.BlockSpec(
        array.shape, lambda *_: (0,) * array.ndim, pipeline_mode=pl.Buffered(1)
    )


def conv_call(plan, step, info, x, mg, kernel, gain, bias, consts, kind):
    bt = plan.batches
    flat = lambda b, block: (0, block)
    fixed = lambda b, info: (0, 0)
    direct, inverse, t_conv = consts[:3]
    wide = 2 * LANES
    slots = plan.conv_windows[1]
    specs = functools.partial(pair_specs, plan, step)
    return pl.pallas_call(
        functools.partial(conv_body, plan),
        grid_spec=pltpu.PrefetchScalarGridSpec(
            num_scalar_prefetch=1,
            grid=(bt,),
            in_specs=[pl.BlockSpec((1, x.shape[1], wide), lambda b, info: (b, 0, step))]
            + specs((plan.tap_rows, LANES), flat)
            + specs((1, LANES), flat)
            + specs((1, LANES), flat)
            + [whole(direct), whole(inverse), whole(t_conv)]
            + [pl.BlockSpec((1, plan.ext, plan.width), lambda b, info: (b, 0, 0))],
            out_specs=[
                pl.BlockSpec((1, plan.ext, wide), lambda b, info: (b, 0, 0)),
                pl.BlockSpec((LANES, plan.width), fixed),
                pl.BlockSpec((LANES, plan.width), fixed),
            ],
            scratch_shapes=[
                pltpu.VMEM((slots, POINTS, wide), jnp.float32),
                pltpu.VMEM((POINTS, wide), jnp.float32),
                pltpu.VMEM((slots, POINTS, wide), jnp.bfloat16),
                pltpu.VMEM((wide, plan.chip_frames), jnp.bfloat16),
                pltpu.VMEM((wide, plan.width), jnp.float32),
            ],
        ),
        out_shape=[
            jax.ShapeDtypeStruct((bt, plan.ext, wide), jnp.float32),
            jax.ShapeDtypeStruct((LANES, plan.width), kind),
            jax.ShapeDtypeStruct((LANES, plan.width), kind),
        ],
        compiler_params=pltpu.CompilerParams(vmem_limit_bytes=VMEM_LIMIT),
        cost_estimate=cost(6.0),
        name="conv",
    )(info, x, kernel, kernel, gain, gain, bias, bias, direct, inverse, t_conv, mg)


def back_body(plan, steps, sources, info, *refs):
    pairs = len(steps)
    x_ref, mg_ref = refs[:2]
    k_refs, gain_refs, bias_refs = (
        refs[2 + 2 * pairs * i : 2 + 2 * pairs * (i + 1)] for i in range(3)
    )
    refs = refs[2 + 6 * pairs :]
    conv_refs, w_refs = refs[:pairs], refs[pairs : -23]
    direct, segment, inverse, t_ref, lag_ref = refs[-23:-18]
    (own_ref, send_ref, stat_ref, weight, conv_buf, ag, gs, tail, spec, xspec, taps, cross,
     parts, os, sums, flat, w_sem, c_sem) = refs[-18:]
    core, offset, side_y = info[0], info[1], info[2]
    f, xh, gh, cf, ext = plan.frames, plan.xhalo, plan.ghalo, plan.chip_frames, plan.ext
    each, count = plan.back_windows
    turn, b = pl.program_id(0), pl.program_id(1)
    live = info[3 + b]

    def weight_copies(pair):
        made = []
        for n, (array, part, target, begin, rows) in enumerate(sources[pair]):
            first, into = begin, target * LANES
            if part is not None:
                at = pl.multiple_of((side_y + part) % 2 * rows, rows)
                if part < 0:
                    at = pl.multiple_of((side_y - part - 1) % 2 * rows, rows)
                    first = pl.multiple_of(begin + at, rows)
                into = pl.multiple_of(target * LANES + at, rows)
            made.append(
                pltpu.make_async_copy(
                    w_refs[array].at[pl.ds(first, rows), :],
                    weight.at[pair, pl.ds(into, rows), :],
                    w_sem.at[pair, n],
                )
            )
        return made

    def conv_copies(pair):
        return [
            pltpu.make_async_copy(conv_refs[pair].at[i], conv_buf.at[pair, i], c_sem.at[pair, i])
            for i in range(plan.batches)
        ]

    @pl.when((turn == 0) & (b == 0))
    def _():
        for pair in range(pairs):
            for copy in weight_copies(pair) + conv_copies(pair):
                copy.start()
        gs[ext:, :] = jnp.zeros((gs.shape[0] - ext, 2 * LANES), jnp.bfloat16)
        tail[...] = jnp.zeros_like(tail)

    for pair in range(pairs):

        @pl.when((turn == pair) & (b == 0))
        def _():
            taps[...] = taps_spectrum(t_ref, k_refs[2 * pair : 2 * pair + 2])
            for row, pick in ((0, gain_refs), (8, bias_refs)):
                for side in range(2):
                    lanes = slice(side * LANES, (side + 1) * LANES)
                    flat[row : row + 8, lanes] = jnp.broadcast_to(
                        pick[2 * pair + side][...], (8, LANES)
                    )
            cross[...] = jnp.zeros_like(cross)
            sums[...] = jnp.zeros_like(sums)

    last_rows = cf - (count - 1) * each
    for j in range(count):
        begin = xh + j * each
        if j < count - 1:
            window = x_ref[0, begin : begin + POINTS, :]
        else:
            tail[:last_rows, :] = x_ref[0, begin : begin + last_rows, :]
            window = tail[...]
        xspec[j] = to_spectrum(segment, window)

    for pair in range(pairs):

        @pl.when((turn == pair) & (b == 0))
        def _():
            for copy in weight_copies(pair) + conv_copies(pair):
                copy.wait()

    ag[...] = lax.dot_general(
        mg_ref[0], weight[turn], (((1,), (1,)), ((), ())), preferred_element_type=jnp.float32
    )
    gain, bias = flat[:1, :], flat[8:9, :]

    gain_sum = jnp.zeros((8, 2 * LANES), jnp.float32)
    bias_sum = jnp.zeros((8, 2 * LANES), jnp.float32)
    for row in range(0, ext, STEP):
        conv = conv_buf[turn, b, row : row + STEP, :]
        pre = gain * conv + bias
        sig = sigmoid(pre)
        value = ag[row : row + STEP, :] * sig * (1.0 + pre * (1.0 - sig))
        gs[row : row + STEP, :] = (value * gain).astype(jnp.bfloat16)
        if gh <= row < gh + cf:
            fold = lambda v: jnp.sum(v.reshape(STEP // 8, 8, 2 * LANES), axis=0)
            gain_sum = gain_sum + fold(value * conv)
            bias_sum = bias_sum + fold(value)
    sums[0] += gain_sum
    sums[1] += bias_sum

    for j in range(count):
        spec[j] = to_spectrum(direct, gs[j * each : j * each + POINTS, :])
    for j in range(count):
        spectral_product(spec, taps, parts, j)
        rows = min(each, cf - j * each)
        value = from_spectrum(inverse, rows, parts, j)
        position = offset + j * each + lax.broadcasted_iota(jnp.int32, value.shape, 0)
        os[j * each : j * each + rows, :] = jnp.where(position < live, value, 0.0).astype(
            jnp.bfloat16
        )
    for row in range(0, HALF, STEP):
        up, down = slice(row, row + STEP), slice(HALF + row, HALF + row + STEP)
        total_r, total_i = cross[up, :], cross[down, :]
        for j in range(count):
            re, im, xr, xi = spec[j, up, :], spec[j, down, :], xspec[j, up, :], xspec[j, down, :]
            total_r = total_r + re * xr + im * xi
            total_i = total_i + im * xr - re * xi
        cross[up, :] = total_r
        cross[down, :] = total_i

    @pl.when(core == 0)
    def _():
        own_ref[0, 0] = os[:f]
        send_ref[0, 0] = os[f:]

    @pl.when(core != 0)
    def _():
        own_ref[0, 0] = os[f:]
        send_ref[0, 0] = os[:f]

    @pl.when(b == plan.batches - 1)
    def _():
        high, low = split(cross[...])
        dot = functools.partial(jnp.dot, preferred_element_type=jnp.float32)
        stat_ref[0, : plan.tap_rows] = (
            dot(lag_ref[0], high) + dot(lag_ref[1], high) + dot(lag_ref[0], low)
        )
        total = [jnp.sum(sums[i], axis=0, keepdims=True) for i in range(2)]
        pad = jnp.zeros((plan.stat_rows - plan.tap_rows - 2, 2 * LANES), jnp.float32)
        stat_ref[0, plan.tap_rows :] = jnp.concatenate(total + [pad], axis=0)


def back_call(plan, steps, info, mg, sources, arrays, convs, x, kernel, gain, bias, consts):
    bt, pairs = plan.batches, len(steps)
    direct, inverse, _, t_back, lags, segment = consts
    wide = 2 * LANES
    slots = plan.back_windows[1]
    any_space = pl.BlockSpec(memory_space=pl.ANY)
    first, down = steps[0], steps[0] - steps[-1]
    assert list(steps) == list(range(first, first - pairs, -1)) and down == pairs - 1

    def by_block(shape):
        return [
            pl.BlockSpec(
                shape, lambda p, b, info, at=plan.block_slot(step, side): (0, info[at]),
                pipeline_mode=pl.Buffered(1),
            )
            for step in steps for side in range(2)
        ]

    each = lambda *tail: pl.BlockSpec((1, 1) + tail, lambda p, b, info: (p, b, 0, 0))
    most = max(len(source) for source in sources)
    return pl.pallas_call(
        functools.partial(back_body, plan, steps, sources),
        grid_spec=pltpu.PrefetchScalarGridSpec(
            num_scalar_prefetch=1,
            grid=(pairs, bt),
            in_specs=[
                pl.BlockSpec((1, x.shape[1], wide), lambda p, b, info: (b, 0, first - p)),
                pl.BlockSpec((1, plan.ext, plan.width), lambda p, b, info: (b, 0, 0)),
            ]
            + by_block((plan.tap_rows, LANES))
            + by_block((1, LANES))
            + by_block((1, LANES))
            + [any_space] * (pairs + len(arrays))
            + [whole(c) for c in (direct, segment, inverse, t_back, lags)],
            out_specs=[
                each(plan.frames, wide),
                each(plan.frames, wide),
                pl.BlockSpec((1, plan.stat_rows, wide), lambda p, b, info: (p, 0, 0)),
            ],
            scratch_shapes=[
                pltpu.VMEM((pairs, wide, plan.width), jnp.bfloat16),
                pltpu.VMEM((pairs, bt, plan.ext, wide), jnp.float32),
                pltpu.VMEM((plan.ext, wide), jnp.float32),
                pltpu.VMEM((plan.window_rows(plan.back_windows), wide), jnp.bfloat16),
                pltpu.VMEM((POINTS, wide), jnp.bfloat16),
                pltpu.VMEM((slots, POINTS, wide), jnp.float32),
                pltpu.VMEM((slots, POINTS, wide), jnp.float32),
                pltpu.VMEM((POINTS, wide), jnp.float32),
                pltpu.VMEM((POINTS, wide), jnp.float32),
                pltpu.VMEM((slots, POINTS, wide), jnp.bfloat16),
                pltpu.VMEM((plan.chip_frames, wide), jnp.bfloat16),
                pltpu.VMEM((2, 8, wide), jnp.float32),
                pltpu.VMEM((16, wide), jnp.float32),
                pltpu.SemaphoreType.DMA((pairs, most)),
                pltpu.SemaphoreType.DMA((pairs, bt)),
            ],
        ),
        out_shape=[
            jax.ShapeDtypeStruct((pairs, bt, plan.frames, wide), jnp.bfloat16),
            jax.ShapeDtypeStruct((pairs, bt, plan.frames, wide), jnp.bfloat16),
            jax.ShapeDtypeStruct((pairs, plan.stat_rows, wide), jnp.float32),
        ],
        compiler_params=pltpu.CompilerParams(vmem_limit_bytes=VMEM_LIMIT),
        cost_estimate=cost(6.0 * pairs),
        name="back",
    )(info, x, mg, *[kernel] * 2 * pairs, *[gain] * 2 * pairs, *[bias] * 2 * pairs,
      *convs, *arrays, direct, segment, inverse, t_back, lags)


def place_body(plan, calls, info, *refs):
    out_ref = refs[-1]
    for i, ref in enumerate(refs[:-1]):
        for turn, step in enumerate(calls[i // 2]):
            for side in range(2):
                block = info[plan.block_slot(step, side)]
                if i % 2:
                    block = block + 1 - 2 * info[0]
                column = pl.multiple_of(block * LANES, LANES)
                lanes = slice(side * LANES, (side + 1) * LANES)
                out_ref[:, :, pl.ds(column, LANES)] = ref[turn, :, :, lanes]


def place_call(plan, calls, info, arrays):
    shape = (plan.batches, plan.frames, plan.width)
    return pl.pallas_call(
        functools.partial(place_body, plan, calls),
        grid_spec=pltpu.PrefetchScalarGridSpec(
            num_scalar_prefetch=1,
            grid=(1,),
            in_specs=[whole(array) for array in arrays],
            out_specs=pl.BlockSpec(shape, lambda g, info: (0, 0, 0)),
        ),
        out_shape=jax.ShapeDtypeStruct(shape, jnp.bfloat16),
        compiler_params=pltpu.CompilerParams(vmem_limit_bytes=VMEM_LIMIT),
        cost_estimate=cost(3.0),
        name="place",
    )(info, *arrays)


def deal_body(plan, calls, info, *refs):
    out_ref = refs[-1]
    for steps, ref in zip(calls, refs[:-1]):
        for turn, step in enumerate(steps):
            for side in range(2):
                chip = info[plan.block_slot(step, side)] // CORES
                out_ref[chip] = ref[turn, :, side * LANES : (side + 1) * LANES]


def deal_call(plan, calls, info, arrays):
    shape = (plan.chips, plan.stat_rows, LANES)
    return pl.pallas_call(
        functools.partial(deal_body, plan, calls),
        grid_spec=pltpu.PrefetchScalarGridSpec(
            num_scalar_prefetch=1,
            grid=(1,),
            in_specs=[whole(array) for array in arrays],
            out_specs=pl.BlockSpec(shape, lambda g, info: (0, 0, 0)),
        ),
        out_shape=jax.ShapeDtypeStruct(shape, jnp.float32),
        cost_estimate=cost(1.0),
        name="deal",
    )(info, *arrays)


def edge_body(plan, x_first, x_last, g_first, g_last, near_ref, far_ref, g_ref):
    core = lax.axis_index("shard") % CORES

    def take(owner, x_ref, grad_ref):
        for i in range(plan.chips):
            for out, parity in ((near_ref, 1 - owner), (far_ref, owner)):
                column = (CORES * i + parity) * LANES
                out[:, :, i * LANES : (i + 1) * LANES] = x_ref[:, :, column : column + LANES]
        g_ref[...] = grad_ref[...]

    pl.when(core == 0)(lambda: take(0, x_first, g_first))
    pl.when(core != 0)(lambda: take(1, x_last, g_last))


def edge_call(plan, x, g):
    def spec(rows, first):
        shape = (plan.batches, rows, plan.width)
        block = 0 if first else plan.frames // rows - 1
        return pl.BlockSpec(shape, lambda i: (0, block, 0))

    xh, gh = plan.xhalo, plan.ghalo
    half = (plan.batches, xh, plan.width // CORES)
    shapes = [half, half, (plan.batches, gh, plan.width)]
    return pl.pallas_call(
        functools.partial(edge_body, plan),
        grid=(1,),
        in_specs=[spec(xh, True), spec(xh, False), spec(gh, True), spec(gh, False)],
        out_specs=[pl.BlockSpec(shape, lambda i: (0, 0, 0)) for shape in shapes],
        out_shape=[jax.ShapeDtypeStruct(shape, jnp.bfloat16) for shape in shapes],
        cost_estimate=cost(1.0),
        name="edge",
    )(x, x, g, g)


def assemble_body(plan, halo, picked, info, own_ref, other_ref, near_ref, far_ref, out_ref):
    core, offset, live = info[0], info[1], info[3 + pl.program_id(0)]
    f = plan.frames

    def put(row, ref):
        rows = ref.shape[1]
        for part in range(0, rows, STEP):
            position = lax.broadcasted_iota(jnp.int32, (STEP, LANES), 0) + (
                offset - halo + row + part
            )
            keep = jnp.where(position < live, 1.0, 0.0).astype(jnp.bfloat16)
            for i in range(plan.chips if picked else plan.count):
                column = i * LANES
                if picked:
                    block = info[plan.block_slot(0, i)]
                    if rows == halo:
                        block = block // CORES
                    column = pl.multiple_of(block * LANES, LANES)
                out_ref[0, row + part : row + part + STEP, i * LANES : (i + 1) * LANES] = (
                    ref[0, part : part + STEP, pl.ds(column, LANES)] * keep
                )

    @pl.when(core == 0)
    def _():
        put(0, near_ref)
        put(halo, own_ref)
        put(halo + f, other_ref)
        put(halo + 2 * f, far_ref)

    @pl.when(core != 0)
    def _():
        put(0, far_ref)
        put(halo, other_ref)
        put(halo + f, own_ref)
        put(halo + 2 * f, near_ref)

    total = 2 * (halo + f)
    if out_ref.shape[1] > total:
        out_ref[0, total:, :] = jnp.zeros(
            (out_ref.shape[1] - total, out_ref.shape[2]), jnp.bfloat16
        )


def assemble_call(plan, info, own, other, near, far, rows, picked):
    halo = near.shape[1]
    width = plan.width // CORES if picked else plan.width
    spec = lambda n: pl.BlockSpec((1, n, plan.width), lambda b, info: (b, 0, 0))
    return pl.pallas_call(
        functools.partial(assemble_body, plan, halo, picked),
        grid_spec=pltpu.PrefetchScalarGridSpec(
            num_scalar_prefetch=1,
            grid=(plan.batches,),
            in_specs=[spec(plan.frames), spec(plan.frames)]
            + [pl.BlockSpec((1, halo, width), lambda b, info: (b, 0, 0))] * 2,
            out_specs=pl.BlockSpec((1, rows, width), lambda b, info: (b, 0, 0)),
        ),
        out_shape=jax.ShapeDtypeStruct((plan.batches, rows, width), jnp.bfloat16),
        compiler_params=pltpu.CompilerParams(vmem_limit_bytes=VMEM_LIMIT),
        cost_estimate=cost(3.0),
        name="assemble",
    )(info, own, other, near, far)


def after(value, *others):
    return lax.optimization_barrier((value, *others))[0]


def ring_shards(plan, grad_out, saved_input, lengths, kernel, gain, bias, proj_weight):
    f, xh, gh = plan.frames, plan.xhalo, plan.ghalo
    index = lax.axis_index("shard")
    group = lax.axis_index("groups")
    core, chip = index % CORES, index // CORES
    place = plan.position_of(chip)
    forward, backward = plan.ring()
    offset = chip * plan.chip_frames
    scale = lax.rsqrt(jnp.sum(lengths).astype(jnp.float32))
    pairs = plan.pairs
    far = jnp.asarray([d for pair in pairs for d in pair], jnp.int32)
    owned = CORES * plan.chip_at((place + far + plan.chips) % plan.chips) + core
    info = jnp.concatenate([jnp.stack([core, offset, group]), lengths, owned]).astype(jnp.int32)
    gain2, bias2 = gain.reshape(1, -1), bias.reshape(1, -1)
    taps = jnp.pad(kernel, ((0, plan.tap_rows - plan.taps), (0, 0)))
    consts = [jnp.asarray(c) for c in transforms(plan)]

    x_near, x_far, g_edge = edge_call(plan, saved_input, grad_out)
    xa = lax.ppermute(x_near, "shard", plan.edges())
    xb = lax.ppermute(x_far, "shard", plan.edges_like())
    xp = lax.ppermute(saved_input, "shard", plan.partners())
    x = assemble_call(
        plan, info, saved_input, xp, xa, xb, plan.window_rows(plan.conv_windows), True
    )
    g_edge = after(g_edge, xa, xb)
    ga = lax.ppermute(g_edge, "shard", plan.edges())
    gb = lax.ppermute(g_edge, "shard", plan.edges_like())
    mgp = lax.ppermute(grad_out, "shard", plan.partners())
    mg = assemble_call(plan, info, grad_out, mgp, ga, gb, plan.ext, False)

    def added(product, received):
        return product + received.astype(jnp.float32)

    halved = plan.weight_parts == 2
    piece = LANES // 2
    convs, products, sends = [], [], []
    around = {}
    going = [proj_weight, proj_weight]
    order = info
    send_f = send_b = recv_f = recv_b = None
    for step in range(plan.rounds):
        last = step == plan.rounds - 1
        if step == plan.rounds - 1 and sends:
            order = after(order, sends[0])
        conv, product_f, product_b = conv_call(
            plan, step, order, x, mg, taps, gain2, bias2, consts,
            jnp.bfloat16 if step == 0 else jnp.float32,
        )
        convs.append(conv)
        products.append((product_f, product_b))
        if step == 0:
            send_f, send_b = product_f, product_b
        elif step == 1 or plan.rounds == 2:
            pass
        order = after(info, product_f)
        if step == 0:
            recv_f = lax.ppermute(send_f, "shard", forward)
            recv_b = lax.ppermute(send_b, "shard", backward)
        if step == plan.rounds - 2:
            sends.append(None)
            send_f = added(products[1][0], recv_f).astype(jnp.bfloat16)
            send_b = added(products[1][1], recv_b)
            if plan.rounds > 2:
                send_b = send_b.astype(jnp.bfloat16)
            sends[0] = send_f
        if step == 1 and halved:
            going = [lax.dynamic_slice_in_dim(w, group * piece, piece, 0) for w in going]
        before = x if step == 0 else products[step - 1 if step < plan.rounds - 1 else step][0]
        going = list(lax.optimization_barrier((*going, before))[:2])
        going[0] = lax.ppermute(going[0], "shard", forward)
        around[-step - 1] = going[0]
        if not last:
            going[1] = lax.ppermute(going[1], "shard", backward)
            around[step + 1] = going[1]
    around[plan.rounds] = around.pop(-plan.rounds)

    arrays = [proj_weight]
    source = {0: [(0, None, 0, LANES)]}

    def keep(array):
        arrays.append(array)
        return len(arrays) - 1

    swap = [
        (g * plan.count + s, (1 - g) * plan.count + s) for g in range(2) for s in range(plan.count)
    ]
    batches = [[1, -1]] + [[h, -h] for h in range(2, plan.rounds - 1)]
    batches.append([plan.rounds - 1, 1 - plan.rounds, plan.rounds])
    for n, distances in enumerate(batches):
        if n == 0 or not halved:
            for d in distances:
                source[d] = [(keep(around[d]), None, 0, LANES)]
            continue
        swapped = keep(
            lax.ppermute(
                jnp.concatenate([around[d] for d in distances], 0), ("groups", "shard"), swap
            )
        )
        for i, d in enumerate(distances):
            source[d] = [(keep(around[d]), 0, 0, piece), (swapped, 1, i * piece, piece)]

    calls = [(3, 2), (1, 0)] if plan.rounds == 4 else [(s,) for s in reversed(range(plan.rounds))]
    pieces, stats = [], []
    for n, steps in enumerate(calls):
        order = after(info, products[-1][0], sends[-1])
        sources = [
            [
                (array, part, block, begin, rows)
                for block, d in enumerate(pairs[step])
                for array, part, begin, rows in source[d]
            ]
            for step in steps
        ]
        own, send, stat = back_call(
            plan, steps, order, mg, sources, arrays, [convs[step] for step in steps],
            x, taps, gain2, bias2, consts,
        )
        stats.append(stat)
        pieces += [own, lax.ppermute(send, "shard", plan.partners())]
        if len(sends) < plan.rounds - 1:
            recv_f = lax.ppermute(send_f, "shard", forward)
            recv_b = lax.ppermute(send_b, "shard", backward)
            product_f, product_b = products[len(sends) + 1]
            send_f = added(product_f, recv_f).astype(jnp.bfloat16)
            send_b = added(product_b, recv_b)
            if len(sends) < plan.rounds - 2:
                send_b = send_b.astype(jnp.bfloat16)
            sends.append(send_f)
    while len(sends) < plan.rounds - 1:
        recv_f = lax.ppermute(send_f, "shard", forward)
        recv_b = lax.ppermute(send_b, "shard", backward)
        product_f, product_b = products[len(sends) + 1]
        send_f = added(product_f, recv_f).astype(jnp.bfloat16)
        send_b = added(product_b, recv_b)
        if len(sends) < plan.rounds - 2:
            send_b = send_b.astype(jnp.bfloat16)
        sends.append(send_f)
    recv_f = lax.ppermute(send_f, "shard", forward)
    proj_grad = added(send_b, recv_f) * scale
    full = place_call(plan, calls, info, pieces)

    dealt = deal_call(plan, calls, info, stats)
    groups = [[CORES * p + c for p in range(plan.chips)] for c in range(CORES)]
    summed = jnp.sum(
        lax.all_to_all(dealt, "shard", 0, 0, axis_index_groups=groups), axis=0
    ) * scale
    return (
        full, proj_grad, summed[: plan.taps], summed[plan.tap_rows : plan.tap_rows + 2]
    )


def shards(count, group_count, grad_out, saved_input, lengths, kernel, gain, bias, proj_weight):
    batches, frames, model_width = grad_out.shape
    plan = Plan(count, group_count, batches, frames, model_width, kernel.shape[0])
    args = (grad_out, saved_input, lengths, kernel, gain, bias, proj_weight)
    return ring_shards(plan, *args) if plan.usable() else plain_shards(*args)


def solution(mesh):
    placed = (
        P("groups", "shard", None),
        P("groups", "shard", None),
        P("groups"),
        P(),
        P(),
        P(),
        P("shard", None),
    )
    return jax.shard_map(
        functools.partial(shards, mesh.shape["shard"], mesh.shape["groups"]),
        mesh=mesh,
        in_specs=placed,
        out_specs=(
            P("groups", "shard", None),
            P(("groups", "shard"), None),
            P("groups", "shard"),
            P("groups", "shard"),
        ),
        check_vma=False,
    )
```

```python
import functools

import jax
import jax.numpy as jnp
import numpy as np
from jax import lax
from jax.experimental import pallas as pl
from jax.experimental.pallas import tpu as pltpu
from jax.sharding import PartitionSpec as P


LANES = 128
CORES = 2
VMEM_LIMIT = 56 * 1024 * 1024
POINTS = 256


def cost(micros):
    return pl.CostEstimate(flops=0, transcendentals=0, bytes_accessed=int(micros * 3.6e6))


def extended(block, width):
    count = lax.axis_size("shard")
    forward = [(i, i + 1) for i in range(count - 1)]
    backward = [(target, source) for source, target in forward]
    low = lax.ppermute(block[:, block.shape[1] - width :], "shard", forward)
    high = lax.ppermute(block[:, :width], "shard", backward)
    return jnp.concatenate([low, block, high], axis=1)


def frame_mask(lengths, offset, count):
    position = offset + jnp.arange(count, dtype=jnp.int32)
    return (position[None, :] < lengths[:, None])[:, :, None]


def plain_shards(grad_out, saved_input, lengths, kernel, gain, bias, proj_weight):
    batches, frames, model_width = grad_out.shape
    tap_count = kernel.shape[0]
    half_span = (tap_count - 1) // 2
    offset = lax.axis_index("shard") * frames
    norm_scale = lax.rsqrt(jnp.sum(lengths).astype(jnp.float32))
    own_mask = frame_mask(lengths, offset, frames)
    masked_in = jnp.where(own_mask, saved_input, jnp.zeros_like(saved_input))
    masked_grad = jnp.where(own_mask, grad_out, jnp.zeros_like(grad_out))
    in_ext = extended(masked_in, half_span)
    conv = jnp.zeros(grad_out.shape, jnp.float32)
    for tap in range(tap_count):
        conv = conv + kernel[tap] * in_ext[:, tap : tap + frames].astype(jnp.float32)
    pre_act = gain * conv + bias
    gate_sig = jax.nn.sigmoid(pre_act)
    activated = (pre_act * gate_sig).astype(jnp.bfloat16)
    rows = masked_grad.reshape(batches * frames, model_width)
    weight = lax.all_gather(proj_weight, "shard", axis=0, tiled=True)
    act_grad = lax.dot_general(
        rows, weight, (((1,), (1,)), ((), ())), preferred_element_type=jnp.float32
    ).reshape(batches, frames, model_width)
    pre_grad = act_grad * gate_sig * (1.0 + pre_act * (1.0 - gate_sig))
    conv_grad = (pre_grad * gain).astype(jnp.bfloat16)
    grad_ext = extended(conv_grad, half_span)
    back_sum = jnp.zeros(grad_out.shape, jnp.float32)
    grad_float = conv_grad.astype(jnp.float32)
    tap_rows = []
    for tap in range(tap_count):
        begin = 2 * half_span - tap
        back_sum = back_sum + kernel[tap] * grad_ext[:, begin : begin + frames].astype(jnp.float32)
        tap_rows.append(
            jnp.sum(in_ext[:, tap : tap + frames].astype(jnp.float32) * grad_float, axis=(0, 1))
        )
    input_grad = jnp.where(own_mask, back_sum, 0.0).astype(jnp.bfloat16)
    tap_rows.append(jnp.sum(pre_grad * conv, axis=(0, 1)))
    tap_rows.append(jnp.sum(pre_grad, axis=(0, 1)))
    stats = jnp.stack(tap_rows, 0) * norm_scale
    summed = lax.psum_scatter(stats, "shard", scatter_dimension=1, tiled=True)
    product = lax.dot_general(
        activated.reshape(batches * frames, model_width),
        rows,
        (((0,), (0,)), ((), ())),
        preferred_element_type=jnp.float32,
    )
    proj_grad = lax.psum_scatter(product * norm_scale, "shard", scatter_dimension=0, tiled=True)
    return (input_grad, proj_grad, summed[:tap_count], summed[tap_count:])


class Plan:
    def __init__(self, count, groups, batches, frames, model_width, tap_count):
        self.count = count
        self.chips = count // CORES
        self.rounds = self.chips // 2
        self.batches = batches
        self.frames = frames
        self.chip_frames = CORES * frames
        self.width = model_width
        self.block = model_width // count
        self.taps = tap_count
        self.half = (tap_count - 1) // 2
        self.ghalo = -(-self.half // 16) * 16
        self.xhalo = 2 * self.ghalo
        self.ext = self.chip_frames + 2 * self.ghalo
        self.xext = self.chip_frames + 2 * self.xhalo
        self.tap_rows = -(-tap_count // 16) * 16
        self.stat_rows = self.tap_rows + 8
        self.weight_parts = 2 if groups == 2 else 1
        self.pairs = [(h, 1 - h) for h in range(self.rounds, 0, -1)]
        self.conv_windows = windows(self.ext, self.xhalo - self.ghalo - self.half + tap_count)
        self.back_windows = windows(self.chip_frames, self.ghalo + self.half + 1)

    def window_rows(self, found):
        return found[0] * (found[1] - 1) + POINTS

    def block_slot(self, step, side):
        return 3 + self.batches + 2 * step + side

    def usable(self):
        return (
            self.count % (2 * CORES) == 0
            and self.block == LANES
            and self.block * self.count == self.width
            and self.frames % 128 == 0
            and self.frames >= self.xhalo
            and self.taps % 2 == 1
            and 4 * self.ghalo <= POINTS // 2
            and self.window_rows(self.conv_windows) >= self.xext
            and self.window_rows(self.back_windows) >= self.ext
            and self.window_rows(self.conv_windows)
            >= self.xhalo + self.window_rows(self.back_windows) - self.back_windows[0]
            and self.chips == 8
            and self.batches == 2
        )

    def chip_at(self, position):
        half = self.chips // 2
        return jnp.where(position < half, 2 * position, 2 * (self.chips - 1 - position) + 1)

    def position_of(self, chip):
        return jnp.where(chip % 2 == 0, chip // 2, self.chips - 1 - chip // 2)

    def ring(self):
        half = self.chips // 2
        order = [2 * i for i in range(half)] + [2 * i + 1 for i in reversed(range(half))]
        forward = []
        for core in range(CORES):
            for i in range(self.chips):
                source, target = order[i], order[(i + 1) % self.chips]
                forward.append((CORES * source + core, CORES * target + core))
        return forward, [(t, s) for s, t in forward]

    def edges(self):
        pairs = []
        for chip in range(self.chips - 1):
            last, first = CORES * chip + 1, CORES * (chip + 1)
            pairs += [(last, first), (first, last)]
        return pairs

    def edges_like(self):
        pairs = []
        for chip in range(self.chips - 1):
            pairs.append((CORES * chip + 1, CORES * (chip + 1) + 1))
            pairs.append((CORES * (chip + 1), CORES * chip))
        return pairs

    def partners(self):
        return [(s, s ^ 1) for s in range(self.count)]


def sigmoid(value):
    return 0.5 * jnp.tanh(0.5 * value) + 0.5


def split(value):
    high = value.astype(jnp.bfloat16)
    return high, (value - high.astype(jnp.float32)).astype(jnp.bfloat16)


def split_matrix(matrix):
    high = matrix.astype(jnp.bfloat16)
    return high, (matrix - high.astype(np.float64)).astype(jnp.bfloat16)


def transforms(plan):
    time = np.arange(POINTS)
    theta = np.pi * (2 * np.arange(POINTS // 2) + 1) / POINTS
    angle = theta[:, None] * time[None, :]
    direct = np.concatenate([np.cos(angle), -np.sin(angle)], 0)
    inverse = direct.T * (2.0 / POINTS)

    def spectrum(lags):
        phase = theta[:, None] * lags[None, :]
        matrix = np.concatenate([np.cos(phase), np.sin(phase)], 0)
        return np.pad(matrix, ((0, 0), (0, plan.tap_rows - plan.taps)))

    taps = np.arange(plan.taps)
    back_lags = plan.ghalo + plan.half - taps
    lag_rows = np.pad(inverse[back_lags], ((0, plan.tap_rows - plan.taps), (0, 0)))
    half = lambda m: m.astype(jnp.bfloat16)
    conv_lags = plan.xhalo - plan.ghalo - plan.half + taps
    return (
        half(direct),
        half(inverse),
        np.stack(split_matrix(spectrum(conv_lags))),
        np.stack(split_matrix(spectrum(back_lags))),
        np.stack(split_matrix(lag_rows)),
        half(direct * (time < plan.back_windows[0])),
    )


def taps_spectrum(t_ref, k_ref):
    high, low = split(jnp.concatenate([k_ref[0][...], k_ref[1][...]], axis=1))
    dot = functools.partial(jnp.dot, preferred_element_type=jnp.float32)
    return dot(t_ref[0], high) + dot(t_ref[1], high) + dot(t_ref[0], low)


def to_spectrum(direct_ref, window):
    return jnp.dot(direct_ref[...], window, preferred_element_type=jnp.float32)


def from_spectrum(inverse_ref, rows, parts, slot):
    return jnp.dot(inverse_ref[:rows, :], parts[slot], preferred_element_type=jnp.float32)


def windows(rows_out, reach):
    count = -(-rows_out // ((POINTS - reach) // 16 * 16))
    return -(-rows_out // count // 16) * 16, count


STEP = 16
HALF = POINTS // 2


def spectral_product(spec, taps, parts, slot):
    for row in range(0, HALF, STEP):
        up, down = slice(row, row + STEP), slice(HALF + row, HALF + row + STEP)
        re, im, kr, ks = spec[slot, up, :], spec[slot, down, :], taps[up, :], taps[down, :]
        parts[slot, up, :] = (re * kr - im * ks).astype(jnp.bfloat16)
        parts[slot, down, :] = (re * ks + im * kr).astype(jnp.bfloat16)


def conv_body(plan, info, *refs):
    own_x, other_x, near_x, far_x, k_ref, gain_ref, bias_ref = (
        refs[2 * i : 2 * i + 2] for i in range(7)
    )
    direct, inverse, t_ref, own_g, other_g = refs[14:19]
    conv_ref, x_ref, out_f, out_b, spec, taps, parts, act, acc = refs[19:]
    each, count = plan.conv_windows
    f, xh, gh, cf = plan.frames, plan.xhalo, plan.ghalo, plan.chip_frames
    b = pl.program_id(0)
    core, offset, live = info[0], info[1], info[3 + b]

    @pl.when(b == 0)
    def _():
        taps[...] = taps_spectrum(t_ref, k_ref)

    def put(row, pair):
        for part in range(0, pair[0].shape[1], STEP):
            position = lax.broadcasted_iota(jnp.int32, (STEP, LANES), 0) + (
                offset - xh + row + part
            )
            keep = jnp.where(position < live, 1.0, 0.0).astype(jnp.bfloat16)
            for side in range(2):
                lanes = slice(side * LANES, (side + 1) * LANES)
                x_ref[0, row + part : row + part + STEP, lanes] = (
                    pair[side][0, part : part + STEP, :] * keep
                )

    @pl.when(core == 0)
    def _():
        put(0, near_x)
        put(xh, own_x)
        put(xh + f, other_x)
        put(xh + 2 * f, far_x)

    @pl.when(core != 0)
    def _():
        put(0, far_x)
        put(xh, other_x)
        put(xh + f, own_x)
        put(xh + 2 * f, near_x)

    x_ref[0, plan.xext :, :] = jnp.zeros((x_ref.shape[1] - plan.xext, 2 * LANES), jnp.bfloat16)

    for j in range(count):
        spec[j] = to_spectrum(direct, x_ref[0, j * each : j * each + POINTS, :])
    for j in range(count):
        spectral_product(spec, taps, parts, j)
        rows = min(each, plan.ext - j * each)
        conv_ref[0, j * each : j * each + rows, :] = from_spectrum(inverse, rows, parts, j)

    for i in range(cf // LANES):
        for side in range(2):
            lanes = slice(side * LANES, (side + 1) * LANES)
            begin = gh + i * LANES
            conv = conv_ref[0, begin : begin + LANES, lanes]
            pre = gain_ref[side][...] * conv + bias_ref[side][...]
            position = lax.broadcasted_iota(jnp.int32, (LANES, LANES), 0) + (offset + i * LANES)
            value = jnp.where(position < live, pre * sigmoid(pre), 0.0)
            act[lanes, i * LANES : (i + 1) * LANES] = value.T.astype(jnp.bfloat16)

    own = pl.multiple_of(core * f, f)
    other = pl.multiple_of((1 - core) * f, f)

    def product(columns):
        dot = functools.partial(jnp.dot, preferred_element_type=jnp.float32)
        return dot(act[:, pl.ds(own, f)], own_g[0, :, columns]) + dot(
            act[:, pl.ds(other, f)], other_g[0, :, columns]
        )

    tiles = [slice(c, c + 2 * LANES) for c in range(0, plan.width, 2 * LANES)]

    @pl.when(b == 0)
    def _():
        for columns in tiles:
            acc[:, columns] = product(columns)

    @pl.when(b != 0)
    def _():
        for columns in tiles:
            total = acc[:, columns] + product(columns)
            if plan.batches > 2:
                acc[:, columns] = total
            out_f[:, columns] = total[:LANES].astype(out_f.dtype)
            out_b[:, columns] = total[LANES:].astype(out_b.dtype)


def pair_specs(plan, step, shape, index):
    return [
        pl.BlockSpec(
            shape, lambda b, info, at=plan.block_slot(step, side): index(b, info[at])
        )
        for side in range(2)
    ]


def whole(array):
    return pl.BlockSpec(
        array.shape, lambda *_: (0,) * array.ndim, pipeline_mode=pl.Buffered(1)
    )


def conv_call(plan, step, info, x, xp, xa, xb, g, gp, kernel, gain, bias, consts, kind):
    bt = plan.batches
    flat = lambda b, block: (0, block)
    fixed = lambda b, info: (0, 0)
    direct, inverse, t_conv = consts[:3]
    wide = 2 * LANES
    slots = plan.conv_windows[1]
    specs = functools.partial(pair_specs, plan, step)
    frames, halo = (1, plan.frames, LANES), (1, plan.xhalo, LANES)
    by_batch = lambda b, block: (b, 0, block)
    by_chip = lambda b, block: (b, 0, block // CORES)
    x_rows = plan.window_rows(plan.conv_windows)
    return pl.pallas_call(
        functools.partial(conv_body, plan),
        grid_spec=pltpu.PrefetchScalarGridSpec(
            num_scalar_prefetch=1,
            grid=(bt,),
            in_specs=specs(frames, by_batch)
            + specs(frames, by_batch)
            + specs(halo, by_chip)
            + specs(halo, by_chip)
            + specs((plan.tap_rows, LANES), flat)
            + specs((1, LANES), flat)
            + specs((1, LANES), flat)
            + [whole(direct), whole(inverse), whole(t_conv)]
            + [pl.BlockSpec((1, plan.frames, plan.width), lambda b, info: (b, 0, 0))] * 2,
            out_specs=[
                pl.BlockSpec((1, plan.ext, wide), lambda b, info: (b, 0, 0)),
                pl.BlockSpec((1, x_rows, wide), lambda b, info: (b, 0, 0)),
                pl.BlockSpec((LANES, plan.width), fixed),
                pl.BlockSpec((LANES, plan.width), fixed),
            ],
            scratch_shapes=[
                pltpu.VMEM((slots, POINTS, wide), jnp.float32),
                pltpu.VMEM((POINTS, wide), jnp.float32),
                pltpu.VMEM((slots, POINTS, wide), jnp.bfloat16),
                pltpu.VMEM((wide, plan.chip_frames), jnp.bfloat16),
                pltpu.VMEM((wide, plan.width), jnp.float32),
            ],
        ),
        out_shape=[
            jax.ShapeDtypeStruct((bt, plan.ext, wide), jnp.float32),
            jax.ShapeDtypeStruct((bt, x_rows, wide), jnp.bfloat16),
            jax.ShapeDtypeStruct((LANES, plan.width), kind),
            jax.ShapeDtypeStruct((LANES, plan.width), kind),
        ],
        compiler_params=pltpu.CompilerParams(vmem_limit_bytes=VMEM_LIMIT),
        cost_estimate=cost(6.0),
        name="conv",
    )(info, x, x, xp, xp, xa, xa, xb, xb, kernel, kernel, gain, gain, bias, bias,
      direct, inverse, t_conv, g, gp)


def back_body(plan, steps, sources, info, *refs):
    pairs = len(steps)
    mg_ref = refs[0]
    k_refs, gain_refs, bias_refs = (
        refs[1 + 2 * pairs * i : 1 + 2 * pairs * (i + 1)] for i in range(3)
    )
    refs = refs[1 + 6 * pairs :]
    conv_refs, x_refs, w_refs = refs[:pairs], refs[pairs : 2 * pairs], refs[2 * pairs : -25]
    direct, segment, inverse, t_ref, lag_ref = refs[-25:-20]
    (own_ref, send_ref, stat_ref, weight, conv_buf, x_buf, ag, gs, tail, spec, xspec, taps,
     cross, parts, os, sums, flat, w_sem, c_sem, x_sem) = refs[-20:]
    core, offset, side_y = info[0], info[1], info[2]
    f, xh, gh, cf, ext = plan.frames, plan.xhalo, plan.ghalo, plan.chip_frames, plan.ext
    each, count = plan.back_windows
    turn, b = pl.program_id(0), pl.program_id(1)
    live = info[3 + b]

    def weight_copies(pair):
        made = []
        for n, (array, part, target, begin, rows) in enumerate(sources[pair]):
            first, into = begin, target * LANES
            if part is not None:
                into = pl.multiple_of(target * LANES + (side_y + part) % 2 * rows, rows)
            made.append(
                pltpu.make_async_copy(
                    w_refs[array].at[pl.ds(first, rows), :],
                    weight.at[pair, pl.ds(into, rows), :],
                    w_sem.at[pair, n],
                )
            )
        return made

    def conv_copies(pair):
        return [
            pltpu.make_async_copy(conv_refs[pair].at[i], conv_buf.at[pair, i], c_sem.at[pair, i])
            for i in range(plan.batches)
        ] + [
            pltpu.make_async_copy(x_refs[pair].at[i], x_buf.at[pair, i], x_sem.at[pair, i])
            for i in range(plan.batches)
        ]

    @pl.when((turn == 0) & (b == 0))
    def _():
        for pair in range(pairs):
            for copy in weight_copies(pair) + conv_copies(pair):
                copy.start()
        gs[ext:, :] = jnp.zeros((gs.shape[0] - ext, 2 * LANES), jnp.bfloat16)
        tail[...] = jnp.zeros_like(tail)

    for pair in range(pairs):

        @pl.when((turn == pair) & (b == 0))
        def _():
            taps[...] = taps_spectrum(t_ref, k_refs[2 * pair : 2 * pair + 2])
            for row, pick in ((0, gain_refs), (8, bias_refs)):
                for side in range(2):
                    lanes = slice(side * LANES, (side + 1) * LANES)
                    flat[row : row + 8, lanes] = jnp.broadcast_to(
                        pick[2 * pair + side][...], (8, LANES)
                    )
            cross[...] = jnp.zeros_like(cross)
            sums[...] = jnp.zeros_like(sums)
            for copy in weight_copies(pair) + conv_copies(pair):
                copy.wait()

    last_rows = cf - (count - 1) * each
    for j in range(count):
        begin = xh + j * each
        if j < count - 1:
            window = x_buf[turn, b, begin : begin + POINTS, :]
        else:
            tail[:last_rows, :] = x_buf[turn, b, begin : begin + last_rows, :]
            window = tail[...]
        xspec[j] = to_spectrum(segment, window)

    ag[...] = lax.dot_general(
        mg_ref[0], weight[turn], (((1,), (1,)), ((), ())), preferred_element_type=jnp.float32
    )
    gain, bias = flat[:1, :], flat[8:9, :]

    gain_sum = jnp.zeros((8, 2 * LANES), jnp.float32)
    bias_sum = jnp.zeros((8, 2 * LANES), jnp.float32)
    for row in range(0, ext, STEP):
        conv = conv_buf[turn, b, row : row + STEP, :]
        pre = gain * conv + bias
        sig = sigmoid(pre)
        value = ag[row : row + STEP, :] * sig * (1.0 + pre * (1.0 - sig))
        gs[row : row + STEP, :] = (value * gain).astype(jnp.bfloat16)
        if gh <= row < gh + cf:
            fold = lambda v: jnp.sum(v.reshape(STEP // 8, 8, 2 * LANES), axis=0)
            gain_sum = gain_sum + fold(value * conv)
            bias_sum = bias_sum + fold(value)
    sums[0] += gain_sum
    sums[1] += bias_sum

    for j in range(count):
        spec[j] = to_spectrum(direct, gs[j * each : j * each + POINTS, :])
    for j in range(count):
        spectral_product(spec, taps, parts, j)
        rows = min(each, cf - j * each)
        value = from_spectrum(inverse, rows, parts, j)
        position = offset + j * each + lax.broadcasted_iota(jnp.int32, value.shape, 0)
        os[j * each : j * each + rows, :] = jnp.where(position < live, value, 0.0).astype(
            jnp.bfloat16
        )
    for row in range(0, HALF, STEP):
        up, down = slice(row, row + STEP), slice(HALF + row, HALF + row + STEP)
        total_r, total_i = cross[up, :], cross[down, :]
        for j in range(count):
            re, im, xr, xi = spec[j, up, :], spec[j, down, :], xspec[j, up, :], xspec[j, down, :]
            total_r = total_r + re * xr + im * xi
            total_i = total_i + im * xr - re * xi
        cross[up, :] = total_r
        cross[down, :] = total_i

    @pl.when(core == 0)
    def _():
        own_ref[0, 0] = os[:f]
        send_ref[0, 0] = os[f:]

    @pl.when(core != 0)
    def _():
        own_ref[0, 0] = os[f:]
        send_ref[0, 0] = os[:f]

    @pl.when(b == plan.batches - 1)
    def _():
        high, low = split(cross[...])
        dot = functools.partial(jnp.dot, preferred_element_type=jnp.float32)
        stat_ref[0, : plan.tap_rows] = (
            dot(lag_ref[0], high) + dot(lag_ref[1], high) + dot(lag_ref[0], low)
        )
        total = [jnp.sum(sums[i], axis=0, keepdims=True) for i in range(2)]
        pad = jnp.zeros((plan.stat_rows - plan.tap_rows - 2, 2 * LANES), jnp.float32)
        stat_ref[0, plan.tap_rows :] = jnp.concatenate(total + [pad], axis=0)


def back_call(plan, steps, info, mg, sources, arrays, convs, xs, kernel, gain, bias, consts):
    bt, pairs = plan.batches, len(steps)
    direct, inverse, _, t_back, lags, segment = consts
    wide = 2 * LANES
    slots = plan.back_windows[1]
    any_space = pl.BlockSpec(memory_space=pl.ANY)

    def by_block(shape):
        return [
            pl.BlockSpec(
                shape, lambda p, b, info, at=plan.block_slot(step, side): (0, info[at]),
                pipeline_mode=pl.Buffered(1),
            )
            for step in steps for side in range(2)
        ]

    each = lambda *tail: pl.BlockSpec((1, 1) + tail, lambda p, b, info: (p, b, 0, 0))
    most = max(len(source) for source in sources)
    return pl.pallas_call(
        functools.partial(back_body, plan, steps, sources),
        grid_spec=pltpu.PrefetchScalarGridSpec(
            num_scalar_prefetch=1,
            grid=(pairs, bt),
            in_specs=[
                pl.BlockSpec((1, plan.ext, plan.width), lambda p, b, info: (b, 0, 0)),
            ]
            + by_block((plan.tap_rows, LANES))
            + by_block((1, LANES))
            + by_block((1, LANES))
            + [any_space] * (2 * pairs + len(arrays))
            + [whole(c) for c in (direct, segment, inverse, t_back, lags)],
            out_specs=[
                each(plan.frames, wide),
                each(plan.frames, wide),
                pl.BlockSpec((1, plan.stat_rows, wide), lambda p, b, info: (p, 0, 0)),
            ],
            scratch_shapes=[
                pltpu.VMEM((pairs, wide, plan.width), jnp.bfloat16),
                pltpu.VMEM((pairs, bt, plan.ext, wide), jnp.float32),
                pltpu.VMEM((pairs, bt, xs[0].shape[1], wide), jnp.bfloat16),
                pltpu.VMEM((plan.ext, wide), jnp.float32),
                pltpu.VMEM((plan.window_rows(plan.back_windows), wide), jnp.bfloat16),
                pltpu.VMEM((POINTS, wide), jnp.bfloat16),
                pltpu.VMEM((slots, POINTS, wide), jnp.float32),
                pltpu.VMEM((slots, POINTS, wide), jnp.float32),
                pltpu.VMEM((POINTS, wide), jnp.float32),
                pltpu.VMEM((POINTS, wide), jnp.float32),
                pltpu.VMEM((slots, POINTS, wide), jnp.bfloat16),
                pltpu.VMEM((plan.chip_frames, wide), jnp.bfloat16),
                pltpu.VMEM((2, 8, wide), jnp.float32),
                pltpu.VMEM((16, wide), jnp.float32),
                pltpu.SemaphoreType.DMA((pairs, most)),
                pltpu.SemaphoreType.DMA((pairs, bt)),
                pltpu.SemaphoreType.DMA((pairs, bt)),
            ],
        ),
        out_shape=[
            jax.ShapeDtypeStruct((pairs, bt, plan.frames, wide), jnp.bfloat16),
            jax.ShapeDtypeStruct((pairs, bt, plan.frames, wide), jnp.bfloat16),
            jax.ShapeDtypeStruct((pairs, plan.stat_rows, wide), jnp.float32),
        ],
        compiler_params=pltpu.CompilerParams(vmem_limit_bytes=VMEM_LIMIT),
        cost_estimate=cost(6.0 * pairs),
        name="back",
    )(info, mg, *[kernel] * 2 * pairs, *[gain] * 2 * pairs, *[bias] * 2 * pairs,
      *convs, *xs, *arrays, direct, segment, inverse, t_back, lags)


def place_body(plan, calls, info, *refs):
    out_ref = refs[-1]
    for i, ref in enumerate(refs[:-1]):
        for turn, step in enumerate(calls[i // 2]):
            for side in range(2):
                block = info[plan.block_slot(step, side)]
                if i % 2:
                    block = block + 1 - 2 * info[0]
                column = pl.multiple_of(block * LANES, LANES)
                lanes = slice(side * LANES, (side + 1) * LANES)
                out_ref[:, :, pl.ds(column, LANES)] = ref[turn, :, :, lanes]


def place_call(plan, calls, info, arrays):
    shape = (plan.batches, plan.frames, plan.width)
    return pl.pallas_call(
        functools.partial(place_body, plan, calls),
        grid_spec=pltpu.PrefetchScalarGridSpec(
            num_scalar_prefetch=1,
            grid=(1,),
            in_specs=[whole(array) for array in arrays],
            out_specs=pl.BlockSpec(shape, lambda g, info: (0, 0, 0)),
        ),
        out_shape=jax.ShapeDtypeStruct(shape, jnp.bfloat16),
        compiler_params=pltpu.CompilerParams(vmem_limit_bytes=VMEM_LIMIT),
        cost_estimate=cost(3.0),
        name="place",
    )(info, *arrays)


def deal_body(plan, calls, info, *refs):
    out_ref = refs[-1]
    for steps, ref in zip(calls, refs[:-1]):
        for turn, step in enumerate(steps):
            for side in range(2):
                chip = info[plan.block_slot(step, side)] // CORES
                out_ref[chip] = ref[turn, :, side * LANES : (side + 1) * LANES]


def deal_call(plan, calls, info, arrays):
    shape = (plan.chips, plan.stat_rows, LANES)
    return pl.pallas_call(
        functools.partial(deal_body, plan, calls),
        grid_spec=pltpu.PrefetchScalarGridSpec(
            num_scalar_prefetch=1,
            grid=(1,),
            in_specs=[whole(array) for array in arrays],
            out_specs=pl.BlockSpec(shape, lambda g, info: (0, 0, 0)),
        ),
        out_shape=jax.ShapeDtypeStruct(shape, jnp.float32),
        cost_estimate=cost(1.0),
        name="deal",
    )(info, *arrays)


def edge_body(plan, x_first, x_last, g_first, g_last, near_ref, far_ref, g_ref):
    core = lax.axis_index("shard") % CORES

    def take(owner, x_ref, grad_ref):
        for i in range(plan.chips):
            for out, parity in ((near_ref, 1 - owner), (far_ref, owner)):
                column = (CORES * i + parity) * LANES
                out[:, :, i * LANES : (i + 1) * LANES] = x_ref[:, :, column : column + LANES]
        g_ref[...] = grad_ref[...]

    pl.when(core == 0)(lambda: take(0, x_first, g_first))
    pl.when(core != 0)(lambda: take(1, x_last, g_last))


def edge_call(plan, x, g):
    def spec(rows, first):
        shape = (plan.batches, rows, plan.width)
        block = 0 if first else plan.frames // rows - 1
        return pl.BlockSpec(shape, lambda i: (0, block, 0))

    xh, gh = plan.xhalo, plan.ghalo
    half = (plan.batches, xh, plan.width // CORES)
    shapes = [half, half, (plan.batches, gh, plan.width)]
    return pl.pallas_call(
        functools.partial(edge_body, plan),
        grid=(1,),
        in_specs=[spec(xh, True), spec(xh, False), spec(gh, True), spec(gh, False)],
        out_specs=[pl.BlockSpec(shape, lambda i: (0, 0, 0)) for shape in shapes],
        out_shape=[jax.ShapeDtypeStruct(shape, jnp.bfloat16) for shape in shapes],
        cost_estimate=cost(1.0),
        name="edge",
    )(x, x, g, g)


def assemble_body(plan, halo, info, own_ref, other_ref, near_ref, far_ref, out_ref):
    core, offset, live = info[0], info[1], info[3 + pl.program_id(0)]
    f = plan.frames

    def put(row, ref):
        for part in range(0, ref.shape[1], STEP):
            position = lax.broadcasted_iota(jnp.int32, (STEP, LANES), 0) + (
                offset - halo + row + part
            )
            keep = jnp.where(position < live, 1.0, 0.0).astype(jnp.bfloat16)
            for i in range(plan.count):
                lanes = slice(i * LANES, (i + 1) * LANES)
                out_ref[0, row + part : row + part + STEP, lanes] = (
                    ref[0, part : part + STEP, lanes] * keep
                )

    @pl.when(core == 0)
    def _():
        put(0, near_ref)
        put(halo, own_ref)
        put(halo + f, other_ref)
        put(halo + 2 * f, far_ref)

    @pl.when(core != 0)
    def _():
        put(0, far_ref)
        put(halo, other_ref)
        put(halo + f, own_ref)
        put(halo + 2 * f, near_ref)


def assemble_call(plan, info, own, other, near, far):
    halo = near.shape[1]
    spec = lambda n: pl.BlockSpec((1, n, plan.width), lambda b, info: (b, 0, 0))
    return pl.pallas_call(
        functools.partial(assemble_body, plan, halo),
        grid_spec=pltpu.PrefetchScalarGridSpec(
            num_scalar_prefetch=1,
            grid=(plan.batches,),
            in_specs=[spec(plan.frames), spec(plan.frames), spec(halo), spec(halo)],
            out_specs=spec(plan.ext),
        ),
        out_shape=jax.ShapeDtypeStruct((plan.batches, plan.ext, plan.width), jnp.bfloat16),
        compiler_params=pltpu.CompilerParams(vmem_limit_bytes=VMEM_LIMIT),
        cost_estimate=cost(5.0),
        name="assemble",
    )(info, own, other, near, far)


def after(value, *others):
    return lax.optimization_barrier((value, *others))[0]


def ring_shards(plan, grad_out, saved_input, lengths, kernel, gain, bias, proj_weight):
    index = lax.axis_index("shard")
    group = lax.axis_index("groups")
    core, chip = index % CORES, index // CORES
    place = plan.position_of(chip)
    forward, backward = plan.ring()
    offset = chip * plan.chip_frames
    scale = lax.rsqrt(jnp.sum(lengths).astype(jnp.float32))
    pairs = plan.pairs
    far = jnp.asarray([d for pair in pairs for d in pair], jnp.int32)
    owned = CORES * plan.chip_at((place + far + plan.chips) % plan.chips) + core
    info = jnp.concatenate([jnp.stack([core, offset, group]), lengths, owned]).astype(jnp.int32)
    gain2, bias2 = gain.reshape(1, -1), bias.reshape(1, -1)
    taps = jnp.pad(kernel, ((0, plan.tap_rows - plan.taps), (0, 0)))
    consts = [jnp.asarray(c) for c in transforms(plan)]

    x_near, x_far, g_edge = edge_call(plan, saved_input, grad_out)
    xa = lax.ppermute(x_near, "shard", plan.edges())
    xb = lax.ppermute(x_far, "shard", plan.edges_like())
    xp = lax.ppermute(saved_input, "shard", plan.partners())
    mgp = lax.ppermute(grad_out, "shard", plan.partners())

    halved = plan.weight_parts == 2
    piece = LANES // 2
    around = {}
    going = [after(proj_weight, xa, xb)] * 2

    def weight_round(step):
        going[0] = lax.ppermute(going[0], "shard", forward)
        around[-step] = going[0]
        if step < plan.rounds:
            going[1] = lax.ppermute(going[1], "shard", backward)
            around[step] = going[1]
        else:
            around[step] = around.pop(-step)

    convs, xs, products = [], [], []

    def conv_step(step, order):
        conv, x, *product = conv_call(
            plan, step, order, saved_input, xp, xa, xb, grad_out,
            mgp, taps, gain2, bias2, consts, jnp.bfloat16 if step == 0 else jnp.float32,
        )
        convs.append(conv)
        xs.append(x)
        products.append(product)

    def sum_round(step, send, *behind):
        received = (
            lax.ppermute(send[0], "shard", forward), lax.ppermute(send[1], "shard", backward)
        )
        kinds = (jnp.bfloat16, jnp.bfloat16 if step < plan.rounds - 1 else jnp.float32)
        own = lax.optimization_barrier((*products[step], *received, *behind))[:2]
        return [
            (product + value.astype(jnp.float32)).astype(kind)
            for product, value, kind in zip(own, received, kinds)
        ]

    weight_round(1)
    conv_step(0, info)
    g_edge = after(g_edge, products[0][0])
    ga = lax.ppermute(g_edge, "shard", plan.edges())
    gb = lax.ppermute(g_edge, "shard", plan.edges_like())
    conv_step(1, after(info, products[0][0]))
    going = list(lax.optimization_barrier((*going, products[1][0]))[:2])
    if halved:
        going = [lax.dynamic_slice_in_dim(w, group * piece, piece, 0) for w in going]
    weight_round(2)
    mg = assemble_call(plan, after(info, products[1][0]), grad_out, mgp, ga, gb)
    send = sum_round(1, products[0], mg)
    going = list(lax.optimization_barrier((*going, mg))[:2])
    weight_round(3)
    conv_step(2, after(info, products[1][0], *send, mg))
    going = list(lax.optimization_barrier((*going, products[2][0]))[:2])
    weight_round(4)
    conv_step(3, after(info, products[2][0]))
    send = sum_round(2, send, products[3][0])

    arrays = [proj_weight]
    source = {0: [(0, None, 0, LANES)]}

    def keep(array):
        arrays.append(array)
        return len(arrays) - 1

    swap = [
        (g * plan.count + s, (1 - g) * plan.count + s) for g in range(2) for s in range(plan.count)
    ]
    for n, distances in enumerate([[1, -1], [2, -2], [3, -3, 4]]):
        if n == 0 or not halved:
            for d in distances:
                source[d] = [(keep(around[d]), None, 0, LANES)]
            continue
        swapped = keep(
            lax.ppermute(
                jnp.concatenate([around[d] for d in distances], 0),
                ("groups", "shard"), swap,
            )
        )
        for i, d in enumerate(distances):
            source[d] = [(keep(around[d]), 0, 0, piece), (swapped, 1, i * piece, piece)]

    calls = [(3, 2), (1, 0)]
    pieces, stats = [], []
    for steps in calls:
        if steps == calls[-1]:
            send = sum_round(3, send, pieces[0])
        order = after(info, products[-1][0], *send)
        used = sorted({a[0] for step in steps for d in pairs[step] for a in source[d]})
        sources = [
            [
                (used.index(array), part, block, begin, rows)
                for block, d in enumerate(pairs[step])
                for array, part, begin, rows in source[d]
            ]
            for step in steps
        ]
        own, given, stat = back_call(
            plan, steps, order, mg, sources, [arrays[i] for i in used],
            [convs[step] for step in steps], [xs[step] for step in steps],
            taps, gain2, bias2, consts,
        )
        stats.append(stat)
        pieces += [own, lax.ppermute(given, "shard", plan.partners())]
    recv_f = after(lax.ppermute(send[0], "shard", forward), stats[-1])
    proj_grad = (send[1] + recv_f.astype(jnp.float32)) * scale
    full = place_call(plan, calls, info, pieces)

    dealt = deal_call(plan, calls, info, stats)
    groups = [[CORES * p + c for p in range(plan.chips)] for c in range(CORES)]
    summed = jnp.sum(
        lax.all_to_all(dealt, "shard", 0, 0, axis_index_groups=groups), axis=0
    ) * scale
    return (
        full, proj_grad, summed[: plan.taps], summed[plan.tap_rows : plan.tap_rows + 2]
    )


def shards(count, group_count, grad_out, saved_input, lengths, kernel, gain, bias, proj_weight):
    batches, frames, model_width = grad_out.shape
    plan = Plan(count, group_count, batches, frames, model_width, kernel.shape[0])
    args = (grad_out, saved_input, lengths, kernel, gain, bias, proj_weight)
    return ring_shards(plan, *args) if plan.usable() else plain_shards(*args)


def solution(mesh):
    placed = (
        P("groups", "shard", None),
        P("groups", "shard", None),
        P("groups"),
        P(),
        P(),
        P(),
        P("shard", None),
    )

    def body(*args):
        return shards(mesh.shape["shard"], mesh.shape["groups"], *args)

    return jax.shard_map(
        body,
        mesh=mesh,
        in_specs=placed,
        out_specs=(
            P("groups", "shard", None),
            P(("groups", "shard"), None),
            P("groups", "shard"),
            P("groups", "shard"),
        ),
        check_vma=False,
    )
```

```python
import functools

import jax
import jax.numpy as jnp
import numpy as np
from jax import lax
from jax.experimental import pallas as pl
from jax.experimental.pallas import tpu as pltpu
from jax.sharding import PartitionSpec as P


LANES = 128
CORES = 2
VMEM_LIMIT = 56 * 1024 * 1024
POINTS = 256


def cost(micros):
    return pl.CostEstimate(flops=0, transcendentals=0, bytes_accessed=int(micros * 3.6e6))


def extended(block, width):
    count = lax.axis_size("shard")
    forward = [(i, i + 1) for i in range(count - 1)]
    backward = [(target, source) for source, target in forward]
    low = lax.ppermute(block[:, block.shape[1] - width :], "shard", forward)
    high = lax.ppermute(block[:, :width], "shard", backward)
    return jnp.concatenate([low, block, high], axis=1)


def frame_mask(lengths, offset, count):
    position = offset + jnp.arange(count, dtype=jnp.int32)
    return (position[None, :] < lengths[:, None])[:, :, None]


def plain_shards(grad_out, saved_input, lengths, kernel, gain, bias, proj_weight):
    batches, frames, model_width = grad_out.shape
    tap_count = kernel.shape[0]
    half_span = (tap_count - 1) // 2
    offset = lax.axis_index("shard") * frames
    norm_scale = lax.rsqrt(jnp.sum(lengths).astype(jnp.float32))
    own_mask = frame_mask(lengths, offset, frames)
    masked_in = jnp.where(own_mask, saved_input, jnp.zeros_like(saved_input))
    masked_grad = jnp.where(own_mask, grad_out, jnp.zeros_like(grad_out))
    in_ext = extended(masked_in, half_span)
    conv = jnp.zeros(grad_out.shape, jnp.float32)
    for tap in range(tap_count):
        conv = conv + kernel[tap] * in_ext[:, tap : tap + frames].astype(jnp.float32)
    pre_act = gain * conv + bias
    gate_sig = jax.nn.sigmoid(pre_act)
    activated = (pre_act * gate_sig).astype(jnp.bfloat16)
    rows = masked_grad.reshape(batches * frames, model_width)
    weight = lax.all_gather(proj_weight, "shard", axis=0, tiled=True)
    act_grad = lax.dot_general(
        rows, weight, (((1,), (1,)), ((), ())), preferred_element_type=jnp.float32
    ).reshape(batches, frames, model_width)
    pre_grad = act_grad * gate_sig * (1.0 + pre_act * (1.0 - gate_sig))
    conv_grad = (pre_grad * gain).astype(jnp.bfloat16)
    grad_ext = extended(conv_grad, half_span)
    back_sum = jnp.zeros(grad_out.shape, jnp.float32)
    grad_float = conv_grad.astype(jnp.float32)
    tap_rows = []
    for tap in range(tap_count):
        begin = 2 * half_span - tap
        back_sum = back_sum + kernel[tap] * grad_ext[:, begin : begin + frames].astype(jnp.float32)
        tap_rows.append(
            jnp.sum(in_ext[:, tap : tap + frames].astype(jnp.float32) * grad_float, axis=(0, 1))
        )
    input_grad = jnp.where(own_mask, back_sum, 0.0).astype(jnp.bfloat16)
    tap_rows.append(jnp.sum(pre_grad * conv, axis=(0, 1)))
    tap_rows.append(jnp.sum(pre_grad, axis=(0, 1)))
    stats = jnp.stack(tap_rows, 0) * norm_scale
    summed = lax.psum_scatter(stats, "shard", scatter_dimension=1, tiled=True)
    product = lax.dot_general(
        activated.reshape(batches * frames, model_width),
        rows,
        (((0,), (0,)), ((), ())),
        preferred_element_type=jnp.float32,
    )
    proj_grad = lax.psum_scatter(product * norm_scale, "shard", scatter_dimension=0, tiled=True)
    return (input_grad, proj_grad, summed[:tap_count], summed[tap_count:])


class Plan:
    def __init__(self, count, groups, batches, frames, model_width, tap_count):
        self.count = count
        self.chips = count // CORES
        self.rounds = self.chips // 2
        self.batches = batches
        self.frames = frames
        self.chip_frames = CORES * frames
        self.width = model_width
        self.block = model_width // count
        self.taps = tap_count
        self.half = (tap_count - 1) // 2
        self.ghalo = -(-self.half // 16) * 16
        self.xhalo = 2 * self.ghalo
        self.ext = self.chip_frames + 2 * self.ghalo
        self.xext = self.chip_frames + 2 * self.xhalo
        self.tap_rows = -(-tap_count // 16) * 16
        self.stat_rows = self.tap_rows + 8
        self.weight_parts = 2 if groups == 2 else 1
        self.pairs = [(h, 1 - h) for h in range(self.rounds, 0, -1)]
        self.conv_windows = windows(self.ext, self.xhalo - self.ghalo - self.half + tap_count)
        self.back_windows = windows(self.chip_frames, self.ghalo + self.half + 1)

    def window_rows(self, found):
        return found[0] * (found[1] - 1) + POINTS

    def block_slot(self, step, side):
        return 3 + self.batches + 2 * step + side

    def usable(self):
        return (
            self.count % (2 * CORES) == 0
            and self.block == LANES
            and self.block * self.count == self.width
            and self.frames % 128 == 0
            and self.frames >= self.xhalo
            and self.taps % 2 == 1
            and 4 * self.ghalo <= POINTS // 2
            and self.window_rows(self.conv_windows) >= self.xext
            and self.window_rows(self.back_windows) >= self.ext
            and self.window_rows(self.conv_windows)
            >= self.xhalo + self.window_rows(self.back_windows) - self.back_windows[0]
            and self.chips == 8
            and self.batches == 2
        )

    def chip_at(self, position):
        half = self.chips // 2
        return jnp.where(position < half, 2 * position, 2 * (self.chips - 1 - position) + 1)

    def position_of(self, chip):
        return jnp.where(chip % 2 == 0, chip // 2, self.chips - 1 - chip // 2)

    def ring(self):
        half = self.chips // 2
        order = [2 * i for i in range(half)] + [2 * i + 1 for i in reversed(range(half))]
        forward = []
        for core in range(CORES):
            for i in range(self.chips):
                source, target = order[i], order[(i + 1) % self.chips]
                forward.append((CORES * source + core, CORES * target + core))
        return forward, [(t, s) for s, t in forward]

    def edges(self):
        pairs = []
        for chip in range(self.chips - 1):
            last, first = CORES * chip + 1, CORES * (chip + 1)
            pairs += [(last, first), (first, last)]
        return pairs

    def edges_like(self):
        pairs = []
        for chip in range(self.chips - 1):
            pairs.append((CORES * chip + 1, CORES * (chip + 1) + 1))
            pairs.append((CORES * (chip + 1), CORES * chip))
        return pairs

    def partners(self):
        return [(s, s ^ 1) for s in range(self.count)]


def sigmoid(value):
    return 0.5 * jnp.tanh(0.5 * value) + 0.5


def split(value):
    high = value.astype(jnp.bfloat16)
    return high, (value - high.astype(jnp.float32)).astype(jnp.bfloat16)


def split_matrix(matrix):
    high = matrix.astype(jnp.bfloat16)
    return high, (matrix - high.astype(np.float64)).astype(jnp.bfloat16)


def transforms(plan):
    time = np.arange(POINTS)
    theta = np.pi * (2 * np.arange(POINTS // 2) + 1) / POINTS
    angle = theta[:, None] * time[None, :]
    direct = np.concatenate([np.cos(angle), -np.sin(angle)], 0)
    inverse = direct.T * (2.0 / POINTS)

    def spectrum(lags):
        phase = theta[:, None] * lags[None, :]
        matrix = np.concatenate([np.cos(phase), np.sin(phase)], 0)
        return np.pad(matrix, ((0, 0), (0, plan.tap_rows - plan.taps)))

    taps = np.arange(plan.taps)
    back_lags = plan.ghalo + plan.half - taps
    lag_rows = np.pad(inverse[back_lags], ((0, plan.tap_rows - plan.taps), (0, 0)))
    half = lambda m: m.astype(jnp.bfloat16)
    conv_lags = plan.xhalo - plan.ghalo - plan.half + taps
    return (
        half(direct),
        half(inverse),
        np.stack(split_matrix(spectrum(conv_lags))),
        np.stack(split_matrix(spectrum(back_lags))),
        np.stack(split_matrix(lag_rows)),
        half(direct * (time < plan.back_windows[0])),
    )


def taps_spectrum(t_ref, k_ref):
    high, low = split(jnp.concatenate([k_ref[0][...], k_ref[1][...]], axis=1))
    dot = functools.partial(jnp.dot, preferred_element_type=jnp.float32)
    return dot(t_ref[0], high) + dot(t_ref[1], high) + dot(t_ref[0], low)


def to_spectrum(direct_ref, window):
    return jnp.dot(direct_ref[...], window, preferred_element_type=jnp.float32)


def from_spectrum(inverse_ref, rows, parts, slot):
    return jnp.dot(inverse_ref[:rows, :], parts[slot], preferred_element_type=jnp.float32)


def windows(rows_out, reach):
    count = -(-rows_out // ((POINTS - reach) // 16 * 16))
    return -(-rows_out // count // 16) * 16, count


STEP = 16
HALF = POINTS // 2


def spectral_product(spec, taps, parts, slot):
    for row in range(0, HALF, STEP):
        up, down = slice(row, row + STEP), slice(HALF + row, HALF + row + STEP)
        re, im, kr, ks = spec[slot, up, :], spec[slot, down, :], taps[up, :], taps[down, :]
        parts[slot, up, :] = (re * kr - im * ks).astype(jnp.bfloat16)
        parts[slot, down, :] = (re * ks + im * kr).astype(jnp.bfloat16)


def conv_body(plan, info, *refs):
    own_x, other_x, near_x, far_x, k_ref, gain_ref, bias_ref = (
        refs[2 * i : 2 * i + 2] for i in range(7)
    )
    direct, inverse, t_ref, own_g, other_g = refs[14:19]
    conv_ref, x_ref, out_f, out_b, spec, taps, parts, act, acc = refs[19:]
    each, count = plan.conv_windows
    f, xh, gh, cf = plan.frames, plan.xhalo, plan.ghalo, plan.chip_frames
    b = pl.program_id(0)
    core, offset, live = info[0], info[1], info[3 + b]

    @pl.when(b == 0)
    def _():
        taps[...] = taps_spectrum(t_ref, k_ref)

    def put(row, pair):
        for part in range(0, pair[0].shape[1], STEP):
            position = lax.broadcasted_iota(jnp.int32, (STEP, LANES), 0) + (
                offset - xh + row + part
            )
            keep = jnp.where(position < live, 1.0, 0.0).astype(jnp.bfloat16)
            for side in range(2):
                lanes = slice(side * LANES, (side + 1) * LANES)
                x_ref[0, row + part : row + part + STEP, lanes] = (
                    pair[side][0, part : part + STEP, :] * keep
                )

    @pl.when(core == 0)
    def _():
        put(0, near_x)
        put(xh, own_x)
        put(xh + f, other_x)
        put(xh + 2 * f, far_x)

    @pl.when(core != 0)
    def _():
        put(0, far_x)
        put(xh, other_x)
        put(xh + f, own_x)
        put(xh + 2 * f, near_x)

    x_ref[0, plan.xext :, :] = jnp.zeros((x_ref.shape[1] - plan.xext, 2 * LANES), jnp.bfloat16)

    for j in range(count):
        spec[j] = to_spectrum(direct, x_ref[0, j * each : j * each + POINTS, :])
    for j in range(count):
        spectral_product(spec, taps, parts, j)
        rows = min(each, plan.ext - j * each)
        conv_ref[0, j * each : j * each + rows, :] = from_spectrum(inverse, rows, parts, j)

    for i in range(cf // LANES):
        for side in range(2):
            lanes = slice(side * LANES, (side + 1) * LANES)
            begin = gh + i * LANES
            conv = conv_ref[0, begin : begin + LANES, lanes]
            pre = gain_ref[side][...] * conv + bias_ref[side][...]
            position = lax.broadcasted_iota(jnp.int32, (LANES, LANES), 0) + (offset + i * LANES)
            value = jnp.where(position < live, pre * sigmoid(pre), 0.0)
            act[lanes, i * LANES : (i + 1) * LANES] = value.T.astype(jnp.bfloat16)

    own = pl.multiple_of(core * f, f)
    other = pl.multiple_of((1 - core) * f, f)

    def product(columns):
        dot = functools.partial(jnp.dot, preferred_element_type=jnp.float32)
        return dot(act[:, pl.ds(own, f)], own_g[0, :, columns]) + dot(
            act[:, pl.ds(other, f)], other_g[0, :, columns]
        )

    tiles = [slice(c, c + 2 * LANES) for c in range(0, plan.width, 2 * LANES)]

    @pl.when(b == 0)
    def _():
        for columns in tiles:
            acc[:, columns] = product(columns)

    @pl.when(b != 0)
    def _():
        for columns in tiles:
            total = acc[:, columns] + product(columns)
            if plan.batches > 2:
                acc[:, columns] = total
            out_f[:, columns] = total[:LANES].astype(out_f.dtype)
            out_b[:, columns] = total[LANES:].astype(out_b.dtype)


def pair_specs(plan, step, shape, index):
    return [
        pl.BlockSpec(
            shape, lambda b, info, at=plan.block_slot(step, side): index(b, info[at])
        )
        for side in range(2)
    ]


def whole(array):
    return pl.BlockSpec(
        array.shape, lambda *_: (0,) * array.ndim, pipeline_mode=pl.Buffered(1)
    )


def conv_call(plan, step, info, x, xp, xa, xb, g, gp, kernel, gain, bias, consts, kind):
    bt = plan.batches
    flat = lambda b, block: (0, block)
    fixed = lambda b, info: (0, 0)
    direct, inverse, t_conv = consts[:3]
    wide = 2 * LANES
    slots = plan.conv_windows[1]
    specs = functools.partial(pair_specs, plan, step)
    frames, halo = (1, plan.frames, LANES), (1, plan.xhalo, LANES)
    by_batch = lambda b, block: (b, 0, block)
    by_chip = lambda b, block: (b, 0, block // CORES)
    x_rows = plan.window_rows(plan.conv_windows)
    return pl.pallas_call(
        functools.partial(conv_body, plan),
        grid_spec=pltpu.PrefetchScalarGridSpec(
            num_scalar_prefetch=1,
            grid=(bt,),
            in_specs=specs(frames, by_batch)
            + specs(frames, by_batch)
            + specs(halo, by_chip)
            + specs(halo, by_chip)
            + specs((plan.tap_rows, LANES), flat)
            + specs((1, LANES), flat)
            + specs((1, LANES), flat)
            + [whole(direct), whole(inverse), whole(t_conv)]
            + [pl.BlockSpec((1, plan.frames, plan.width), lambda b, info: (b, 0, 0))] * 2,
            out_specs=[
                pl.BlockSpec((1, plan.ext, wide), lambda b, info: (b, 0, 0)),
                pl.BlockSpec((1, x_rows, wide), lambda b, info: (b, 0, 0)),
                pl.BlockSpec((LANES, plan.width), fixed),
                pl.BlockSpec((LANES, plan.width), fixed),
            ],
            scratch_shapes=[
                pltpu.VMEM((slots, POINTS, wide), jnp.float32),
                pltpu.VMEM((POINTS, wide), jnp.float32),
                pltpu.VMEM((slots, POINTS, wide), jnp.bfloat16),
                pltpu.VMEM((wide, plan.chip_frames), jnp.bfloat16),
                pltpu.VMEM((wide, plan.width), jnp.float32),
            ],
        ),
        out_shape=[
            jax.ShapeDtypeStruct((bt, plan.ext, wide), jnp.float32),
            jax.ShapeDtypeStruct((bt, x_rows, wide), jnp.bfloat16),
            jax.ShapeDtypeStruct((LANES, plan.width), kind),
            jax.ShapeDtypeStruct((LANES, plan.width), kind),
        ],
        compiler_params=pltpu.CompilerParams(vmem_limit_bytes=VMEM_LIMIT),
        cost_estimate=cost(6.0),
        name="conv",
    )(info, x, x, xp, xp, xa, xa, xb, xb, kernel, kernel, gain, gain, bias, bias,
      direct, inverse, t_conv, g, gp)


def back_body(plan, steps, sources, info, *refs):
    pairs = len(steps)
    mg_ref = refs[0]
    k_refs, gain_refs, bias_refs = (
        refs[1 + 2 * pairs * i : 1 + 2 * pairs * (i + 1)] for i in range(3)
    )
    refs = refs[1 + 6 * pairs :]
    conv_refs, x_refs, w_refs = refs[:pairs], refs[pairs : 2 * pairs], refs[2 * pairs : -25]
    direct, segment, inverse, t_ref, lag_ref = refs[-25:-20]
    (own_ref, send_ref, stat_ref, weight, conv_buf, x_buf, ag, gs, tail, spec, xspec, taps,
     cross, parts, os, sums, flat, w_sem, c_sem, x_sem) = refs[-20:]
    core, offset, side_y = info[0], info[1], info[2]
    f, xh, gh, cf, ext = plan.frames, plan.xhalo, plan.ghalo, plan.chip_frames, plan.ext
    each, count = plan.back_windows
    turn, b = pl.program_id(0), pl.program_id(1)
    live = info[3 + b]

    def weight_copies(pair):
        made = []
        for n, (array, part, target, begin, rows) in enumerate(sources[pair]):
            first, into = begin, target * LANES
            if part is not None:
                into = pl.multiple_of(target * LANES + (side_y + part) % 2 * rows, rows)
            made.append(
                pltpu.make_async_copy(
                    w_refs[array].at[pl.ds(first, rows), :],
                    weight.at[pair, pl.ds(into, rows), :],
                    w_sem.at[pair, n],
                )
            )
        return made

    def conv_copies(pair):
        return [
            pltpu.make_async_copy(conv_refs[pair].at[i], conv_buf.at[pair, i], c_sem.at[pair, i])
            for i in range(plan.batches)
        ] + [
            pltpu.make_async_copy(x_refs[pair].at[i], x_buf.at[pair, i], x_sem.at[pair, i])
            for i in range(plan.batches)
        ]

    @pl.when((turn == 0) & (b == 0))
    def _():
        for pair in range(pairs):
            for copy in weight_copies(pair) + conv_copies(pair):
                copy.start()
        gs[ext:, :] = jnp.zeros((gs.shape[0] - ext, 2 * LANES), jnp.bfloat16)
        tail[...] = jnp.zeros_like(tail)

    for pair in range(pairs):

        @pl.when((turn == pair) & (b == 0))
        def _():
            taps[...] = taps_spectrum(t_ref, k_refs[2 * pair : 2 * pair + 2])
            for row, pick in ((0, gain_refs), (8, bias_refs)):
                for side in range(2):
                    lanes = slice(side * LANES, (side + 1) * LANES)
                    flat[row : row + 8, lanes] = jnp.broadcast_to(
                        pick[2 * pair + side][...], (8, LANES)
                    )
            cross[...] = jnp.zeros_like(cross)
            sums[...] = jnp.zeros_like(sums)
            for copy in weight_copies(pair) + conv_copies(pair):
                copy.wait()

    last_rows = cf - (count - 1) * each
    for j in range(count):
        begin = xh + j * each
        if j < count - 1:
            window = x_buf[turn, b, begin : begin + POINTS, :]
        else:
            tail[:last_rows, :] = x_buf[turn, b, begin : begin + last_rows, :]
            window = tail[...]
        xspec[j] = to_spectrum(segment, window)

    ag[...] = lax.dot_general(
        mg_ref[0], weight[turn], (((1,), (1,)), ((), ())), preferred_element_type=jnp.float32
    )
    gain, bias = flat[:1, :], flat[8:9, :]

    gain_sum = jnp.zeros((8, 2 * LANES), jnp.float32)
    bias_sum = jnp.zeros((8, 2 * LANES), jnp.float32)
    for row in range(0, ext, STEP):
        conv = conv_buf[turn, b, row : row + STEP, :]
        pre = gain * conv + bias
        sig = sigmoid(pre)
        value = ag[row : row + STEP, :] * sig * (1.0 + pre * (1.0 - sig))
        gs[row : row + STEP, :] = (value * gain).astype(jnp.bfloat16)
        if gh <= row < gh + cf:
            fold = lambda v: jnp.sum(v.reshape(STEP // 8, 8, 2 * LANES), axis=0)
            gain_sum = gain_sum + fold(value * conv)
            bias_sum = bias_sum + fold(value)
    sums[0] += gain_sum
    sums[1] += bias_sum

    for j in range(count):
        spec[j] = to_spectrum(direct, gs[j * each : j * each + POINTS, :])
    for j in range(count):
        spectral_product(spec, taps, parts, j)
        rows = min(each, cf - j * each)
        value = from_spectrum(inverse, rows, parts, j)
        position = offset + j * each + lax.broadcasted_iota(jnp.int32, value.shape, 0)
        os[j * each : j * each + rows, :] = jnp.where(position < live, value, 0.0).astype(
            jnp.bfloat16
        )
    for row in range(0, HALF, STEP):
        up, down = slice(row, row + STEP), slice(HALF + row, HALF + row + STEP)
        total_r, total_i = cross[up, :], cross[down, :]
        for j in range(count):
            re, im, xr, xi = spec[j, up, :], spec[j, down, :], xspec[j, up, :], xspec[j, down, :]
            total_r = total_r + re * xr + im * xi
            total_i = total_i + im * xr - re * xi
        cross[up, :] = total_r
        cross[down, :] = total_i

    @pl.when(core == 0)
    def _():
        own_ref[0, 0] = os[:f]
        send_ref[0, 0] = os[f:]

    @pl.when(core != 0)
    def _():
        own_ref[0, 0] = os[f:]
        send_ref[0, 0] = os[:f]

    @pl.when(b == plan.batches - 1)
    def _():
        high, low = split(cross[...])
        dot = functools.partial(jnp.dot, preferred_element_type=jnp.float32)
        stat_ref[0, : plan.tap_rows] = (
            dot(lag_ref[0], high) + dot(lag_ref[1], high) + dot(lag_ref[0], low)
        )
        total = [jnp.sum(sums[i], axis=0, keepdims=True) for i in range(2)]
        pad = jnp.zeros((plan.stat_rows - plan.tap_rows - 2, 2 * LANES), jnp.float32)
        stat_ref[0, plan.tap_rows :] = jnp.concatenate(total + [pad], axis=0)


def back_call(plan, steps, info, mg, sources, arrays, convs, xs, kernel, gain, bias, consts):
    bt, pairs = plan.batches, len(steps)
    direct, inverse, _, t_back, lags, segment = consts
    wide = 2 * LANES
    slots = plan.back_windows[1]
    any_space = pl.BlockSpec(memory_space=pl.ANY)

    def by_block(shape):
        return [
            pl.BlockSpec(
                shape, lambda p, b, info, at=plan.block_slot(step, side): (0, info[at]),
                pipeline_mode=pl.Buffered(1),
            )
            for step in steps for side in range(2)
        ]

    each = lambda *tail: pl.BlockSpec((1, 1) + tail, lambda p, b, info: (p, b, 0, 0))
    most = max(len(source) for source in sources)
    return pl.pallas_call(
        functools.partial(back_body, plan, steps, sources),
        grid_spec=pltpu.PrefetchScalarGridSpec(
            num_scalar_prefetch=1,
            grid=(pairs, bt),
            in_specs=[
                pl.BlockSpec((1, plan.ext, plan.width), lambda p, b, info: (b, 0, 0)),
            ]
            + by_block((plan.tap_rows, LANES))
            + by_block((1, LANES))
            + by_block((1, LANES))
            + [any_space] * (2 * pairs + len(arrays))
            + [whole(c) for c in (direct, segment, inverse, t_back, lags)],
            out_specs=[
                each(plan.frames, wide),
                each(plan.frames, wide),
                pl.BlockSpec((1, plan.stat_rows, wide), lambda p, b, info: (p, 0, 0)),
            ],
            scratch_shapes=[
                pltpu.VMEM((pairs, wide, plan.width), jnp.bfloat16),
                pltpu.VMEM((pairs, bt, plan.ext, wide), jnp.float32),
                pltpu.VMEM((pairs, bt, xs[0].shape[1], wide), jnp.bfloat16),
                pltpu.VMEM((plan.ext, wide), jnp.float32),
                pltpu.VMEM((plan.window_rows(plan.back_windows), wide), jnp.bfloat16),
                pltpu.VMEM((POINTS, wide), jnp.bfloat16),
                pltpu.VMEM((slots, POINTS, wide), jnp.float32),
                pltpu.VMEM((slots, POINTS, wide), jnp.float32),
                pltpu.VMEM((POINTS, wide), jnp.float32),
                pltpu.VMEM((POINTS, wide), jnp.float32),
                pltpu.VMEM((slots, POINTS, wide), jnp.bfloat16),
                pltpu.VMEM((plan.chip_frames, wide), jnp.bfloat16),
                pltpu.VMEM((2, 8, wide), jnp.float32),
                pltpu.VMEM((16, wide), jnp.float32),
                pltpu.SemaphoreType.DMA((pairs, most)),
                pltpu.SemaphoreType.DMA((pairs, bt)),
                pltpu.SemaphoreType.DMA((pairs, bt)),
            ],
        ),
        out_shape=[
            jax.ShapeDtypeStruct((pairs, bt, plan.frames, wide), jnp.bfloat16),
            jax.ShapeDtypeStruct((pairs, bt, plan.frames, wide), jnp.bfloat16),
            jax.ShapeDtypeStruct((pairs, plan.stat_rows, wide), jnp.float32),
        ],
        compiler_params=pltpu.CompilerParams(vmem_limit_bytes=VMEM_LIMIT),
        cost_estimate=cost(6.0 * pairs),
        name="back",
    )(info, mg, *[kernel] * 2 * pairs, *[gain] * 2 * pairs, *[bias] * 2 * pairs,
      *convs, *xs, *arrays, direct, segment, inverse, t_back, lags)


def place_body(plan, calls, info, *refs):
    out_ref = refs[-1]
    for i, ref in enumerate(refs[:-1]):
        for turn, step in enumerate(calls[i // 2]):
            for side in range(2):
                block = info[plan.block_slot(step, side)]
                if i % 2:
                    block = block + 1 - 2 * info[0]
                column = pl.multiple_of(block * LANES, LANES)
                lanes = slice(side * LANES, (side + 1) * LANES)
                out_ref[:, :, pl.ds(column, LANES)] = ref[turn, :, :, lanes]


def place_call(plan, calls, info, arrays):
    shape = (plan.batches, plan.frames, plan.width)
    return pl.pallas_call(
        functools.partial(place_body, plan, calls),
        grid_spec=pltpu.PrefetchScalarGridSpec(
            num_scalar_prefetch=1,
            grid=(1,),
            in_specs=[whole(array) for array in arrays],
            out_specs=pl.BlockSpec(shape, lambda g, info: (0, 0, 0)),
        ),
        out_shape=jax.ShapeDtypeStruct(shape, jnp.bfloat16),
        compiler_params=pltpu.CompilerParams(vmem_limit_bytes=VMEM_LIMIT),
        cost_estimate=cost(3.0),
        name="place",
    )(info, *arrays)


def deal_body(plan, calls, info, *refs):
    out_ref = refs[-1]
    for steps, ref in zip(calls, refs[:-1]):
        for turn, step in enumerate(steps):
            for side in range(2):
                chip = info[plan.block_slot(step, side)] // CORES
                out_ref[chip] = ref[turn, :, side * LANES : (side + 1) * LANES]


def deal_call(plan, calls, info, arrays):
    shape = (plan.chips, plan.stat_rows, LANES)
    return pl.pallas_call(
        functools.partial(deal_body, plan, calls),
        grid_spec=pltpu.PrefetchScalarGridSpec(
            num_scalar_prefetch=1,
            grid=(1,),
            in_specs=[whole(array) for array in arrays],
            out_specs=pl.BlockSpec(shape, lambda g, info: (0, 0, 0)),
        ),
        out_shape=jax.ShapeDtypeStruct(shape, jnp.float32),
        cost_estimate=cost(1.0),
        name="deal",
    )(info, *arrays)


def edge_body(plan, x_first, x_last, g_first, g_last, near_ref, far_ref, g_ref):
    core = lax.axis_index("shard") % CORES

    def take(owner, x_ref, grad_ref):
        for i in range(plan.chips):
            for out, parity in ((near_ref, 1 - owner), (far_ref, owner)):
                column = (CORES * i + parity) * LANES
                out[:, :, i * LANES : (i + 1) * LANES] = x_ref[:, :, column : column + LANES]
        g_ref[...] = grad_ref[...]

    pl.when(core == 0)(lambda: take(0, x_first, g_first))
    pl.when(core != 0)(lambda: take(1, x_last, g_last))


def edge_call(plan, x, g):
    def spec(rows, first):
        shape = (plan.batches, rows, plan.width)
        block = 0 if first else plan.frames // rows - 1
        return pl.BlockSpec(shape, lambda i: (0, block, 0))

    xh, gh = plan.xhalo, plan.ghalo
    half = (plan.batches, xh, plan.width // CORES)
    shapes = [half, half, (plan.batches, gh, plan.width)]
    return pl.pallas_call(
        functools.partial(edge_body, plan),
        grid=(1,),
        in_specs=[spec(xh, True), spec(xh, False), spec(gh, True), spec(gh, False)],
        out_specs=[pl.BlockSpec(shape, lambda i: (0, 0, 0)) for shape in shapes],
        out_shape=[jax.ShapeDtypeStruct(shape, jnp.bfloat16) for shape in shapes],
        cost_estimate=cost(1.0),
        name="edge",
    )(x, x, g, g)


def assemble_body(plan, halo, info, own_ref, other_ref, near_ref, far_ref, out_ref):
    core, offset, live = info[0], info[1], info[3 + pl.program_id(0)]
    f = plan.frames

    def put(row, ref):
        for part in range(0, ref.shape[1], STEP):
            position = lax.broadcasted_iota(jnp.int32, (STEP, LANES), 0) + (
                offset - halo + row + part
            )
            keep = jnp.where(position < live, 1.0, 0.0).astype(jnp.bfloat16)
            for i in range(plan.count):
                lanes = slice(i * LANES, (i + 1) * LANES)
                out_ref[0, row + part : row + part + STEP, lanes] = (
                    ref[0, part : part + STEP, lanes] * keep
                )

    @pl.when(core == 0)
    def _():
        put(0, near_ref)
        put(halo, own_ref)
        put(halo + f, other_ref)
        put(halo + 2 * f, far_ref)

    @pl.when(core != 0)
    def _():
        put(0, far_ref)
        put(halo, other_ref)
        put(halo + f, own_ref)
        put(halo + 2 * f, near_ref)


def assemble_call(plan, info, own, other, near, far):
    halo = near.shape[1]
    spec = lambda n: pl.BlockSpec((1, n, plan.width), lambda b, info: (b, 0, 0))
    return pl.pallas_call(
        functools.partial(assemble_body, plan, halo),
        grid_spec=pltpu.PrefetchScalarGridSpec(
            num_scalar_prefetch=1,
            grid=(plan.batches,),
            in_specs=[spec(plan.frames), spec(plan.frames), spec(halo), spec(halo)],
            out_specs=spec(plan.ext),
        ),
        out_shape=jax.ShapeDtypeStruct((plan.batches, plan.ext, plan.width), jnp.bfloat16),
        compiler_params=pltpu.CompilerParams(vmem_limit_bytes=VMEM_LIMIT),
        cost_estimate=cost(5.0),
        name="assemble",
    )(info, own, other, near, far)


def after(value, *others):
    return lax.optimization_barrier((value, *others))[0]


def ring_shards(plan, grad_out, saved_input, lengths, kernel, gain, bias, proj_weight):
    index = lax.axis_index("shard")
    group = lax.axis_index("groups")
    core, chip = index % CORES, index // CORES
    place = plan.position_of(chip)
    forward, backward = plan.ring()
    offset = chip * plan.chip_frames
    scale = lax.rsqrt(jnp.sum(lengths).astype(jnp.float32))
    pairs = plan.pairs
    far = jnp.asarray([d for pair in pairs for d in pair], jnp.int32)
    owned = CORES * plan.chip_at((place + far + plan.chips) % plan.chips) + core
    info = jnp.concatenate([jnp.stack([core, offset, group]), lengths, owned]).astype(jnp.int32)
    gain2, bias2 = gain.reshape(1, -1), bias.reshape(1, -1)
    taps = jnp.pad(kernel, ((0, plan.tap_rows - plan.taps), (0, 0)))
    consts = [jnp.asarray(c) for c in transforms(plan)]

    x_near, x_far, g_edge = edge_call(plan, saved_input, grad_out)
    xa = lax.ppermute(x_near, "shard", plan.edges())
    xb = lax.ppermute(x_far, "shard", plan.edges_like())
    xp = lax.ppermute(saved_input, "shard", plan.partners())
    mgp = lax.ppermute(grad_out, "shard", plan.partners())

    halved = plan.weight_parts == 2
    piece = LANES // 2
    around = {}
    going = [proj_weight] * 2
    if halved:
        going = [lax.dynamic_slice_in_dim(proj_weight, group * piece, piece, 0)] * 2
    xa, xb, taps, info = lax.optimization_barrier((xa, xb, taps, info))

    def weight_round(step):
        going[0] = lax.ppermute(going[0], "shard", forward)
        around[-step] = going[0]
        if step < plan.rounds:
            going[1] = lax.ppermute(going[1], "shard", backward)
            around[step] = going[1]
        else:
            around[step] = around.pop(-step)

    convs, xs, products = [], [], []

    def conv_step(step, order):
        conv, x, *product = conv_call(
            plan, step, order, saved_input, xp, xa, xb, grad_out,
            mgp, taps, gain2, bias2, consts, jnp.bfloat16 if step == 0 else jnp.float32,
        )
        convs.append(conv)
        xs.append(x)
        products.append(product)

    def sum_round(step, send, *behind):
        received = (
            lax.ppermute(send[0], "shard", forward), lax.ppermute(send[1], "shard", backward)
        )
        kinds = (jnp.bfloat16, jnp.bfloat16 if step < plan.rounds - 1 else jnp.float32)
        own = lax.optimization_barrier((*products[step], *received, *behind))[:2]
        return [
            (product + value.astype(jnp.float32)).astype(kind)
            for product, value, kind in zip(own, received, kinds)
        ]

    def wait_for(value):
        going[:] = lax.optimization_barrier((*going, value))[:2]

    weight_round(1)
    conv_step(0, info)
    g_edge = after(g_edge, products[0][0])
    ga = lax.ppermute(g_edge, "shard", plan.edges())
    gb = lax.ppermute(g_edge, "shard", plan.edges_like())
    wait_for(products[0][0])
    weight_round(2)
    conv_step(1, after(info, products[0][0]))
    wait_for(products[1][0])
    weight_round(3)
    mg = assemble_call(plan, after(info, products[1][0]), grad_out, mgp, ga, gb)
    wait_for(mg)
    weight_round(4)
    send = sum_round(1, products[0], mg)
    conv_step(2, after(info, products[1][0], *send, mg))
    conv_step(3, after(info, products[2][0]))
    send = sum_round(2, send, products[3][0])

    arrays = [proj_weight]
    source = {0: [(0, None, 0, LANES)]}

    def keep(array):
        arrays.append(array)
        return len(arrays) - 1

    swap = [
        (g * plan.count + s, (1 - g) * plan.count + s) for g in range(2) for s in range(plan.count)
    ]
    for distances in ([1, -1], [2, -2], [3, -3, 4]):
        if not halved:
            for d in distances:
                source[d] = [(keep(around[d]), None, 0, LANES)]
            continue
        swapped = keep(
            lax.ppermute(
                jnp.concatenate([around[d] for d in distances], 0),
                ("groups", "shard"), swap,
            )
        )
        for i, d in enumerate(distances):
            source[d] = [(keep(around[d]), 0, 0, piece), (swapped, 1, i * piece, piece)]

    calls = [(3, 2), (1, 0)]
    pieces, stats = [], []
    for steps in calls:
        if steps == calls[-1]:
            send = sum_round(3, send, pieces[0])
        order = after(info, products[-1][0], *send)
        used = sorted({a[0] for step in steps for d in pairs[step] for a in source[d]})
        sources = [
            [
                (used.index(array), part, block, begin, rows)
                for block, d in enumerate(pairs[step])
                for array, part, begin, rows in source[d]
            ]
            for step in steps
        ]
        own, given, stat = back_call(
            plan, steps, order, mg, sources, [arrays[i] for i in used],
            [convs[step] for step in steps], [xs[step] for step in steps],
            taps, gain2, bias2, consts,
        )
        stats.append(stat)
        pieces += [own, lax.ppermute(given, "shard", plan.partners())]
    recv_f = after(lax.ppermute(send[0], "shard", forward), stats[-1])
    proj_grad = (send[1] + recv_f.astype(jnp.float32)) * scale
    dealt = deal_call(plan, calls, info, stats)
    groups = [[CORES * p + c for p in range(plan.chips)] for c in range(CORES)]
    shares = lax.all_to_all(dealt, "shard", 0, 0, axis_index_groups=groups)
    full = place_call(plan, calls, after(info, dealt), pieces)
    summed = jnp.sum(after(shares, full, proj_grad), axis=0) * scale
    return (
        full, proj_grad, summed[: plan.taps], summed[plan.tap_rows : plan.tap_rows + 2]
    )


def shards(count, group_count, grad_out, saved_input, lengths, kernel, gain, bias, proj_weight):
    batches, frames, model_width = grad_out.shape
    plan = Plan(count, group_count, batches, frames, model_width, kernel.shape[0])
    args = (grad_out, saved_input, lengths, kernel, gain, bias, proj_weight)
    return ring_shards(plan, *args) if plan.usable() else plain_shards(*args)


def solution(mesh):
    placed = (
        P("groups", "shard", None),
        P("groups", "shard", None),
        P("groups"),
        P(),
        P(),
        P(),
        P("shard", None),
    )

    def body(*args):
        return shards(mesh.shape["shard"], mesh.shape["groups"], *args)

    return jax.shard_map(
        body,
        mesh=mesh,
        in_specs=placed,
        out_specs=(
            P("groups", "shard", None),
            P(("groups", "shard"), None),
            P("groups", "shard"),
            P("groups", "shard"),
        ),
        check_vma=False,
    )
```

```python
import functools

import jax
import jax.numpy as jnp
import numpy as np
from jax import lax
from jax.experimental import pallas as pl
from jax.experimental.pallas import tpu as pltpu
from jax.sharding import PartitionSpec as P


LANES = 128
CORES = 2
VMEM_LIMIT = 56 * 1024 * 1024
POINTS = 256


def cost(micros):
    return pl.CostEstimate(flops=0, transcendentals=0, bytes_accessed=int(micros * 3.6e6))


def extended(block, width):
    count = lax.axis_size("shard")
    forward = [(i, i + 1) for i in range(count - 1)]
    backward = [(target, source) for source, target in forward]
    low = lax.ppermute(block[:, block.shape[1] - width :], "shard", forward)
    high = lax.ppermute(block[:, :width], "shard", backward)
    return jnp.concatenate([low, block, high], axis=1)


def frame_mask(lengths, offset, count):
    position = offset + jnp.arange(count, dtype=jnp.int32)
    return (position[None, :] < lengths[:, None])[:, :, None]


def plain_shards(grad_out, saved_input, lengths, kernel, gain, bias, proj_weight):
    batches, frames, model_width = grad_out.shape
    tap_count = kernel.shape[0]
    half_span = (tap_count - 1) // 2
    offset = lax.axis_index("shard") * frames
    norm_scale = lax.rsqrt(jnp.sum(lengths).astype(jnp.float32))
    own_mask = frame_mask(lengths, offset, frames)
    masked_in = jnp.where(own_mask, saved_input, jnp.zeros_like(saved_input))
    masked_grad = jnp.where(own_mask, grad_out, jnp.zeros_like(grad_out))
    in_ext = extended(masked_in, half_span)
    conv = jnp.zeros(grad_out.shape, jnp.float32)
    for tap in range(tap_count):
        conv = conv + kernel[tap] * in_ext[:, tap : tap + frames].astype(jnp.float32)
    pre_act = gain * conv + bias
    gate_sig = jax.nn.sigmoid(pre_act)
    activated = (pre_act * gate_sig).astype(jnp.bfloat16)
    rows = masked_grad.reshape(batches * frames, model_width)
    weight = lax.all_gather(proj_weight, "shard", axis=0, tiled=True)
    act_grad = lax.dot_general(
        rows, weight, (((1,), (1,)), ((), ())), preferred_element_type=jnp.float32
    ).reshape(batches, frames, model_width)
    pre_grad = act_grad * gate_sig * (1.0 + pre_act * (1.0 - gate_sig))
    conv_grad = (pre_grad * gain).astype(jnp.bfloat16)
    grad_ext = extended(conv_grad, half_span)
    back_sum = jnp.zeros(grad_out.shape, jnp.float32)
    grad_float = conv_grad.astype(jnp.float32)
    tap_rows = []
    for tap in range(tap_count):
        begin = 2 * half_span - tap
        back_sum = back_sum + kernel[tap] * grad_ext[:, begin : begin + frames].astype(jnp.float32)
        tap_rows.append(
            jnp.sum(in_ext[:, tap : tap + frames].astype(jnp.float32) * grad_float, axis=(0, 1))
        )
    input_grad = jnp.where(own_mask, back_sum, 0.0).astype(jnp.bfloat16)
    tap_rows.append(jnp.sum(pre_grad * conv, axis=(0, 1)))
    tap_rows.append(jnp.sum(pre_grad, axis=(0, 1)))
    stats = jnp.stack(tap_rows, 0) * norm_scale
    summed = lax.psum_scatter(stats, "shard", scatter_dimension=1, tiled=True)
    product = lax.dot_general(
        activated.reshape(batches * frames, model_width),
        rows,
        (((0,), (0,)), ((), ())),
        preferred_element_type=jnp.float32,
    )
    proj_grad = lax.psum_scatter(product * norm_scale, "shard", scatter_dimension=0, tiled=True)
    return (input_grad, proj_grad, summed[:tap_count], summed[tap_count:])


class Plan:
    def __init__(self, count, groups, batches, frames, model_width, tap_count):
        self.count = count
        self.chips = count // CORES
        self.rounds = self.chips // 2
        self.batches = batches
        self.frames = frames
        self.chip_frames = CORES * frames
        self.width = model_width
        self.block = model_width // count
        self.taps = tap_count
        self.half = (tap_count - 1) // 2
        self.ghalo = -(-self.half // 16) * 16
        self.xhalo = 2 * self.ghalo
        self.ext = self.chip_frames + 2 * self.ghalo
        self.xext = self.chip_frames + 2 * self.xhalo
        self.tap_rows = -(-tap_count // 16) * 16
        self.stat_rows = self.tap_rows + 8
        self.weight_parts = 2 if groups == 2 else 1
        self.pairs = [(h, 1 - h) for h in range(self.rounds, 0, -1)]
        self.conv_windows = windows(self.ext, self.xhalo - self.ghalo - self.half + tap_count)
        self.back_windows = windows(self.chip_frames, self.ghalo + self.half + 1)

    def window_rows(self, found):
        return found[0] * (found[1] - 1) + POINTS

    def block_slot(self, step, side):
        return 3 + self.batches + 2 * step + side

    def usable(self):
        return (
            self.count % (2 * CORES) == 0
            and self.block == LANES
            and self.block * self.count == self.width
            and self.frames % 128 == 0
            and self.frames >= self.xhalo
            and self.taps % 2 == 1
            and 4 * self.ghalo <= POINTS // 2
            and self.window_rows(self.conv_windows) >= self.xext
            and self.window_rows(self.back_windows) >= self.ext
            and self.window_rows(self.conv_windows)
            >= self.xhalo + self.window_rows(self.back_windows) - self.back_windows[0]
            and self.chips == 8
            and self.batches == 2
        )

    def chip_at(self, position):
        half = self.chips // 2
        return jnp.where(position < half, 2 * position, 2 * (self.chips - 1 - position) + 1)

    def position_of(self, chip):
        return jnp.where(chip % 2 == 0, chip // 2, self.chips - 1 - chip // 2)

    def ring(self):
        half = self.chips // 2
        order = [2 * i for i in range(half)] + [2 * i + 1 for i in reversed(range(half))]
        forward = []
        for core in range(CORES):
            for i in range(self.chips):
                source, target = order[i], order[(i + 1) % self.chips]
                forward.append((CORES * source + core, CORES * target + core))
        return forward, [(t, s) for s, t in forward]

    def edges(self):
        pairs = []
        for chip in range(self.chips - 1):
            last, first = CORES * chip + 1, CORES * (chip + 1)
            pairs += [(last, first), (first, last)]
        return pairs

    def edges_like(self):
        pairs = []
        for chip in range(self.chips - 1):
            pairs.append((CORES * chip + 1, CORES * (chip + 1) + 1))
            pairs.append((CORES * (chip + 1), CORES * chip))
        return pairs

    def partners(self):
        return [(s, s ^ 1) for s in range(self.count)]


def sigmoid(value):
    return 0.5 * jnp.tanh(0.5 * value) + 0.5


def split(value):
    high = value.astype(jnp.bfloat16)
    return high, (value - high.astype(jnp.float32)).astype(jnp.bfloat16)


def split_matrix(matrix):
    high = matrix.astype(jnp.bfloat16)
    return high, (matrix - high.astype(np.float64)).astype(jnp.bfloat16)


def transforms(plan):
    time = np.arange(POINTS)
    theta = np.pi * (2 * np.arange(POINTS // 2) + 1) / POINTS
    angle = theta[:, None] * time[None, :]
    direct = np.concatenate([np.cos(angle), -np.sin(angle)], 0)
    inverse = direct.T * (2.0 / POINTS)

    def spectrum(lags):
        phase = theta[:, None] * lags[None, :]
        matrix = np.concatenate([np.cos(phase), np.sin(phase)], 0)
        return np.pad(matrix, ((0, 0), (0, plan.tap_rows - plan.taps)))

    taps = np.arange(plan.taps)
    back_lags = plan.ghalo + plan.half - taps
    lag_rows = np.pad(inverse[back_lags], ((0, plan.tap_rows - plan.taps), (0, 0)))
    half = lambda m: m.astype(jnp.bfloat16)
    conv_lags = plan.xhalo - plan.ghalo - plan.half + taps
    return (
        half(direct),
        half(inverse),
        np.stack(split_matrix(spectrum(conv_lags))),
        np.stack(split_matrix(spectrum(back_lags))),
        np.stack(split_matrix(lag_rows)),
        half(direct * (time < plan.back_windows[0])),
    )


def taps_spectrum(t_ref, k_ref):
    high, low = split(jnp.concatenate([k_ref[0][...], k_ref[1][...]], axis=1))
    dot = functools.partial(jnp.dot, preferred_element_type=jnp.float32)
    return dot(t_ref[0], high) + dot(t_ref[1], high) + dot(t_ref[0], low)


def to_spectrum(direct_ref, window):
    return jnp.dot(direct_ref[...], window, preferred_element_type=jnp.float32)


def from_spectrum(inverse_ref, rows, parts, slot):
    return jnp.dot(inverse_ref[:rows, :], parts[slot], preferred_element_type=jnp.float32)


def windows(rows_out, reach):
    count = -(-rows_out // ((POINTS - reach) // 16 * 16))
    return -(-rows_out // count // 16) * 16, count


STEP = 16
HALF = POINTS // 2


def spectral_product(spec, taps, parts, slot):
    for row in range(0, HALF, STEP):
        up, down = slice(row, row + STEP), slice(HALF + row, HALF + row + STEP)
        re, im, kr, ks = spec[slot, up, :], spec[slot, down, :], taps[up, :], taps[down, :]
        parts[slot, up, :] = (re * kr - im * ks).astype(jnp.bfloat16)
        parts[slot, down, :] = (re * ks + im * kr).astype(jnp.bfloat16)


def conv_body(plan, info, *refs):
    own_x, other_x, near_x, far_x, k_ref, gain_ref, bias_ref = (
        refs[2 * i : 2 * i + 2] for i in range(7)
    )
    direct, inverse, t_ref, own_g, other_g = refs[14:19]
    conv_ref, x_ref, out_f, out_b, spec, taps, parts, act, acc = refs[19:]
    each, count = plan.conv_windows
    f, xh, gh, cf = plan.frames, plan.xhalo, plan.ghalo, plan.chip_frames
    b = pl.program_id(0)
    core, offset, live = info[0], info[1], info[3 + b]

    @pl.when(b == 0)
    def _():
        taps[...] = taps_spectrum(t_ref, k_ref)

    def put(row, pair):
        for part in range(0, pair[0].shape[1], STEP):
            position = lax.broadcasted_iota(jnp.int32, (STEP, LANES), 0) + (
                offset - xh + row + part
            )
            keep = jnp.where(position < live, 1.0, 0.0).astype(jnp.bfloat16)
            for side in range(2):
                lanes = slice(side * LANES, (side + 1) * LANES)
                x_ref[0, row + part : row + part + STEP, lanes] = (
                    pair[side][0, part : part + STEP, :] * keep
                )

    @pl.when(core == 0)
    def _():
        put(0, near_x)
        put(xh, own_x)
        put(xh + f, other_x)
        put(xh + 2 * f, far_x)

    @pl.when(core != 0)
    def _():
        put(0, far_x)
        put(xh, other_x)
        put(xh + f, own_x)
        put(xh + 2 * f, near_x)

    x_ref[0, plan.xext :, :] = jnp.zeros((x_ref.shape[1] - plan.xext, 2 * LANES), jnp.bfloat16)

    for j in range(count):
        spec[j] = to_spectrum(direct, x_ref[0, j * each : j * each + POINTS, :])
    for j in range(count):
        spectral_product(spec, taps, parts, j)
        rows = min(each, plan.ext - j * each)
        conv_ref[0, j * each : j * each + rows, :] = from_spectrum(inverse, rows, parts, j)

    for i in range(cf // LANES):
        for side in range(2):
            lanes = slice(side * LANES, (side + 1) * LANES)
            begin = gh + i * LANES
            conv = conv_ref[0, begin : begin + LANES, lanes]
            pre = gain_ref[side][...] * conv + bias_ref[side][...]
            position = lax.broadcasted_iota(jnp.int32, (LANES, LANES), 0) + (offset + i * LANES)
            value = jnp.where(position < live, pre * sigmoid(pre), 0.0)
            act[lanes, i * LANES : (i + 1) * LANES] = value.T.astype(jnp.bfloat16)

    own = pl.multiple_of(core * f, f)
    other = pl.multiple_of((1 - core) * f, f)

    def product(columns):
        dot = functools.partial(jnp.dot, preferred_element_type=jnp.float32)
        return dot(act[:, pl.ds(own, f)], own_g[0, :, columns]) + dot(
            act[:, pl.ds(other, f)], other_g[0, :, columns]
        )

    tiles = [slice(c, c + 2 * LANES) for c in range(0, plan.width, 2 * LANES)]

    @pl.when(b == 0)
    def _():
        for columns in tiles:
            acc[:, columns] = product(columns)

    @pl.when(b != 0)
    def _():
        for columns in tiles:
            total = acc[:, columns] + product(columns)
            if plan.batches > 2:
                acc[:, columns] = total
            out_f[:, columns] = total[:LANES].astype(out_f.dtype)
            out_b[:, columns] = total[LANES:].astype(out_b.dtype)


def pair_specs(plan, step, shape, index):
    return [
        pl.BlockSpec(
            shape, lambda b, info, at=plan.block_slot(step, side): index(b, info[at])
        )
        for side in range(2)
    ]


def whole(array):
    return pl.BlockSpec(
        array.shape, lambda *_: (0,) * array.ndim, pipeline_mode=pl.Buffered(1)
    )


def conv_call(plan, step, info, x, xp, xa, xb, g, gp, kernel, gain, bias, consts, kind):
    bt = plan.batches
    flat = lambda b, block: (0, block)
    fixed = lambda b, info: (0, 0)
    direct, inverse, t_conv = consts[:3]
    wide = 2 * LANES
    slots = plan.conv_windows[1]
    specs = functools.partial(pair_specs, plan, step)
    frames, halo = (1, plan.frames, LANES), (1, plan.xhalo, LANES)
    by_batch = lambda b, block: (b, 0, block)
    by_chip = lambda b, block: (b, 0, block // CORES)
    x_rows = plan.window_rows(plan.conv_windows)
    return pl.pallas_call(
        functools.partial(conv_body, plan),
        grid_spec=pltpu.PrefetchScalarGridSpec(
            num_scalar_prefetch=1,
            grid=(bt,),
            in_specs=specs(frames, by_batch)
            + specs(frames, by_batch)
            + specs(halo, by_chip)
            + specs(halo, by_chip)
            + specs((plan.tap_rows, LANES), flat)
            + specs((1, LANES), flat)
            + specs((1, LANES), flat)
            + [whole(direct), whole(inverse), whole(t_conv)]
            + [pl.BlockSpec((1, plan.frames, plan.width), lambda b, info: (b, 0, 0))] * 2,
            out_specs=[
                pl.BlockSpec((1, plan.ext, wide), lambda b, info: (b, 0, 0)),
                pl.BlockSpec((1, x_rows, wide), lambda b, info: (b, 0, 0)),
                pl.BlockSpec((LANES, plan.width), fixed),
                pl.BlockSpec((LANES, plan.width), fixed),
            ],
            scratch_shapes=[
                pltpu.VMEM((slots, POINTS, wide), jnp.float32),
                pltpu.VMEM((POINTS, wide), jnp.float32),
                pltpu.VMEM((slots, POINTS, wide), jnp.bfloat16),
                pltpu.VMEM((wide, plan.chip_frames), jnp.bfloat16),
                pltpu.VMEM((wide, plan.width), jnp.float32),
            ],
        ),
        out_shape=[
            jax.ShapeDtypeStruct((bt, plan.ext, wide), jnp.float32),
            jax.ShapeDtypeStruct((bt, x_rows, wide), jnp.bfloat16),
            jax.ShapeDtypeStruct((LANES, plan.width), kind),
            jax.ShapeDtypeStruct((LANES, plan.width), kind),
        ],
        compiler_params=pltpu.CompilerParams(vmem_limit_bytes=VMEM_LIMIT),
        cost_estimate=cost(6.0),
        name="conv",
    )(info, x, x, xp, xp, xa, xa, xb, xb, kernel, kernel, gain, gain, bias, bias,
      direct, inverse, t_conv, g, gp)


def back_body(plan, steps, sources, info, *refs):
    pairs = len(steps)
    mg_ref = refs[0]
    k_refs, gain_refs, bias_refs = (
        refs[1 + 2 * pairs * i : 1 + 2 * pairs * (i + 1)] for i in range(3)
    )
    refs = refs[1 + 6 * pairs :]
    conv_refs, x_refs, w_refs = refs[:pairs], refs[pairs : 2 * pairs], refs[2 * pairs : -27]
    (own_ref, send_ref, stat_ref, weight, mg, conv_buf, x_buf, ag_first, ag_second, gs, tail,
     spec, xspec, taps, cross, parts, os, flat, w_sem, c_sem, x_sem, g_sem) = refs[-22:]
    direct, segment, inverse, t_ref, lag_ref = refs[-27:-22]
    core, offset, side_y = info[0], info[1], info[2]
    f, xh, gh, cf, ext = plan.frames, plan.xhalo, plan.ghalo, plan.chip_frames, plan.ext
    each, count = plan.back_windows
    turn = pl.program_id(0)

    def weight_copies(pair):
        made = []
        for n, (array, part, target, begin, rows) in enumerate(sources[pair]):
            first, into = begin, target * LANES
            if part is not None:
                into = pl.multiple_of(target * LANES + (side_y + part) % 2 * rows, rows)
            made.append(
                pltpu.make_async_copy(
                    w_refs[array].at[pl.ds(first, rows), :],
                    weight.at[pair, pl.ds(into, rows), :],
                    w_sem.at[pair, n],
                )
            )
        return made

    def frame_copies(pair):
        return [
            pltpu.make_async_copy(conv_refs[pair].at[i], conv_buf.at[pair, i], c_sem.at[pair, i])
            for i in range(plan.batches)
        ] + [
            pltpu.make_async_copy(x_refs[pair].at[i], x_buf.at[pair, i], x_sem.at[pair, i])
            for i in range(plan.batches)
        ]

    def grad_copy(b):
        return pltpu.make_async_copy(mg_ref.at[b], mg.at[b], g_sem.at[b])

    def act_grad(pair, b):
        return lax.dot_general(
            mg[b], weight[pair], (((1,), (1,)), ((), ())), preferred_element_type=jnp.float32
        )

    @pl.when(turn == 0)
    def _():
        for copy in weight_copies(0) + [grad_copy(0)] + frame_copies(0) + [grad_copy(1)]:
            copy.start()
        for pair in range(1, pairs):
            for copy in weight_copies(pair) + frame_copies(pair):
                copy.start()
        for b in range(plan.batches):
            gs[b, ext:, :] = jnp.zeros((gs.shape[1] - ext, 2 * LANES), jnp.bfloat16)
            tail[b] = jnp.zeros(tail.shape[1:], tail.dtype)
        for copy in weight_copies(0) + [grad_copy(0)]:
            copy.wait()
        ag_first[...] = act_grad(0, 0)
        for copy in frame_copies(0) + [grad_copy(1)]:
            copy.wait()

    for pair in range(pairs):

        @pl.when(turn == pair)
        def _():
            taps[...] = taps_spectrum(t_ref, k_refs[2 * pair : 2 * pair + 2])
            for row, pick in ((0, gain_refs), (8, bias_refs)):
                for side in range(2):
                    lanes = slice(side * LANES, (side + 1) * LANES)
                    flat[row : row + 8, lanes] = jnp.broadcast_to(
                        pick[2 * pair + side][...], (8, LANES)
                    )
            if pair > 0:
                for copy in frame_copies(pair):
                    copy.wait()
            if pair + 1 < pairs:
                for copy in weight_copies(pair + 1):
                    copy.wait()

    gain, bias = flat[:1, :], flat[8:9, :]
    last_rows = cf - (count - 1) * each
    fold = lambda v: jnp.sum(v.reshape(STEP // 8, 8, 2 * LANES), axis=0)
    gain_sum = jnp.zeros((8, 2 * LANES), jnp.float32)
    bias_sum = jnp.zeros((8, 2 * LANES), jnp.float32)
    for b in range(plan.batches):
        live = info[3 + b]
        here, ahead = (ag_first, ag_second) if b == 0 else (ag_second, ag_first)
        following = turn if b == 0 else jnp.minimum(turn + 1, pairs - 1)
        ahead[...] = act_grad(following, 1 - b)
        for j in range(count):
            begin = xh + j * each
            if j < count - 1:
                window = x_buf[turn, b, begin : begin + POINTS, :]
            else:
                tail[b, :last_rows, :] = x_buf[turn, b, begin : begin + last_rows, :]
                window = tail[b]
            xspec[b * count + j] = to_spectrum(segment, window)
        for row in range(0, ext, STEP):
            conv = conv_buf[turn, b, row : row + STEP, :]
            pre = gain * conv + bias
            sig = sigmoid(pre)
            value = here[row : row + STEP, :] * sig * (1.0 + pre * (1.0 - sig))
            gs[b, row : row + STEP, :] = (value * gain).astype(jnp.bfloat16)
            if gh <= row < gh + cf:
                gain_sum = gain_sum + fold(value * conv)
                bias_sum = bias_sum + fold(value)
        for j in range(count):
            spec[b * count + j] = to_spectrum(direct, gs[b, j * each : j * each + POINTS, :])
        for j in range(count):
            slot = b * count + j
            spectral_product(spec, taps, parts, slot)
            rows = min(each, cf - j * each)
            value = from_spectrum(inverse, rows, parts, slot)
            position = offset + j * each + lax.broadcasted_iota(jnp.int32, value.shape, 0)
            os[b, j * each : j * each + rows, :] = jnp.where(
                position < live, value, 0.0
            ).astype(jnp.bfloat16)

    for row in range(0, HALF, STEP):
        up, down = slice(row, row + STEP), slice(HALF + row, HALF + row + STEP)
        total_r = total_i = jnp.zeros((STEP, 2 * LANES), jnp.float32)
        for j in range(plan.batches * count):
            re, im, xr, xi = spec[j, up, :], spec[j, down, :], xspec[j, up, :], xspec[j, down, :]
            total_r = total_r + (re * xr + im * xi)
            total_i = total_i + (im * xr - re * xi)
        cross[up, :] = total_r
        cross[down, :] = total_i

    @pl.when(core == 0)
    def _():
        own_ref[0] = os[:, :f]
        send_ref[0] = os[:, f:]

    @pl.when(core != 0)
    def _():
        own_ref[0] = os[:, f:]
        send_ref[0] = os[:, :f]

    high, low = split(cross[...])
    dot = functools.partial(jnp.dot, preferred_element_type=jnp.float32)
    stat_ref[0, : plan.tap_rows] = (
        dot(lag_ref[0], high) + dot(lag_ref[1], high) + dot(lag_ref[0], low)
    )
    total = [jnp.sum(value, axis=0, keepdims=True) for value in (gain_sum, bias_sum)]
    pad = jnp.zeros((plan.stat_rows - plan.tap_rows - 2, 2 * LANES), jnp.float32)
    stat_ref[0, plan.tap_rows :] = jnp.concatenate(total + [pad], axis=0)


def back_call(plan, steps, info, mg, sources, arrays, convs, xs, kernel, gain, bias, consts):
    bt, pairs = plan.batches, len(steps)
    direct, inverse, _, t_back, lags, segment = consts
    wide = 2 * LANES
    slots = bt * plan.back_windows[1]
    any_space = pl.BlockSpec(memory_space=pl.ANY)

    def by_block(shape):
        return [
            pl.BlockSpec(
                shape, lambda p, info, at=plan.block_slot(step, side): (0, info[at]),
                pipeline_mode=pl.Buffered(1),
            )
            for step in steps for side in range(2)
        ]

    frames = (bt, plan.frames, wide)
    each = pl.BlockSpec((1,) + frames, lambda p, info: (p, 0, 0, 0))
    most = max(len(source) for source in sources)
    return pl.pallas_call(
        functools.partial(back_body, plan, steps, sources),
        grid_spec=pltpu.PrefetchScalarGridSpec(
            num_scalar_prefetch=1,
            grid=(pairs,),
            in_specs=[any_space]
            + by_block((plan.tap_rows, LANES))
            + by_block((1, LANES))
            + by_block((1, LANES))
            + [any_space] * (2 * pairs + len(arrays))
            + [whole(c) for c in (direct, segment, inverse, t_back, lags)],
            out_specs=[
                each,
                each,
                pl.BlockSpec((1, plan.stat_rows, wide), lambda p, info: (p, 0, 0)),
            ],
            scratch_shapes=[
                pltpu.VMEM((pairs, wide, plan.width), jnp.bfloat16),
                pltpu.VMEM((bt, plan.ext, plan.width), jnp.bfloat16),
                pltpu.VMEM((pairs, bt, plan.ext, wide), jnp.float32),
                pltpu.VMEM((pairs, bt, xs[0].shape[1], wide), jnp.bfloat16),
                pltpu.VMEM((plan.ext, wide), jnp.float32),
                pltpu.VMEM((plan.ext, wide), jnp.float32),
                pltpu.VMEM((bt, plan.window_rows(plan.back_windows), wide), jnp.bfloat16),
                pltpu.VMEM((bt, POINTS, wide), jnp.bfloat16),
                pltpu.VMEM((slots, POINTS, wide), jnp.float32),
                pltpu.VMEM((slots, POINTS, wide), jnp.float32),
                pltpu.VMEM((POINTS, wide), jnp.float32),
                pltpu.VMEM((POINTS, wide), jnp.float32),
                pltpu.VMEM((slots, POINTS, wide), jnp.bfloat16),
                pltpu.VMEM((bt, plan.chip_frames, wide), jnp.bfloat16),
                pltpu.VMEM((16, wide), jnp.float32),
                pltpu.SemaphoreType.DMA((pairs, most)),
                pltpu.SemaphoreType.DMA((pairs, bt)),
                pltpu.SemaphoreType.DMA((pairs, bt)),
                pltpu.SemaphoreType.DMA((bt,)),
            ],
        ),
        out_shape=[
            jax.ShapeDtypeStruct((pairs,) + frames, jnp.bfloat16),
            jax.ShapeDtypeStruct((pairs,) + frames, jnp.bfloat16),
            jax.ShapeDtypeStruct((pairs, plan.stat_rows, wide), jnp.float32),
        ],
        compiler_params=pltpu.CompilerParams(vmem_limit_bytes=VMEM_LIMIT),
        cost_estimate=cost(6.0 * pairs),
        name="back",
    )(info, mg, *[kernel] * 2 * pairs, *[gain] * 2 * pairs, *[bias] * 2 * pairs,
      *convs, *xs, *arrays, direct, segment, inverse, t_back, lags)


def place_body(plan, calls, info, *refs):
    out_ref = refs[-1]
    for i, ref in enumerate(refs[:-1]):
        for turn, step in enumerate(calls[i // 2]):
            for side in range(2):
                block = info[plan.block_slot(step, side)]
                if i % 2:
                    block = block + 1 - 2 * info[0]
                column = pl.multiple_of(block * LANES, LANES)
                lanes = slice(side * LANES, (side + 1) * LANES)
                out_ref[:, :, pl.ds(column, LANES)] = ref[turn, :, :, lanes]


def place_call(plan, calls, info, arrays):
    shape = (plan.batches, plan.frames, plan.width)
    return pl.pallas_call(
        functools.partial(place_body, plan, calls),
        grid_spec=pltpu.PrefetchScalarGridSpec(
            num_scalar_prefetch=1,
            grid=(1,),
            in_specs=[whole(array) for array in arrays],
            out_specs=pl.BlockSpec(shape, lambda g, info: (0, 0, 0)),
        ),
        out_shape=jax.ShapeDtypeStruct(shape, jnp.bfloat16),
        compiler_params=pltpu.CompilerParams(vmem_limit_bytes=VMEM_LIMIT),
        cost_estimate=cost(3.0),
        name="place",
    )(info, *arrays)


def deal_body(plan, calls, info, *refs):
    out_ref = refs[-1]
    for steps, ref in zip(calls, refs[:-1]):
        for turn, step in enumerate(steps):
            for side in range(2):
                chip = info[plan.block_slot(step, side)] // CORES
                out_ref[chip] = ref[turn, :, side * LANES : (side + 1) * LANES]


def deal_call(plan, calls, info, arrays):
    shape = (plan.chips, plan.stat_rows, LANES)
    return pl.pallas_call(
        functools.partial(deal_body, plan, calls),
        grid_spec=pltpu.PrefetchScalarGridSpec(
            num_scalar_prefetch=1,
            grid=(1,),
            in_specs=[whole(array) for array in arrays],
            out_specs=pl.BlockSpec(shape, lambda g, info: (0, 0, 0)),
        ),
        out_shape=jax.ShapeDtypeStruct(shape, jnp.float32),
        cost_estimate=cost(1.0),
        name="deal",
    )(info, *arrays)


def edge_body(plan, x_first, x_last, g_first, g_last, near_ref, far_ref, g_ref):
    core = lax.axis_index("shard") % CORES

    def take(owner, x_ref, grad_ref):
        for i in range(plan.chips):
            for out, parity in ((near_ref, 1 - owner), (far_ref, owner)):
                column = (CORES * i + parity) * LANES
                out[:, :, i * LANES : (i + 1) * LANES] = x_ref[:, :, column : column + LANES]
        g_ref[...] = grad_ref[...]

    pl.when(core == 0)(lambda: take(0, x_first, g_first))
    pl.when(core != 0)(lambda: take(1, x_last, g_last))


def edge_call(plan, x, g):
    def spec(rows, first):
        shape = (plan.batches, rows, plan.width)
        block = 0 if first else plan.frames // rows - 1
        return pl.BlockSpec(shape, lambda i: (0, block, 0))

    xh, gh = plan.xhalo, plan.ghalo
    half = (plan.batches, xh, plan.width // CORES)
    shapes = [half, half, (plan.batches, gh, plan.width)]
    return pl.pallas_call(
        functools.partial(edge_body, plan),
        grid=(1,),
        in_specs=[spec(xh, True), spec(xh, False), spec(gh, True), spec(gh, False)],
        out_specs=[pl.BlockSpec(shape, lambda i: (0, 0, 0)) for shape in shapes],
        out_shape=[jax.ShapeDtypeStruct(shape, jnp.bfloat16) for shape in shapes],
        cost_estimate=cost(1.0),
        name="edge",
    )(x, x, g, g)


def assemble_body(plan, halo, info, own_ref, other_ref, near_ref, far_ref, out_ref):
    core, offset, live = info[0], info[1], info[3 + pl.program_id(0)]
    f = plan.frames

    def put(row, ref):
        for part in range(0, ref.shape[1], STEP):
            position = lax.broadcasted_iota(jnp.int32, (STEP, LANES), 0) + (
                offset - halo + row + part
            )
            keep = jnp.where(position < live, 1.0, 0.0).astype(jnp.bfloat16)
            for i in range(plan.count):
                lanes = slice(i * LANES, (i + 1) * LANES)
                out_ref[0, row + part : row + part + STEP, lanes] = (
                    ref[0, part : part + STEP, lanes] * keep
                )

    @pl.when(core == 0)
    def _():
        put(0, near_ref)
        put(halo, own_ref)
        put(halo + f, other_ref)
        put(halo + 2 * f, far_ref)

    @pl.when(core != 0)
    def _():
        put(0, far_ref)
        put(halo, other_ref)
        put(halo + f, own_ref)
        put(halo + 2 * f, near_ref)


def assemble_call(plan, info, own, other, near, far):
    halo = near.shape[1]
    spec = lambda n: pl.BlockSpec((1, n, plan.width), lambda b, info: (b, 0, 0))
    return pl.pallas_call(
        functools.partial(assemble_body, plan, halo),
        grid_spec=pltpu.PrefetchScalarGridSpec(
            num_scalar_prefetch=1,
            grid=(plan.batches,),
            in_specs=[spec(plan.frames), spec(plan.frames), spec(halo), spec(halo)],
            out_specs=spec(plan.ext),
        ),
        out_shape=jax.ShapeDtypeStruct((plan.batches, plan.ext, plan.width), jnp.bfloat16),
        compiler_params=pltpu.CompilerParams(vmem_limit_bytes=VMEM_LIMIT),
        cost_estimate=cost(5.0),
        name="assemble",
    )(info, own, other, near, far)


def after(value, *others):
    return lax.optimization_barrier((value, *others))[0]


def ring_shards(plan, grad_out, saved_input, lengths, kernel, gain, bias, proj_weight):
    index = lax.axis_index("shard")
    group = lax.axis_index("groups")
    core, chip = index % CORES, index // CORES
    place = plan.position_of(chip)
    forward, backward = plan.ring()
    offset = chip * plan.chip_frames
    scale = lax.rsqrt(jnp.sum(lengths).astype(jnp.float32))
    pairs = plan.pairs
    far = jnp.asarray([d for pair in pairs for d in pair], jnp.int32)
    owned = CORES * plan.chip_at((place + far + plan.chips) % plan.chips) + core
    info = jnp.concatenate([jnp.stack([core, offset, group]), lengths, owned]).astype(jnp.int32)
    gain2, bias2 = gain.reshape(1, -1), bias.reshape(1, -1)
    taps = jnp.pad(kernel, ((0, plan.tap_rows - plan.taps), (0, 0)))
    consts = [jnp.asarray(c) for c in transforms(plan)]

    x_near, x_far, g_edge = edge_call(plan, saved_input, grad_out)
    xa = lax.ppermute(x_near, "shard", plan.edges())
    xb = lax.ppermute(x_far, "shard", plan.edges_like())
    xp = lax.ppermute(saved_input, "shard", plan.partners())
    mgp = lax.ppermute(grad_out, "shard", plan.partners())

    halved = plan.weight_parts == 2
    piece = LANES // 2
    around = {}
    going = [proj_weight] * 2
    if halved:
        going = [lax.dynamic_slice_in_dim(proj_weight, group * piece, piece, 0)] * 2
    xa, xb, taps, info = lax.optimization_barrier((xa, xb, taps, info))

    def weight_round(step):
        going[0] = lax.ppermute(going[0], "shard", forward)
        around[-step] = going[0]
        if step < plan.rounds:
            going[1] = lax.ppermute(going[1], "shard", backward)
            around[step] = going[1]
        else:
            around[step] = around.pop(-step)

    convs, xs, products = [], [], []

    def conv_step(step, order):
        conv, x, *product = conv_call(
            plan, step, order, saved_input, xp, xa, xb, grad_out,
            mgp, taps, gain2, bias2, consts, jnp.bfloat16 if step == 0 else jnp.float32,
        )
        convs.append(conv)
        xs.append(x)
        products.append(product)

    def sum_round(step, send, *behind):
        received = (
            lax.ppermute(send[0], "shard", forward), lax.ppermute(send[1], "shard", backward)
        )
        kinds = (jnp.bfloat16, jnp.bfloat16 if step < plan.rounds - 1 else jnp.float32)
        own = lax.optimization_barrier((*products[step], *received, *behind))[:2]
        return [
            (product + value.astype(jnp.float32)).astype(kind)
            for product, value, kind in zip(own, received, kinds)
        ]

    def wait_for(value):
        going[:] = lax.optimization_barrier((*going, value))[:2]

    weight_round(1)
    conv_step(0, info)
    g_edge = after(g_edge, products[0][0])
    ga = lax.ppermute(g_edge, "shard", plan.edges())
    gb = lax.ppermute(g_edge, "shard", plan.edges_like())
    wait_for(products[0][0])
    weight_round(2)
    conv_step(1, after(info, products[0][0]))
    wait_for(products[1][0])
    weight_round(3)
    mg = assemble_call(plan, after(info, products[1][0]), grad_out, mgp, ga, gb)
    wait_for(mg)
    weight_round(4)
    send = sum_round(1, products[0], mg)
    conv_step(2, after(info, products[1][0], *send, mg))
    conv_step(3, after(info, products[2][0]))
    send = sum_round(2, send, products[3][0])

    arrays = [proj_weight]
    source = {0: [(0, None, 0, LANES)]}

    def keep(array):
        arrays.append(array)
        return len(arrays) - 1

    swap = [
        (g * plan.count + s, (1 - g) * plan.count + s) for g in range(2) for s in range(plan.count)
    ]
    for distances in ([1, -1], [2, -2], [3, -3, 4]):
        if not halved:
            for d in distances:
                source[d] = [(keep(around[d]), None, 0, LANES)]
            continue
        swapped = keep(
            lax.ppermute(
                jnp.concatenate([around[d] for d in distances], 0),
                ("groups", "shard"), swap,
            )
        )
        for i, d in enumerate(distances):
            source[d] = [(keep(around[d]), 0, 0, piece), (swapped, 1, i * piece, piece)]

    calls = [(3, 2), (1, 0)]
    pieces, stats = [], []
    for steps in calls:
        if steps == calls[-1]:
            send = sum_round(3, send, pieces[0])
        order = after(info, products[-1][0], *send)
        used = sorted({a[0] for step in steps for d in pairs[step] for a in source[d]})
        sources = [
            [
                (used.index(array), part, block, begin, rows)
                for block, d in enumerate(pairs[step])
                for array, part, begin, rows in source[d]
            ]
            for step in steps
        ]
        own, given, stat = back_call(
            plan, steps, order, mg, sources, [arrays[i] for i in used],
            [convs[step] for step in steps], [xs[step] for step in steps],
            taps, gain2, bias2, consts,
        )
        stats.append(stat)
        pieces += [own, lax.ppermute(given, "shard", plan.partners())]
    recv_f = after(lax.ppermute(send[0], "shard", forward), stats[-1])
    proj_grad = (send[1] + recv_f.astype(jnp.float32)) * scale
    dealt = deal_call(plan, calls, info, stats)
    groups = [[CORES * p + c for p in range(plan.chips)] for c in range(CORES)]
    shares = lax.all_to_all(dealt, "shard", 0, 0, axis_index_groups=groups)
    full = place_call(plan, calls, after(info, dealt), pieces)
    summed = jnp.sum(after(shares, full, proj_grad), axis=0) * scale
    return (
        full, proj_grad, summed[: plan.taps], summed[plan.tap_rows : plan.tap_rows + 2]
    )


def shards(count, group_count, grad_out, saved_input, lengths, kernel, gain, bias, proj_weight):
    batches, frames, model_width = grad_out.shape
    plan = Plan(count, group_count, batches, frames, model_width, kernel.shape[0])
    args = (grad_out, saved_input, lengths, kernel, gain, bias, proj_weight)
    return ring_shards(plan, *args) if plan.usable() else plain_shards(*args)


def solution(mesh):
    placed = (
        P("groups", "shard", None),
        P("groups", "shard", None),
        P("groups"),
        P(),
        P(),
        P(),
        P("shard", None),
    )

    def body(*args):
        return shards(mesh.shape["shard"], mesh.shape["groups"], *args)

    return jax.shard_map(
        body,
        mesh=mesh,
        in_specs=placed,
        out_specs=(
            P("groups", "shard", None),
            P(("groups", "shard"), None),
            P("groups", "shard"),
            P("groups", "shard"),
        ),
        check_vma=False,
    )
```

```python
import functools

import jax
import jax.numpy as jnp
import numpy as np
from jax import lax
from jax.experimental import pallas as pl
from jax.experimental.pallas import tpu as pltpu
from jax.sharding import PartitionSpec as P


LANES = 128
CORES = 2
VMEM_LIMIT = 56 * 1024 * 1024
POINTS = 256


def cost(micros):
    return pl.CostEstimate(flops=0, transcendentals=0, bytes_accessed=int(micros * 3.6e6))


def extended(block, width):
    count = lax.axis_size("shard")
    forward = [(i, i + 1) for i in range(count - 1)]
    backward = [(target, source) for source, target in forward]
    low = lax.ppermute(block[:, block.shape[1] - width :], "shard", forward)
    high = lax.ppermute(block[:, :width], "shard", backward)
    return jnp.concatenate([low, block, high], axis=1)


def frame_mask(lengths, offset, count):
    position = offset + jnp.arange(count, dtype=jnp.int32)
    return (position[None, :] < lengths[:, None])[:, :, None]


def plain_shards(grad_out, saved_input, lengths, kernel, gain, bias, proj_weight):
    batches, frames, model_width = grad_out.shape
    tap_count = kernel.shape[0]
    half_span = (tap_count - 1) // 2
    offset = lax.axis_index("shard") * frames
    norm_scale = lax.rsqrt(jnp.sum(lengths).astype(jnp.float32))
    own_mask = frame_mask(lengths, offset, frames)
    masked_in = jnp.where(own_mask, saved_input, jnp.zeros_like(saved_input))
    masked_grad = jnp.where(own_mask, grad_out, jnp.zeros_like(grad_out))
    in_ext = extended(masked_in, half_span)
    conv = jnp.zeros(grad_out.shape, jnp.float32)
    for tap in range(tap_count):
        conv = conv + kernel[tap] * in_ext[:, tap : tap + frames].astype(jnp.float32)
    pre_act = gain * conv + bias
    gate_sig = jax.nn.sigmoid(pre_act)
    activated = (pre_act * gate_sig).astype(jnp.bfloat16)
    rows = masked_grad.reshape(batches * frames, model_width)
    weight = lax.all_gather(proj_weight, "shard", axis=0, tiled=True)
    act_grad = lax.dot_general(
        rows, weight, (((1,), (1,)), ((), ())), preferred_element_type=jnp.float32
    ).reshape(batches, frames, model_width)
    pre_grad = act_grad * gate_sig * (1.0 + pre_act * (1.0 - gate_sig))
    conv_grad = (pre_grad * gain).astype(jnp.bfloat16)
    grad_ext = extended(conv_grad, half_span)
    back_sum = jnp.zeros(grad_out.shape, jnp.float32)
    grad_float = conv_grad.astype(jnp.float32)
    tap_rows = []
    for tap in range(tap_count):
        begin = 2 * half_span - tap
        back_sum = back_sum + kernel[tap] * grad_ext[:, begin : begin + frames].astype(jnp.float32)
        tap_rows.append(
            jnp.sum(in_ext[:, tap : tap + frames].astype(jnp.float32) * grad_float, axis=(0, 1))
        )
    input_grad = jnp.where(own_mask, back_sum, 0.0).astype(jnp.bfloat16)
    tap_rows.append(jnp.sum(pre_grad * conv, axis=(0, 1)))
    tap_rows.append(jnp.sum(pre_grad, axis=(0, 1)))
    stats = jnp.stack(tap_rows, 0) * norm_scale
    summed = lax.psum_scatter(stats, "shard", scatter_dimension=1, tiled=True)
    product = lax.dot_general(
        activated.reshape(batches * frames, model_width),
        rows,
        (((0,), (0,)), ((), ())),
        preferred_element_type=jnp.float32,
    )
    proj_grad = lax.psum_scatter(product * norm_scale, "shard", scatter_dimension=0, tiled=True)
    return (input_grad, proj_grad, summed[:tap_count], summed[tap_count:])


class Plan:
    def __init__(self, count, groups, batches, frames, model_width, tap_count):
        self.count = count
        self.chips = count // CORES
        self.rounds = self.chips // 2
        self.batches = batches
        self.frames = frames
        self.chip_frames = CORES * frames
        self.width = model_width
        self.block = model_width // count
        self.taps = tap_count
        self.half = (tap_count - 1) // 2
        self.ghalo = -(-self.half // 16) * 16
        self.xhalo = 2 * self.ghalo
        self.ext = self.chip_frames + 2 * self.ghalo
        self.xext = self.chip_frames + 2 * self.xhalo
        self.tap_rows = -(-tap_count // 16) * 16
        self.stat_rows = self.tap_rows + 8
        self.weight_parts = 2 if groups == 2 else 1
        self.pairs = [(h, 1 - h) for h in range(self.rounds, 0, -1)]
        self.conv_windows = windows(self.ext, self.xhalo - self.ghalo - self.half + tap_count)
        self.back_windows = windows(self.chip_frames, self.ghalo + self.half + 1)

    def window_rows(self, found):
        return found[0] * (found[1] - 1) + POINTS

    def block_slot(self, step, side):
        return 3 + self.batches + 2 * step + side

    def usable(self):
        return (
            self.count % (2 * CORES) == 0
            and self.block == LANES
            and self.block * self.count == self.width
            and self.frames % 128 == 0
            and self.frames >= self.xhalo
            and self.taps % 2 == 1
            and 4 * self.ghalo <= POINTS // 2
            and self.window_rows(self.conv_windows) >= self.xext
            and self.window_rows(self.back_windows) >= self.ext
            and self.window_rows(self.conv_windows)
            >= self.xhalo + self.window_rows(self.back_windows) - self.back_windows[0]
            and self.chips == 8
            and self.batches == 2
        )

    def chip_at(self, position):
        half = self.chips // 2
        return jnp.where(position < half, 2 * position, 2 * (self.chips - 1 - position) + 1)

    def position_of(self, chip):
        return jnp.where(chip % 2 == 0, chip // 2, self.chips - 1 - chip // 2)

    def ring(self):
        half = self.chips // 2
        order = [2 * i for i in range(half)] + [2 * i + 1 for i in reversed(range(half))]
        forward = []
        for core in range(CORES):
            for i in range(self.chips):
                source, target = order[i], order[(i + 1) % self.chips]
                forward.append((CORES * source + core, CORES * target + core))
        return forward, [(t, s) for s, t in forward]

    def edges(self):
        pairs = []
        for chip in range(self.chips - 1):
            last, first = CORES * chip + 1, CORES * (chip + 1)
            pairs += [(last, first), (first, last)]
        return pairs

    def edges_like(self):
        pairs = []
        for chip in range(self.chips - 1):
            pairs.append((CORES * chip + 1, CORES * (chip + 1) + 1))
            pairs.append((CORES * (chip + 1), CORES * chip))
        return pairs

    def partners(self):
        return [(s, s ^ 1) for s in range(self.count)]


def sigmoid(value):
    return 0.5 * jnp.tanh(0.5 * value) + 0.5


def split(value):
    high = value.astype(jnp.bfloat16)
    return high, (value - high.astype(jnp.float32)).astype(jnp.bfloat16)


def split_matrix(matrix):
    high = matrix.astype(jnp.bfloat16)
    return high, (matrix - high.astype(np.float64)).astype(jnp.bfloat16)


def transforms(plan):
    time = np.arange(POINTS)
    theta = np.pi * (2 * np.arange(POINTS // 2) + 1) / POINTS
    angle = theta[:, None] * time[None, :]
    direct = np.concatenate([np.cos(angle), -np.sin(angle)], 0)
    inverse = direct.T * (2.0 / POINTS)

    def spectrum(lags):
        phase = theta[:, None] * lags[None, :]
        matrix = np.concatenate([np.cos(phase), np.sin(phase)], 0)
        return np.pad(matrix, ((0, 0), (0, plan.tap_rows - plan.taps)))

    taps = np.arange(plan.taps)
    back_lags = plan.ghalo + plan.half - taps
    lag_rows = np.pad(inverse[back_lags], ((0, plan.tap_rows - plan.taps), (0, 0)))
    half = lambda m: m.astype(jnp.bfloat16)
    conv_lags = plan.xhalo - plan.ghalo - plan.half + taps
    return (
        half(direct),
        half(inverse),
        np.stack(split_matrix(spectrum(conv_lags))),
        np.stack(split_matrix(spectrum(back_lags))),
        np.stack(split_matrix(lag_rows)),
        half(direct * (time < plan.back_windows[0])),
    )


def taps_spectrum(t_ref, k_ref):
    high, low = split(jnp.concatenate([k_ref[0][...], k_ref[1][...]], axis=1))
    dot = functools.partial(jnp.dot, preferred_element_type=jnp.float32)
    return dot(t_ref[0], high) + dot(t_ref[1], high) + dot(t_ref[0], low)


def to_spectrum(direct_ref, window):
    return jnp.dot(direct_ref[...], window, preferred_element_type=jnp.float32)


def from_spectrum(inverse_ref, rows, parts, slot):
    return jnp.dot(inverse_ref[:rows, :], parts[slot], preferred_element_type=jnp.float32)


def windows(rows_out, reach):
    count = -(-rows_out // ((POINTS - reach) // 16 * 16))
    return -(-rows_out // count // 16) * 16, count


STEP = 16
HALF = POINTS // 2


def spectral_product(spec, taps, parts, slot):
    for row in range(0, HALF, STEP):
        up, down = slice(row, row + STEP), slice(HALF + row, HALF + row + STEP)
        re, im, kr, ks = spec[slot, up, :], spec[slot, down, :], taps[up, :], taps[down, :]
        parts[slot, up, :] = (re * kr - im * ks).astype(jnp.bfloat16)
        parts[slot, down, :] = (re * ks + im * kr).astype(jnp.bfloat16)


def conv_body(plan, info, *refs):
    own_x, other_x, near_x, far_x, k_ref, gain_ref, bias_ref = (
        refs[2 * i : 2 * i + 2] for i in range(7)
    )
    direct, inverse, t_ref, own_g, other_g = refs[14:19]
    conv_ref, x_ref, out_f, out_b, spec, taps, parts, act, acc = refs[19:]
    each, count = plan.conv_windows
    f, xh, gh, cf = plan.frames, plan.xhalo, plan.ghalo, plan.chip_frames
    b = pl.program_id(0)
    core, offset, live = info[0], info[1], info[3 + b]

    @pl.when(b == 0)
    def _():
        taps[...] = taps_spectrum(t_ref, k_ref)

    def put(row, pair):
        for part in range(0, pair[0].shape[1], STEP):
            position = lax.broadcasted_iota(jnp.int32, (STEP, LANES), 0) + (
                offset - xh + row + part
            )
            keep = jnp.where(position < live, 1.0, 0.0).astype(jnp.bfloat16)
            for side in range(2):
                lanes = slice(side * LANES, (side + 1) * LANES)
                x_ref[0, row + part : row + part + STEP, lanes] = (
                    pair[side][0, part : part + STEP, :] * keep
                )

    @pl.when(core == 0)
    def _():
        put(0, near_x)
        put(xh, own_x)
        put(xh + f, other_x)
        put(xh + 2 * f, far_x)

    @pl.when(core != 0)
    def _():
        put(0, far_x)
        put(xh, other_x)
        put(xh + f, own_x)
        put(xh + 2 * f, near_x)

    x_ref[0, plan.xext :, :] = jnp.zeros((x_ref.shape[1] - plan.xext, 2 * LANES), jnp.bfloat16)

    for j in range(count):
        spec[j] = to_spectrum(direct, x_ref[0, j * each : j * each + POINTS, :])
    for j in range(count):
        spectral_product(spec, taps, parts, j)
        rows = min(each, plan.ext - j * each)
        conv_ref[0, j * each : j * each + rows, :] = from_spectrum(inverse, rows, parts, j)

    for i in range(cf // LANES):
        for side in range(2):
            lanes = slice(side * LANES, (side + 1) * LANES)
            begin = gh + i * LANES
            conv = conv_ref[0, begin : begin + LANES, lanes]
            pre = gain_ref[side][...] * conv + bias_ref[side][...]
            position = lax.broadcasted_iota(jnp.int32, (LANES, LANES), 0) + (offset + i * LANES)
            value = jnp.where(position < live, pre * sigmoid(pre), 0.0)
            act[lanes, i * LANES : (i + 1) * LANES] = value.T.astype(jnp.bfloat16)

    own = pl.multiple_of(core * f, f)
    other = pl.multiple_of((1 - core) * f, f)

    def product(columns):
        dot = functools.partial(jnp.dot, preferred_element_type=jnp.float32)
        return dot(act[:, pl.ds(own, f)], own_g[0, :, columns]) + dot(
            act[:, pl.ds(other, f)], other_g[0, :, columns]
        )

    tiles = [slice(c, c + 2 * LANES) for c in range(0, plan.width, 2 * LANES)]

    @pl.when(b == 0)
    def _():
        for columns in tiles:
            acc[:, columns] = product(columns)

    @pl.when(b != 0)
    def _():
        for columns in tiles:
            total = acc[:, columns] + product(columns)
            if plan.batches > 2:
                acc[:, columns] = total
            out_f[:, columns] = total[:LANES].astype(out_f.dtype)
            out_b[:, columns] = total[LANES:].astype(out_b.dtype)


def pair_specs(plan, step, shape, index):
    return [
        pl.BlockSpec(
            shape, lambda b, info, at=plan.block_slot(step, side): index(b, info[at])
        )
        for side in range(2)
    ]


def whole(array):
    return pl.BlockSpec(
        array.shape, lambda *_: (0,) * array.ndim, pipeline_mode=pl.Buffered(1)
    )


def conv_call(plan, step, info, x, xp, xa, xb, g, gp, kernel, gain, bias, consts, kind):
    bt = plan.batches
    flat = lambda b, block: (0, block)
    fixed = lambda b, info: (0, 0)
    direct, inverse, t_conv = consts[:3]
    wide = 2 * LANES
    slots = plan.conv_windows[1]
    specs = functools.partial(pair_specs, plan, step)
    frames, halo = (1, plan.frames, LANES), (1, plan.xhalo, LANES)
    by_batch = lambda b, block: (b, 0, block)
    by_chip = lambda b, block: (b, 0, block // CORES)
    x_rows = plan.window_rows(plan.conv_windows)
    return pl.pallas_call(
        functools.partial(conv_body, plan),
        grid_spec=pltpu.PrefetchScalarGridSpec(
            num_scalar_prefetch=1,
            grid=(bt,),
            in_specs=specs(frames, by_batch)
            + specs(frames, by_batch)
            + specs(halo, by_chip)
            + specs(halo, by_chip)
            + specs((plan.tap_rows, LANES), flat)
            + specs((1, LANES), flat)
            + specs((1, LANES), flat)
            + [whole(direct), whole(inverse), whole(t_conv)]
            + [pl.BlockSpec((1, plan.frames, plan.width), lambda b, info: (b, 0, 0))] * 2,
            out_specs=[
                pl.BlockSpec((1, plan.ext, wide), lambda b, info: (b, 0, 0)),
                pl.BlockSpec((1, x_rows, wide), lambda b, info: (b, 0, 0)),
                pl.BlockSpec((LANES, plan.width), fixed),
                pl.BlockSpec((LANES, plan.width), fixed),
            ],
            scratch_shapes=[
                pltpu.VMEM((slots, POINTS, wide), jnp.float32),
                pltpu.VMEM((POINTS, wide), jnp.float32),
                pltpu.VMEM((slots, POINTS, wide), jnp.bfloat16),
                pltpu.VMEM((wide, plan.chip_frames), jnp.bfloat16),
                pltpu.VMEM((wide, plan.width), jnp.float32),
            ],
        ),
        out_shape=[
            jax.ShapeDtypeStruct((bt, plan.ext, wide), jnp.float32),
            jax.ShapeDtypeStruct((bt, x_rows, wide), jnp.bfloat16),
            jax.ShapeDtypeStruct((LANES, plan.width), kind),
            jax.ShapeDtypeStruct((LANES, plan.width), kind),
        ],
        compiler_params=pltpu.CompilerParams(vmem_limit_bytes=VMEM_LIMIT),
        cost_estimate=cost(6.0),
        name="conv",
    )(info, x, x, xp, xp, xa, xa, xb, xb, kernel, kernel, gain, gain, bias, bias,
      direct, inverse, t_conv, g, gp)


def back_body(plan, steps, earlier, sources, info, *refs):
    pairs = len(steps)
    g_refs = refs[:4]
    k_refs, gain_refs, bias_refs = (
        refs[4 + 2 * pairs * i : 4 + 2 * pairs * (i + 1)] for i in range(3)
    )
    refs = refs[4 + 6 * pairs :]
    conv_refs, x_refs, w_refs = refs[:pairs], refs[pairs : 2 * pairs], refs[2 * pairs : -28]
    (own_ref, send_ref, stat_ref, weight, mg, conv_buf, x_buf, ag_first, ag_second, gs, tail,
     spec, xspec, taps, cross, parts, os, flat, w_sem, c_sem, x_sem, g_sem) = refs[-22:]
    direct, segment, inverse, t_ref, lag_ref, before_ref = refs[-28:-22]
    core, offset, side_y = info[0], info[1], info[2]
    f, xh, gh, cf, ext = plan.frames, plan.xhalo, plan.ghalo, plan.chip_frames, plan.ext
    each, count = plan.back_windows
    turn = pl.program_id(0)

    def weight_copies(pair):
        made = []
        for n, (array, part, target, begin, rows) in enumerate(sources[pair]):
            first, into = begin, target * LANES
            if part is not None:
                into = pl.multiple_of(target * LANES + (side_y + part) % 2 * rows, rows)
            made.append(
                pltpu.make_async_copy(
                    w_refs[array].at[pl.ds(first, rows), :],
                    weight.at[pair, pl.ds(into, rows), :],
                    w_sem.at[pair, n],
                )
            )
        return made

    def frame_copies(pair):
        return [
            pltpu.make_async_copy(conv_refs[pair].at[i], conv_buf.at[pair, i], c_sem.at[pair, i])
            for i in range(plan.batches)
        ] + [
            pltpu.make_async_copy(x_refs[pair].at[i], x_buf.at[pair, i], x_sem.at[pair, i])
            for i in range(plan.batches)
        ]

    def grad_copies(b):
        own, other, near, far = g_refs
        moves = []
        for ref, turned in ((own, core), (other, 1 - core)):
            moves.append((ref.at[b], pl.multiple_of(gh + turned * f, gh), f, 0, plan.width))
        width = plan.width // CORES
        for ref, turned in ((near, core), (far, 1 - core)):
            for part in range(CORES):
                piece = ref.at[b, pl.ds(xh + part * gh, gh), :]
                moves.append((piece, pl.multiple_of(turned * (gh + cf), gh), gh, part * width, width))
        return [
            pltpu.make_async_copy(
                source, mg.at[b, pl.ds(row, rows), pl.ds(column, columns)], g_sem.at[b, n]
            )
            for n, (source, row, rows, column, columns) in enumerate(moves)
        ]

    def act_grad(pair, b):
        return lax.dot_general(
            mg[b], weight[pair], (((1,), (1,)), ((), ())), preferred_element_type=jnp.float32
        )

    @pl.when(turn == 0)
    def _():
        for copy in weight_copies(0) + grad_copies(0) + frame_copies(0) + grad_copies(1):
            copy.start()
        for pair in range(1, pairs):
            for copy in weight_copies(pair) + frame_copies(pair):
                copy.start()
        for b in range(plan.batches):
            gs[b, ext:, :] = jnp.zeros((gs.shape[1] - ext, 2 * LANES), jnp.bfloat16)
            tail[b] = jnp.zeros(tail.shape[1:], tail.dtype)
        for copy in weight_copies(0) + grad_copies(0):
            copy.wait()
        ag_first[...] = act_grad(0, 0)
        for copy in frame_copies(0) + grad_copies(1):
            copy.wait()

    for pair in range(pairs):

        @pl.when(turn == pair)
        def _():
            taps[...] = taps_spectrum(t_ref, k_refs[2 * pair : 2 * pair + 2])
            for row, pick in ((0, gain_refs), (8, bias_refs)):
                for side in range(2):
                    lanes = slice(side * LANES, (side + 1) * LANES)
                    flat[row : row + 8, lanes] = jnp.broadcast_to(
                        pick[2 * pair + side][...], (8, LANES)
                    )
            if pair > 0:
                for copy in frame_copies(pair):
                    copy.wait()
            if pair + 1 < pairs:
                for copy in weight_copies(pair + 1):
                    copy.wait()

    gain, bias = flat[:1, :], flat[8:9, :]
    last_rows = cf - (count - 1) * each
    fold = lambda v: jnp.sum(v.reshape(STEP // 8, 8, 2 * LANES), axis=0)
    gain_sum = jnp.zeros((8, 2 * LANES), jnp.float32)
    bias_sum = jnp.zeros((8, 2 * LANES), jnp.float32)
    for b in range(plan.batches):
        live = info[3 + b]
        here, ahead = (ag_first, ag_second) if b == 0 else (ag_second, ag_first)
        following = turn if b == 0 else jnp.minimum(turn + 1, pairs - 1)
        ahead[...] = act_grad(following, 1 - b)
        for j in range(count):
            begin = xh + j * each
            if j < count - 1:
                window = x_buf[turn, b, begin : begin + POINTS, :]
            else:
                tail[b, :last_rows, :] = x_buf[turn, b, begin : begin + last_rows, :]
                window = tail[b]
            xspec[b * count + j] = to_spectrum(segment, window)
        for row in range(0, ext, STEP):
            conv = conv_buf[turn, b, row : row + STEP, :]
            pre = gain * conv + bias
            sig = sigmoid(pre)
            value = here[row : row + STEP, :] * sig * (1.0 + pre * (1.0 - sig))
            position = lax.broadcasted_iota(jnp.int32, value.shape, 0) + (offset - gh + row)
            value = jnp.where(position < live, value, 0.0)
            gs[b, row : row + STEP, :] = (value * gain).astype(jnp.bfloat16)
            if gh <= row < gh + cf:
                gain_sum = gain_sum + fold(value * conv)
                bias_sum = bias_sum + fold(value)
        for j in range(count):
            spec[b * count + j] = to_spectrum(direct, gs[b, j * each : j * each + POINTS, :])
        for j in range(count):
            slot = b * count + j
            spectral_product(spec, taps, parts, slot)
            rows = min(each, cf - j * each)
            value = from_spectrum(inverse, rows, parts, slot)
            position = offset + j * each + lax.broadcasted_iota(jnp.int32, value.shape, 0)
            os[b, j * each : j * each + rows, :] = jnp.where(
                position < live, value, 0.0
            ).astype(jnp.bfloat16)

    for row in range(0, HALF, STEP):
        up, down = slice(row, row + STEP), slice(HALF + row, HALF + row + STEP)
        total_r = total_i = jnp.zeros((STEP, 2 * LANES), jnp.float32)
        for j in range(plan.batches * count):
            re, im, xr, xi = spec[j, up, :], spec[j, down, :], xspec[j, up, :], xspec[j, down, :]
            total_r = total_r + (re * xr + im * xi)
            total_i = total_i + (im * xr - re * xi)
        cross[up, :] = total_r
        cross[down, :] = total_i

    @pl.when(core == 0)
    def _():
        own_ref[0] = os[:, :f]
        send_ref[0] = os[:, f:]

    @pl.when(core != 0)
    def _():
        own_ref[0] = os[:, f:]
        send_ref[0] = os[:, :f]

    high, low = split(cross[...])
    dot = functools.partial(jnp.dot, preferred_element_type=jnp.float32)
    taps_total = dot(lag_ref[0], high) + dot(lag_ref[1], high) + dot(lag_ref[0], low)
    total = [jnp.sum(value, axis=0, keepdims=True) for value in (gain_sum, bias_sum)]
    pad = jnp.zeros((plan.stat_rows - plan.tap_rows - 2, 2 * LANES), jnp.float32)
    total = jnp.concatenate([taps_total] + total + [pad], axis=0)
    if earlier is None:
        stat_ref[0] = total
        return
    for side in range(2):
        lanes = slice(side * LANES, (side + 1) * LANES)
        chip = info[plan.block_slot(steps[0], side) - 2 * turn] // CORES
        stat_ref[chip] = total[:, lanes]
        for n, step in enumerate(earlier):
            chip = info[plan.block_slot(step, side)] // CORES
            stat_ref[chip] = before_ref[n, :, lanes]


def back_call(
    plan, steps, info, grads, sources, arrays, convs, xs, kernel, gain, bias, consts, before, earlier
):
    bt, pairs = plan.batches, len(steps)
    direct, inverse, _, t_back, lags, segment = consts
    wide = 2 * LANES
    slots = bt * plan.back_windows[1]
    any_space = pl.BlockSpec(memory_space=pl.ANY)

    def by_block(shape):
        return [
            pl.BlockSpec(
                shape, lambda p, info, at=plan.block_slot(step, side): (0, info[at]),
                pipeline_mode=pl.Buffered(1),
            )
            for step in steps for side in range(2)
        ]

    frames = (bt, plan.frames, wide)
    each = pl.BlockSpec((1,) + frames, lambda p, info: (p, 0, 0, 0))
    most = max(len(source) for source in sources)
    stat_shape = (pairs, plan.stat_rows, wide)
    stat_spec = pl.BlockSpec((1, plan.stat_rows, wide), lambda p, info: (p, 0, 0))
    if before is None:
        earlier, before = None, jnp.zeros((8, LANES), jnp.float32)
    else:
        stat_shape = (plan.chips, plan.stat_rows, LANES)
        stat_spec = pl.BlockSpec(stat_shape, lambda p, info: (0, 0, 0))
    return pl.pallas_call(
        functools.partial(back_body, plan, steps, earlier, sources),
        grid_spec=pltpu.PrefetchScalarGridSpec(
            num_scalar_prefetch=1,
            grid=(pairs,),
            in_specs=[any_space] * len(grads)
            + by_block((plan.tap_rows, LANES))
            + by_block((1, LANES))
            + by_block((1, LANES))
            + [any_space] * (2 * pairs + len(arrays))
            + [whole(c) for c in (direct, segment, inverse, t_back, lags, before)],
            out_specs=[
                each,
                each,
                stat_spec,
            ],
            scratch_shapes=[
                pltpu.VMEM((pairs, wide, plan.width), jnp.bfloat16),
                pltpu.VMEM((bt, plan.ext, plan.width), jnp.bfloat16),
                pltpu.VMEM((pairs, bt, plan.ext, wide), jnp.float32),
                pltpu.VMEM((pairs, bt, xs[0].shape[1], wide), jnp.bfloat16),
                pltpu.VMEM((plan.ext, wide), jnp.float32),
                pltpu.VMEM((plan.ext, wide), jnp.float32),
                pltpu.VMEM((bt, plan.window_rows(plan.back_windows), wide), jnp.bfloat16),
                pltpu.VMEM((bt, POINTS, wide), jnp.bfloat16),
                pltpu.VMEM((slots, POINTS, wide), jnp.float32),
                pltpu.VMEM((slots, POINTS, wide), jnp.float32),
                pltpu.VMEM((POINTS, wide), jnp.float32),
                pltpu.VMEM((POINTS, wide), jnp.float32),
                pltpu.VMEM((slots, POINTS, wide), jnp.bfloat16),
                pltpu.VMEM((bt, plan.chip_frames, wide), jnp.bfloat16),
                pltpu.VMEM((16, wide), jnp.float32),
                pltpu.SemaphoreType.DMA((pairs, most)),
                pltpu.SemaphoreType.DMA((pairs, bt)),
                pltpu.SemaphoreType.DMA((pairs, bt)),
                pltpu.SemaphoreType.DMA((bt, 2 + 2 * CORES)),
            ],
        ),
        out_shape=[
            jax.ShapeDtypeStruct((pairs,) + frames, jnp.bfloat16),
            jax.ShapeDtypeStruct((pairs,) + frames, jnp.bfloat16),
            jax.ShapeDtypeStruct(stat_shape, jnp.float32),
        ],
        compiler_params=pltpu.CompilerParams(vmem_limit_bytes=VMEM_LIMIT),
        cost_estimate=cost(6.0 * pairs),
        name="back",
    )(info, *grads, *[kernel] * 2 * pairs, *[gain] * 2 * pairs, *[bias] * 2 * pairs,
      *convs, *xs, *arrays, direct, segment, inverse, t_back, lags, before)


def place_body(plan, calls, info, *refs):
    out_ref = refs[-1]
    for i, ref in enumerate(refs[:-1]):
        for turn, step in enumerate(calls[i // 2]):
            for side in range(2):
                block = info[plan.block_slot(step, side)]
                if i % 2:
                    block = block + 1 - 2 * info[0]
                column = pl.multiple_of(block * LANES, LANES)
                lanes = slice(side * LANES, (side + 1) * LANES)
                out_ref[:, :, pl.ds(column, LANES)] = ref[turn, :, :, lanes]


def place_call(plan, calls, info, arrays):
    shape = (plan.batches, plan.frames, plan.width)
    return pl.pallas_call(
        functools.partial(place_body, plan, calls),
        grid_spec=pltpu.PrefetchScalarGridSpec(
            num_scalar_prefetch=1,
            grid=(1,),
            in_specs=[whole(array) for array in arrays],
            out_specs=pl.BlockSpec(shape, lambda g, info: (0, 0, 0)),
        ),
        out_shape=jax.ShapeDtypeStruct(shape, jnp.bfloat16),
        compiler_params=pltpu.CompilerParams(vmem_limit_bytes=VMEM_LIMIT),
        cost_estimate=cost(3.0),
        name="place",
    )(info, *arrays)


def edge_body(plan, x_first, x_last, g_first, g_last, near_ref, far_ref):
    core = lax.axis_index("shard") % CORES

    def take(owner, x_ref, grad_ref):
        for i in range(plan.chips):
            for out, parity in ((near_ref, 1 - owner), (far_ref, owner)):
                column = (CORES * i + parity) * LANES
                out[:, : plan.xhalo, i * LANES : (i + 1) * LANES] = x_ref[
                    :, :, column : column + LANES
                ]
        for part in range(CORES):
            row = plan.xhalo + part * plan.ghalo
            width = plan.width // CORES
            near_ref[:, row : row + plan.ghalo, :] = grad_ref[
                :, :, part * width : (part + 1) * width
            ]

    pl.when(core == 0)(lambda: take(0, x_first, g_first))
    pl.when(core != 0)(lambda: take(1, x_last, g_last))


def edge_call(plan, x, g):
    def spec(rows, first):
        shape = (plan.batches, rows, plan.width)
        block = 0 if first else plan.frames // rows - 1
        return pl.BlockSpec(shape, lambda i: (0, block, 0))

    xh, gh = plan.xhalo, plan.ghalo
    shapes = [
        (plan.batches, rows, plan.width // CORES) for rows in (xh + CORES * gh, xh)
    ]
    return pl.pallas_call(
        functools.partial(edge_body, plan),
        grid=(1,),
        in_specs=[spec(xh, True), spec(xh, False), spec(gh, True), spec(gh, False)],
        out_specs=[pl.BlockSpec(shape, lambda i: (0, 0, 0)) for shape in shapes],
        out_shape=[jax.ShapeDtypeStruct(shape, jnp.bfloat16) for shape in shapes],
        cost_estimate=cost(1.0),
        name="edge",
    )(x, x, g, g)


def after(value, *others):
    return lax.optimization_barrier((value, *others))[0]


def ring_shards(plan, grad_out, saved_input, lengths, kernel, gain, bias, proj_weight):
    index = lax.axis_index("shard")
    group = lax.axis_index("groups")
    core, chip = index % CORES, index // CORES
    place = plan.position_of(chip)
    forward, backward = plan.ring()
    offset = chip * plan.chip_frames
    scale = lax.rsqrt(jnp.sum(lengths).astype(jnp.float32))
    pairs = plan.pairs
    far = jnp.asarray([d for pair in pairs for d in pair], jnp.int32)
    owned = CORES * plan.chip_at((place + far + plan.chips) % plan.chips) + core
    info = jnp.concatenate([jnp.stack([core, offset, group]), lengths, owned]).astype(jnp.int32)
    gain2, bias2 = gain.reshape(1, -1), bias.reshape(1, -1)
    taps = jnp.pad(kernel, ((0, plan.tap_rows - plan.taps), (0, 0)))
    consts = [jnp.asarray(c) for c in transforms(plan)]

    x_near, x_far = edge_call(plan, saved_input, grad_out)
    xa = lax.ppermute(x_near, "shard", plan.edges())
    xb = lax.ppermute(x_far, "shard", plan.edges_like())
    xp = lax.ppermute(saved_input, "shard", plan.partners())
    mgp = lax.ppermute(grad_out, "shard", plan.partners())

    halved = plan.weight_parts == 2
    piece = LANES // 2
    around = {}
    going = [proj_weight] * 2
    if halved:
        going = [lax.dynamic_slice_in_dim(proj_weight, group * piece, piece, 0)] * 2
    xa, xb, taps, info, scale = lax.optimization_barrier((xa, xb, taps, info, scale))

    def weight_round(step):
        going[0] = lax.ppermute(going[0], "shard", forward)
        around[-step] = going[0]
        if step < plan.rounds:
            going[1] = lax.ppermute(going[1], "shard", backward)
            around[step] = going[1]
        else:
            around[step] = around.pop(-step)

    convs, xs, products = [], [], []

    def conv_step(step, order):
        conv, x, *product = conv_call(
            plan, step, order, saved_input, xp, xa, xb, grad_out,
            mgp, taps, gain2, bias2, consts, jnp.bfloat16 if step == 0 else jnp.float32,
        )
        convs.append(conv)
        xs.append(x)
        products.append(product)

    def sum_round(step, send, *behind):
        received = (
            lax.ppermute(send[0], "shard", forward), lax.ppermute(send[1], "shard", backward)
        )
        kinds = (jnp.bfloat16, jnp.bfloat16 if step < plan.rounds - 1 else jnp.float32)
        own = lax.optimization_barrier((*products[step], *received, *behind))[:2]
        return [
            (product + value.astype(jnp.float32)).astype(kind)
            for product, value, kind in zip(own, received, kinds)
        ]

    def wait_for(value):
        going[:] = lax.optimization_barrier((*going, value))[:2]

    weight_round(1)
    conv_step(0, info)
    xc = lax.ppermute(after(xa, products[0][0]), "shard", plan.partners())
    wait_for(products[0][0])
    weight_round(2)
    conv_step(1, after(info, products[0][0]))
    wait_for(products[1][0])
    weight_round(3)
    conv_step(2, after(info, products[1][0]))
    wait_for(products[2][0])
    weight_round(4)
    send = sum_round(1, products[0], products[2][0])
    conv_step(3, after(info, products[2][0], *send))
    send = sum_round(2, send, products[3][0])

    arrays = [proj_weight]
    source = {0: [(0, None, 0, LANES)]}

    def keep(array):
        arrays.append(array)
        return len(arrays) - 1

    swap = [
        (g * plan.count + s, (1 - g) * plan.count + s) for g in range(2) for s in range(plan.count)
    ]
    for distances in ([1, -1], [2, -2], [3, -3, 4]):
        if not halved:
            for d in distances:
                source[d] = [(keep(around[d]), None, 0, LANES)]
            continue
        swapped = keep(
            lax.ppermute(
                jnp.concatenate([around[d] for d in distances], 0),
                ("groups", "shard"), swap,
            )
        )
        for i, d in enumerate(distances):
            source[d] = [(keep(around[d]), 0, 0, piece), (swapped, 1, i * piece, piece)]

    calls = [(3, 2), (1, 0)]
    pieces, stats = [], None
    for steps in calls:
        if steps == calls[-1]:
            send = sum_round(3, send, pieces[0])
        order = after(info, products[-1][0], *send)
        used = sorted({a[0] for step in steps for d in pairs[step] for a in source[d]})
        sources = [
            [
                (used.index(array), part, block, begin, rows)
                for block, d in enumerate(pairs[step])
                for array, part, begin, rows in source[d]
            ]
            for step in steps
        ]
        own, given, stat = back_call(
            plan, steps, order, (grad_out, mgp, xa, xc), sources, [arrays[i] for i in used],
            [convs[step] for step in steps], [xs[step] for step in steps],
            taps, gain2, bias2, consts, stats, calls[0],
        )
        stats = stat
        pieces += [own, lax.ppermute(given, "shard", plan.partners())]
    recv_f = after(lax.ppermute(send[0], "shard", forward), stats)
    proj_grad = (send[1] + recv_f.astype(jnp.float32)) * scale
    groups = [[CORES * p + c for p in range(plan.chips)] for c in range(CORES)]
    shares = lax.all_to_all(stats, "shard", 0, 0, axis_index_groups=groups)
    full = place_call(plan, calls, after(info, stats), pieces)
    summed = jnp.sum(after(shares, full, proj_grad), axis=0) * scale
    return (
        full, proj_grad, summed[: plan.taps], summed[plan.tap_rows : plan.tap_rows + 2]
    )


def shards(count, group_count, grad_out, saved_input, lengths, kernel, gain, bias, proj_weight):
    batches, frames, model_width = grad_out.shape
    plan = Plan(count, group_count, batches, frames, model_width, kernel.shape[0])
    args = (grad_out, saved_input, lengths, kernel, gain, bias, proj_weight)
    return ring_shards(plan, *args) if plan.usable() else plain_shards(*args)


def solution(mesh):
    placed = (
        P("groups", "shard", None),
        P("groups", "shard", None),
        P("groups"),
        P(),
        P(),
        P(),
        P("shard", None),
    )

    def body(*args):
        return shards(mesh.shape["shard"], mesh.shape["groups"], *args)

    return jax.shard_map(
        body,
        mesh=mesh,
        in_specs=placed,
        out_specs=(
            P("groups", "shard", None),
            P(("groups", "shard"), None),
            P("groups", "shard"),
            P("groups", "shard"),
        ),
        check_vma=False,
    )
```

```python
import functools

import jax
import jax.numpy as jnp
import numpy as np
from jax import lax
from jax.experimental import pallas as pl
from jax.experimental.pallas import tpu as pltpu
from jax.sharding import PartitionSpec as P


LANES = 128
CORES = 2
VMEM_LIMIT = 56 * 1024 * 1024
POINTS = 256


def cost(micros):
    return pl.CostEstimate(flops=0, transcendentals=0, bytes_accessed=int(micros * 3.6e6))


def extended(block, width):
    count = lax.axis_size("shard")
    forward = [(i, i + 1) for i in range(count - 1)]
    backward = [(target, source) for source, target in forward]
    low = lax.ppermute(block[:, block.shape[1] - width :], "shard", forward)
    high = lax.ppermute(block[:, :width], "shard", backward)
    return jnp.concatenate([low, block, high], axis=1)


def frame_mask(lengths, offset, count):
    position = offset + jnp.arange(count, dtype=jnp.int32)
    return (position[None, :] < lengths[:, None])[:, :, None]


def plain_shards(grad_out, saved_input, lengths, kernel, gain, bias, proj_weight):
    batches, frames, model_width = grad_out.shape
    tap_count = kernel.shape[0]
    half_span = (tap_count - 1) // 2
    offset = lax.axis_index("shard") * frames
    norm_scale = lax.rsqrt(jnp.sum(lengths).astype(jnp.float32))
    own_mask = frame_mask(lengths, offset, frames)
    masked_in = jnp.where(own_mask, saved_input, jnp.zeros_like(saved_input))
    masked_grad = jnp.where(own_mask, grad_out, jnp.zeros_like(grad_out))
    in_ext = extended(masked_in, half_span)
    conv = jnp.zeros(grad_out.shape, jnp.float32)
    for tap in range(tap_count):
        conv = conv + kernel[tap] * in_ext[:, tap : tap + frames].astype(jnp.float32)
    pre_act = gain * conv + bias
    gate_sig = jax.nn.sigmoid(pre_act)
    activated = (pre_act * gate_sig).astype(jnp.bfloat16)
    rows = masked_grad.reshape(batches * frames, model_width)
    weight = lax.all_gather(proj_weight, "shard", axis=0, tiled=True)
    act_grad = lax.dot_general(
        rows, weight, (((1,), (1,)), ((), ())), preferred_element_type=jnp.float32
    ).reshape(batches, frames, model_width)
    pre_grad = act_grad * gate_sig * (1.0 + pre_act * (1.0 - gate_sig))
    conv_grad = (pre_grad * gain).astype(jnp.bfloat16)
    grad_ext = extended(conv_grad, half_span)
    back_sum = jnp.zeros(grad_out.shape, jnp.float32)
    grad_float = conv_grad.astype(jnp.float32)
    tap_rows = []
    for tap in range(tap_count):
        begin = 2 * half_span - tap
        back_sum = back_sum + kernel[tap] * grad_ext[:, begin : begin + frames].astype(jnp.float32)
        tap_rows.append(
            jnp.sum(in_ext[:, tap : tap + frames].astype(jnp.float32) * grad_float, axis=(0, 1))
        )
    input_grad = jnp.where(own_mask, back_sum, 0.0).astype(jnp.bfloat16)
    tap_rows.append(jnp.sum(pre_grad * conv, axis=(0, 1)))
    tap_rows.append(jnp.sum(pre_grad, axis=(0, 1)))
    stats = jnp.stack(tap_rows, 0) * norm_scale
    summed = lax.psum_scatter(stats, "shard", scatter_dimension=1, tiled=True)
    product = lax.dot_general(
        activated.reshape(batches * frames, model_width),
        rows,
        (((0,), (0,)), ((), ())),
        preferred_element_type=jnp.float32,
    )
    proj_grad = lax.psum_scatter(product * norm_scale, "shard", scatter_dimension=0, tiled=True)
    return (input_grad, proj_grad, summed[:tap_count], summed[tap_count:])


class Plan:
    def __init__(self, count, groups, batches, frames, model_width, tap_count):
        self.count = count
        self.chips = count // CORES
        self.rounds = self.chips // 2
        self.batches = batches
        self.frames = frames
        self.chip_frames = CORES * frames
        self.width = model_width
        self.block = model_width // count
        self.taps = tap_count
        self.half = (tap_count - 1) // 2
        self.ghalo = -(-self.half // 16) * 16
        self.xhalo = 2 * self.ghalo
        self.ext = self.chip_frames + 2 * self.ghalo
        self.xext = self.chip_frames + 2 * self.xhalo
        self.tap_rows = -(-tap_count // 16) * 16
        self.stat_rows = self.tap_rows + 8
        self.weight_parts = 2 if groups == 2 else 1
        self.pairs = [(h, 1 - h) for h in range(self.rounds, 0, -1)]
        self.conv_windows = windows(self.ext, self.xhalo - self.ghalo - self.half + tap_count)
        self.back_windows = windows(self.chip_frames, self.ghalo + self.half + 1)

    def window_rows(self, found):
        return found[0] * (found[1] - 1) + POINTS

    def block_slot(self, step, side):
        return 3 + self.batches + 2 * step + side

    def usable(self):
        return (
            self.count % (2 * CORES) == 0
            and self.block == LANES
            and self.block * self.count == self.width
            and self.frames % 128 == 0
            and self.frames >= self.xhalo
            and self.taps % 2 == 1
            and 4 * self.ghalo <= POINTS // 2
            and self.window_rows(self.conv_windows) >= self.xext
            and self.window_rows(self.back_windows) >= self.ext
            and self.window_rows(self.conv_windows)
            >= self.xhalo + self.window_rows(self.back_windows) - self.back_windows[0]
            and self.chips == 8
            and self.batches == 2
        )

    def chip_at(self, position):
        half = self.chips // 2
        return jnp.where(position < half, 2 * position, 2 * (self.chips - 1 - position) + 1)

    def position_of(self, chip):
        return jnp.where(chip % 2 == 0, chip // 2, self.chips - 1 - chip // 2)

    def ring(self):
        half = self.chips // 2
        order = [2 * i for i in range(half)] + [2 * i + 1 for i in reversed(range(half))]
        forward = []
        for core in range(CORES):
            for i in range(self.chips):
                source, target = order[i], order[(i + 1) % self.chips]
                forward.append((CORES * source + core, CORES * target + core))
        return forward, [(t, s) for s, t in forward]

    def edges(self):
        pairs = []
        for chip in range(self.chips - 1):
            last, first = CORES * chip + 1, CORES * (chip + 1)
            pairs += [(last, first), (first, last)]
        return pairs

    def edges_like(self):
        pairs = []
        for chip in range(self.chips - 1):
            pairs.append((CORES * chip + 1, CORES * (chip + 1) + 1))
            pairs.append((CORES * (chip + 1), CORES * chip))
        return pairs

    def partners(self):
        return [(s, s ^ 1) for s in range(self.count)]


def sigmoid(value):
    return 0.5 * jnp.tanh(0.5 * value) + 0.5


def split(value):
    high = value.astype(jnp.bfloat16)
    return high, (value - high.astype(jnp.float32)).astype(jnp.bfloat16)


def split_matrix(matrix):
    high = matrix.astype(jnp.bfloat16)
    return high, (matrix - high.astype(np.float64)).astype(jnp.bfloat16)


def transforms(plan):
    time = np.arange(POINTS)
    theta = np.pi * (2 * np.arange(POINTS // 2) + 1) / POINTS
    angle = theta[:, None] * time[None, :]
    direct = np.concatenate([np.cos(angle), -np.sin(angle)], 0)
    inverse = direct.T * (2.0 / POINTS)

    def spectrum(lags):
        phase = theta[:, None] * lags[None, :]
        matrix = np.concatenate([np.cos(phase), np.sin(phase)], 0)
        return np.pad(matrix, ((0, 0), (0, plan.tap_rows - plan.taps)))

    taps = np.arange(plan.taps)
    back_lags = plan.ghalo + plan.half - taps
    lag_rows = np.pad(inverse[back_lags], ((0, plan.tap_rows - plan.taps), (0, 0)))
    half = lambda m: m.astype(jnp.bfloat16)
    conv_lags = plan.xhalo - plan.ghalo - plan.half + taps
    return (
        half(direct),
        half(inverse),
        np.stack(split_matrix(spectrum(conv_lags))),
        np.stack(split_matrix(spectrum(back_lags))),
        np.stack(split_matrix(lag_rows)),
        half(direct * (time < plan.back_windows[0])),
    )


def taps_spectrum(t_ref, k_ref):
    high, low = split(jnp.concatenate([k_ref[0][...], k_ref[1][...]], axis=1))
    dot = functools.partial(jnp.dot, preferred_element_type=jnp.float32)
    return dot(t_ref[0], high) + dot(t_ref[1], high) + dot(t_ref[0], low)


def to_spectrum(direct_ref, window):
    return jnp.dot(direct_ref[...], window, preferred_element_type=jnp.float32)


def from_spectrum(inverse_ref, rows, parts, slot):
    return jnp.dot(inverse_ref[:rows, :], parts[slot], preferred_element_type=jnp.float32)


def windows(rows_out, reach):
    count = -(-rows_out // ((POINTS - reach) // 16 * 16))
    return -(-rows_out // count // 16) * 16, count


STEP = 16
HALF = POINTS // 2


def spectral_product(spec, taps, parts, slot):
    for row in range(0, HALF, STEP):
        up, down = slice(row, row + STEP), slice(HALF + row, HALF + row + STEP)
        re, im, kr, ks = spec[slot, up, :], spec[slot, down, :], taps[up, :], taps[down, :]
        parts[slot, up, :] = (re * kr - im * ks).astype(jnp.bfloat16)
        parts[slot, down, :] = (re * ks + im * kr).astype(jnp.bfloat16)


def conv_body(plan, info, *refs):
    own_x, other_x, near_x, far_x, k_ref, gain_ref, bias_ref = (
        refs[2 * i : 2 * i + 2] for i in range(7)
    )
    direct, inverse, t_ref, own_g, other_g = refs[14:19]
    conv_ref, x_ref, out_f, out_b, spec, taps, parts, act, acc, grad, sem = refs[19:]
    each, count = plan.conv_windows
    f, xh, gh, cf = plan.frames, plan.xhalo, plan.ghalo, plan.chip_frames
    core, offset = info[0], info[1]

    copies = [
        pltpu.make_async_copy(
            ref.at[b], grad.at[b, pl.ds(pl.multiple_of(turned * f, f), f), :], sem.at[b, n]
        )
        for b in range(plan.batches)
        for n, (ref, turned) in enumerate(((own_g, core), (other_g, 1 - core)))
    ]
    for copy in copies:
        copy.start()
    taps[...] = taps_spectrum(t_ref, k_ref)

    def put(row, pair):
        for b in range(plan.batches):
            for part in range(0, pair[0].shape[1], STEP):
                position = lax.broadcasted_iota(jnp.int32, (STEP, LANES), 0) + (
                    offset - xh + row + part
                )
                keep = jnp.where(position < info[3 + b], 1.0, 0.0).astype(jnp.bfloat16)
                for side in range(2):
                    lanes = slice(side * LANES, (side + 1) * LANES)
                    x_ref[b, row + part : row + part + STEP, lanes] = (
                        pair[side][b, part : part + STEP, :] * keep
                    )

    @pl.when(core == 0)
    def _():
        put(0, near_x)
        put(xh, own_x)
        put(xh + f, other_x)
        put(xh + 2 * f, far_x)

    @pl.when(core != 0)
    def _():
        put(0, far_x)
        put(xh, other_x)
        put(xh + f, own_x)
        put(xh + 2 * f, near_x)

    x_ref[:, plan.xext :, :] = jnp.zeros(
        (plan.batches, x_ref.shape[1] - plan.xext, 2 * LANES), jnp.bfloat16
    )
    tiles = [slice(c, c + 2 * LANES) for c in range(0, plan.width, 2 * LANES)]

    def product(b, columns):
        return jnp.dot(act[b], grad[b, :, columns], preferred_element_type=jnp.float32)

    for b in range(plan.batches):
        if b == 1:
            for copy in copies:
                copy.wait()
            for columns in tiles:
                acc[:, columns] = product(0, columns)
        for j in range(count):
            spec[b * count + j] = to_spectrum(
                direct, x_ref[b, j * each : j * each + POINTS, :]
            )
        for j in range(count):
            slot = b * count + j
            spectral_product(spec, taps, parts, slot)
            rows = min(each, plan.ext - j * each)
            conv_ref[b, j * each : j * each + rows, :] = from_spectrum(
                inverse, rows, parts, slot
            )
        for i in range(cf // LANES):
            for side in range(2):
                lanes = slice(side * LANES, (side + 1) * LANES)
                begin = gh + i * LANES
                conv = conv_ref[b, begin : begin + LANES, lanes]
                pre = gain_ref[side][...] * conv + bias_ref[side][...]
                position = lax.broadcasted_iota(jnp.int32, (LANES, LANES), 0) + (
                    offset + i * LANES
                )
                value = jnp.where(position < info[3 + b], pre * sigmoid(pre), 0.0)
                act[b, lanes, i * LANES : (i + 1) * LANES] = value.T.astype(jnp.bfloat16)

    for columns in tiles:
        total = acc[:, columns] + product(1, columns)
        out_f[:, columns] = total[:LANES].astype(out_f.dtype)
        out_b[:, columns] = total[LANES:].astype(out_b.dtype)


def pair_specs(plan, step, shape, index):
    return [
        pl.BlockSpec(
            shape, lambda b, info, at=plan.block_slot(step, side): index(b, info[at])
        )
        for side in range(2)
    ]


def whole(array):
    return pl.BlockSpec(
        array.shape, lambda *_: (0,) * array.ndim, pipeline_mode=pl.Buffered(1)
    )


def conv_call(plan, step, info, x, xp, xa, xb, g, gp, kernel, gain, bias, consts, kind):
    bt = plan.batches
    flat = lambda b, block: (0, block)
    fixed = lambda b, info: (0, 0)
    direct, inverse, t_conv = consts[:3]
    wide = 2 * LANES
    slots = bt * plan.conv_windows[1]
    specs = functools.partial(pair_specs, plan, step)
    frames, halo = (bt, plan.frames, LANES), (bt, plan.xhalo, LANES)
    by_batch = lambda b, block: (0, 0, block)
    by_chip = lambda b, block: (0, 0, block // CORES)
    x_rows = plan.window_rows(plan.conv_windows)
    return pl.pallas_call(
        functools.partial(conv_body, plan),
        grid_spec=pltpu.PrefetchScalarGridSpec(
            num_scalar_prefetch=1,
            grid=(1,),
            in_specs=specs(frames, by_batch)
            + specs(frames, by_batch)
            + specs(halo, by_chip)
            + specs(halo, by_chip)
            + specs((plan.tap_rows, LANES), flat)
            + specs((1, LANES), flat)
            + specs((1, LANES), flat)
            + [whole(direct), whole(inverse), whole(t_conv)]
            + [pl.BlockSpec(memory_space=pl.ANY)] * 2,
            out_specs=[
                pl.BlockSpec((bt, plan.ext, wide), lambda b, info: (0, 0, 0)),
                pl.BlockSpec((bt, x_rows, wide), lambda b, info: (0, 0, 0)),
                pl.BlockSpec((LANES, plan.width), fixed),
                pl.BlockSpec((LANES, plan.width), fixed),
            ],
            scratch_shapes=[
                pltpu.VMEM((slots, POINTS, wide), jnp.float32),
                pltpu.VMEM((POINTS, wide), jnp.float32),
                pltpu.VMEM((slots, POINTS, wide), jnp.bfloat16),
                pltpu.VMEM((bt, wide, plan.chip_frames), jnp.bfloat16),
                pltpu.VMEM((wide, plan.width), jnp.float32),
                pltpu.VMEM((bt, plan.chip_frames, plan.width), jnp.bfloat16),
                pltpu.SemaphoreType.DMA((bt, 2)),
            ],
        ),
        out_shape=[
            jax.ShapeDtypeStruct((bt, plan.ext, wide), jnp.float32),
            jax.ShapeDtypeStruct((bt, x_rows, wide), jnp.bfloat16),
            jax.ShapeDtypeStruct((LANES, plan.width), kind),
            jax.ShapeDtypeStruct((LANES, plan.width), kind),
        ],
        compiler_params=pltpu.CompilerParams(vmem_limit_bytes=VMEM_LIMIT),
        cost_estimate=cost(6.0),
        name="conv",
    )(info, x, x, xp, xp, xa, xa, xb, xb, kernel, kernel, gain, gain, bias, bias,
      direct, inverse, t_conv, g, gp)


def back_body(plan, steps, earlier, sources, info, *refs):
    pairs = len(steps)
    g_refs = refs[:4]
    k_refs, gain_refs, bias_refs = (
        refs[4 + 2 * pairs * i : 4 + 2 * pairs * (i + 1)] for i in range(3)
    )
    refs = refs[4 + 6 * pairs :]
    conv_refs, x_refs, w_refs = refs[:pairs], refs[pairs : 2 * pairs], refs[2 * pairs : -28]
    (own_ref, send_ref, stat_ref, weight, mg, conv_buf, x_buf, ag_first, ag_second, gs, tail,
     spec, xspec, taps, cross, parts, os, flat, w_sem, c_sem, x_sem, g_sem) = refs[-22:]
    direct, segment, inverse, t_ref, lag_ref, before_ref = refs[-28:-22]
    core, offset, side_y = info[0], info[1], info[2]
    f, xh, gh, cf, ext = plan.frames, plan.xhalo, plan.ghalo, plan.chip_frames, plan.ext
    each, count = plan.back_windows
    turn = pl.program_id(0)

    def weight_copies(pair):
        made = []
        for n, (array, part, target, begin, rows) in enumerate(sources[pair]):
            first, into = begin, target * LANES
            if part is not None:
                into = pl.multiple_of(target * LANES + (side_y + part) % 2 * rows, rows)
            made.append(
                pltpu.make_async_copy(
                    w_refs[array].at[pl.ds(first, rows), :],
                    weight.at[pair, pl.ds(into, rows), :],
                    w_sem.at[pair, n],
                )
            )
        return made

    def frame_copies(pair):
        return [
            pltpu.make_async_copy(conv_refs[pair].at[i], conv_buf.at[pair, i], c_sem.at[pair, i])
            for i in range(plan.batches)
        ] + [
            pltpu.make_async_copy(x_refs[pair].at[i], x_buf.at[pair, i], x_sem.at[pair, i])
            for i in range(plan.batches)
        ]

    def grad_copies(b):
        own, other, near, far = g_refs
        moves = []
        for ref, turned in ((own, core), (other, 1 - core)):
            moves.append((ref.at[b], pl.multiple_of(gh + turned * f, gh), f, 0, plan.width))
        width = plan.width // CORES
        for ref, turned in ((near, core), (far, 1 - core)):
            for part in range(CORES):
                piece = ref.at[b, pl.ds(xh + part * gh, gh), :]
                moves.append((piece, pl.multiple_of(turned * (gh + cf), gh), gh, part * width, width))
        return [
            pltpu.make_async_copy(
                source, mg.at[b, pl.ds(row, rows), pl.ds(column, columns)], g_sem.at[b, n]
            )
            for n, (source, row, rows, column, columns) in enumerate(moves)
        ]

    def act_grad(pair, b):
        return lax.dot_general(
            mg[b], weight[pair], (((1,), (1,)), ((), ())), preferred_element_type=jnp.float32
        )

    @pl.when(turn == 0)
    def _():
        for copy in weight_copies(0) + grad_copies(0) + frame_copies(0) + grad_copies(1):
            copy.start()
        for pair in range(1, pairs):
            for copy in weight_copies(pair) + frame_copies(pair):
                copy.start()
        for b in range(plan.batches):
            gs[b, ext:, :] = jnp.zeros((gs.shape[1] - ext, 2 * LANES), jnp.bfloat16)
            tail[b] = jnp.zeros(tail.shape[1:], tail.dtype)
        for copy in weight_copies(0) + grad_copies(0):
            copy.wait()
        ag_first[...] = act_grad(0, 0)
        for copy in frame_copies(0) + grad_copies(1):
            copy.wait()

    for pair in range(pairs):

        @pl.when(turn == pair)
        def _():
            taps[...] = taps_spectrum(t_ref, k_refs[2 * pair : 2 * pair + 2])
            for row, pick in ((0, gain_refs), (8, bias_refs)):
                for side in range(2):
                    lanes = slice(side * LANES, (side + 1) * LANES)
                    flat[row : row + 8, lanes] = jnp.broadcast_to(
                        pick[2 * pair + side][...], (8, LANES)
                    )
            if pair > 0:
                for copy in frame_copies(pair):
                    copy.wait()
            if pair + 1 < pairs:
                for copy in weight_copies(pair + 1):
                    copy.wait()

    gain, bias = flat[:1, :], flat[8:9, :]
    last_rows = cf - (count - 1) * each
    fold = lambda v: jnp.sum(v.reshape(STEP // 8, 8, 2 * LANES), axis=0)
    gain_sum = jnp.zeros((8, 2 * LANES), jnp.float32)
    bias_sum = jnp.zeros((8, 2 * LANES), jnp.float32)
    for b in range(plan.batches):
        live = info[3 + b]
        here, ahead = (ag_first, ag_second) if b == 0 else (ag_second, ag_first)
        following = turn if b == 0 else jnp.minimum(turn + 1, pairs - 1)
        ahead[...] = act_grad(following, 1 - b)
        for j in range(count):
            begin = xh + j * each
            if j < count - 1:
                window = x_buf[turn, b, begin : begin + POINTS, :]
            else:
                tail[b, :last_rows, :] = x_buf[turn, b, begin : begin + last_rows, :]
                window = tail[b]
            xspec[b * count + j] = to_spectrum(segment, window)
        for row in range(0, ext, STEP):
            conv = conv_buf[turn, b, row : row + STEP, :]
            pre = gain * conv + bias
            sig = sigmoid(pre)
            value = here[row : row + STEP, :] * sig * (1.0 + pre * (1.0 - sig))
            position = lax.broadcasted_iota(jnp.int32, value.shape, 0) + (offset - gh + row)
            value = jnp.where(position < live, value, 0.0)
            gs[b, row : row + STEP, :] = (value * gain).astype(jnp.bfloat16)
            if gh <= row < gh + cf:
                gain_sum = gain_sum + fold(value * conv)
                bias_sum = bias_sum + fold(value)
        for j in range(count):
            spec[b * count + j] = to_spectrum(direct, gs[b, j * each : j * each + POINTS, :])
        for j in range(count):
            slot = b * count + j
            spectral_product(spec, taps, parts, slot)
            rows = min(each, cf - j * each)
            value = from_spectrum(inverse, rows, parts, slot)
            position = offset + j * each + lax.broadcasted_iota(jnp.int32, value.shape, 0)
            os[b, j * each : j * each + rows, :] = jnp.where(
                position < live, value, 0.0
            ).astype(jnp.bfloat16)

    for row in range(0, HALF, STEP):
        up, down = slice(row, row + STEP), slice(HALF + row, HALF + row + STEP)
        total_r = total_i = jnp.zeros((STEP, 2 * LANES), jnp.float32)
        for j in range(plan.batches * count):
            re, im, xr, xi = spec[j, up, :], spec[j, down, :], xspec[j, up, :], xspec[j, down, :]
            total_r = total_r + (re * xr + im * xi)
            total_i = total_i + (im * xr - re * xi)
        cross[up, :] = total_r
        cross[down, :] = total_i

    @pl.when(core == 0)
    def _():
        own_ref[0] = os[:, :f]
        send_ref[0] = os[:, f:]

    @pl.when(core != 0)
    def _():
        own_ref[0] = os[:, f:]
        send_ref[0] = os[:, :f]

    high, low = split(cross[...])
    dot = functools.partial(jnp.dot, preferred_element_type=jnp.float32)
    taps_total = dot(lag_ref[0], high) + dot(lag_ref[1], high) + dot(lag_ref[0], low)
    total = [jnp.sum(value, axis=0, keepdims=True) for value in (gain_sum, bias_sum)]
    pad = jnp.zeros((plan.stat_rows - plan.tap_rows - 2, 2 * LANES), jnp.float32)
    total = jnp.concatenate([taps_total] + total + [pad], axis=0)
    if earlier is None:
        stat_ref[0] = total
        return
    for side in range(2):
        lanes = slice(side * LANES, (side + 1) * LANES)
        chip = info[plan.block_slot(steps[0], side) - 2 * turn] // CORES
        stat_ref[chip] = total[:, lanes]
        for n, step in enumerate(earlier):
            chip = info[plan.block_slot(step, side)] // CORES
            stat_ref[chip] = before_ref[n, :, lanes]


def back_call(
    plan, steps, info, grads, sources, arrays, convs, xs, kernel, gain, bias, consts, before, earlier
):
    bt, pairs = plan.batches, len(steps)
    direct, inverse, _, t_back, lags, segment = consts
    wide = 2 * LANES
    slots = bt * plan.back_windows[1]
    any_space = pl.BlockSpec(memory_space=pl.ANY)

    def by_block(shape):
        return [
            pl.BlockSpec(
                shape, lambda p, info, at=plan.block_slot(step, side): (0, info[at]),
                pipeline_mode=pl.Buffered(1),
            )
            for step in steps for side in range(2)
        ]

    frames = (bt, plan.frames, wide)
    each = pl.BlockSpec((1,) + frames, lambda p, info: (p, 0, 0, 0))
    most = max(len(source) for source in sources)
    stat_shape = (pairs, plan.stat_rows, wide)
    stat_spec = pl.BlockSpec((1, plan.stat_rows, wide), lambda p, info: (p, 0, 0))
    if before is None:
        earlier, before = None, jnp.zeros((8, LANES), jnp.float32)
    else:
        stat_shape = (plan.chips, plan.stat_rows, LANES)
        stat_spec = pl.BlockSpec(stat_shape, lambda p, info: (0, 0, 0))
    return pl.pallas_call(
        functools.partial(back_body, plan, steps, earlier, sources),
        grid_spec=pltpu.PrefetchScalarGridSpec(
            num_scalar_prefetch=1,
            grid=(pairs,),
            in_specs=[any_space] * len(grads)
            + by_block((plan.tap_rows, LANES))
            + by_block((1, LANES))
            + by_block((1, LANES))
            + [any_space] * (2 * pairs + len(arrays))
            + [whole(c) for c in (direct, segment, inverse, t_back, lags, before)],
            out_specs=[
                each,
                each,
                stat_spec,
            ],
            scratch_shapes=[
                pltpu.VMEM((pairs, wide, plan.width), jnp.bfloat16),
                pltpu.VMEM((bt, plan.ext, plan.width), jnp.bfloat16),
                pltpu.VMEM((pairs, bt, plan.ext, wide), jnp.float32),
                pltpu.VMEM((pairs, bt, xs[0].shape[1], wide), jnp.bfloat16),
                pltpu.VMEM((plan.ext, wide), jnp.float32),
                pltpu.VMEM((plan.ext, wide), jnp.float32),
                pltpu.VMEM((bt, plan.window_rows(plan.back_windows), wide), jnp.bfloat16),
                pltpu.VMEM((bt, POINTS, wide), jnp.bfloat16),
                pltpu.VMEM((slots, POINTS, wide), jnp.float32),
                pltpu.VMEM((slots, POINTS, wide), jnp.float32),
                pltpu.VMEM((POINTS, wide), jnp.float32),
                pltpu.VMEM((POINTS, wide), jnp.float32),
                pltpu.VMEM((slots, POINTS, wide), jnp.bfloat16),
                pltpu.VMEM((bt, plan.chip_frames, wide), jnp.bfloat16),
                pltpu.VMEM((16, wide), jnp.float32),
                pltpu.SemaphoreType.DMA((pairs, most)),
                pltpu.SemaphoreType.DMA((pairs, bt)),
                pltpu.SemaphoreType.DMA((pairs, bt)),
                pltpu.SemaphoreType.DMA((bt, 2 + 2 * CORES)),
            ],
        ),
        out_shape=[
            jax.ShapeDtypeStruct((pairs,) + frames, jnp.bfloat16),
            jax.ShapeDtypeStruct((pairs,) + frames, jnp.bfloat16),
            jax.ShapeDtypeStruct(stat_shape, jnp.float32),
        ],
        compiler_params=pltpu.CompilerParams(vmem_limit_bytes=VMEM_LIMIT),
        cost_estimate=cost(6.0 * pairs),
        name="back",
    )(info, *grads, *[kernel] * 2 * pairs, *[gain] * 2 * pairs, *[bias] * 2 * pairs,
      *convs, *xs, *arrays, direct, segment, inverse, t_back, lags, before)


def place_body(plan, calls, info, *refs):
    out_ref = refs[-1]
    for i, ref in enumerate(refs[:-1]):
        for turn, step in enumerate(calls[i // 2]):
            for side in range(2):
                block = info[plan.block_slot(step, side)]
                if i % 2:
                    block = block + 1 - 2 * info[0]
                column = pl.multiple_of(block * LANES, LANES)
                lanes = slice(side * LANES, (side + 1) * LANES)
                out_ref[:, :, pl.ds(column, LANES)] = ref[turn, :, :, lanes]


def place_call(plan, calls, info, arrays):
    shape = (plan.batches, plan.frames, plan.width)
    return pl.pallas_call(
        functools.partial(place_body, plan, calls),
        grid_spec=pltpu.PrefetchScalarGridSpec(
            num_scalar_prefetch=1,
            grid=(1,),
            in_specs=[whole(array) for array in arrays],
            out_specs=pl.BlockSpec(shape, lambda g, info: (0, 0, 0)),
        ),
        out_shape=jax.ShapeDtypeStruct(shape, jnp.bfloat16),
        compiler_params=pltpu.CompilerParams(vmem_limit_bytes=VMEM_LIMIT),
        cost_estimate=cost(3.0),
        name="place",
    )(info, *arrays)


def edge_body(plan, x_first, x_last, g_first, g_last, near_ref, far_ref):
    core = lax.axis_index("shard") % CORES

    def take(owner, x_ref, grad_ref):
        for i in range(plan.chips):
            for out, parity in ((near_ref, 1 - owner), (far_ref, owner)):
                column = (CORES * i + parity) * LANES
                out[:, : plan.xhalo, i * LANES : (i + 1) * LANES] = x_ref[
                    :, :, column : column + LANES
                ]
        for part in range(CORES):
            row = plan.xhalo + part * plan.ghalo
            width = plan.width // CORES
            near_ref[:, row : row + plan.ghalo, :] = grad_ref[
                :, :, part * width : (part + 1) * width
            ]

    pl.when(core == 0)(lambda: take(0, x_first, g_first))
    pl.when(core != 0)(lambda: take(1, x_last, g_last))


def edge_call(plan, x, g):
    def spec(rows, first):
        shape = (plan.batches, rows, plan.width)
        block = 0 if first else plan.frames // rows - 1
        return pl.BlockSpec(shape, lambda i: (0, block, 0))

    xh, gh = plan.xhalo, plan.ghalo
    shapes = [
        (plan.batches, rows, plan.width // CORES) for rows in (xh + CORES * gh, xh)
    ]
    return pl.pallas_call(
        functools.partial(edge_body, plan),
        grid=(1,),
        in_specs=[spec(xh, True), spec(xh, False), spec(gh, True), spec(gh, False)],
        out_specs=[pl.BlockSpec(shape, lambda i: (0, 0, 0)) for shape in shapes],
        out_shape=[jax.ShapeDtypeStruct(shape, jnp.bfloat16) for shape in shapes],
        cost_estimate=cost(1.0),
        name="edge",
    )(x, x, g, g)


def after(value, *others):
    return lax.optimization_barrier((value, *others))[0]


def ring_shards(plan, grad_out, saved_input, lengths, kernel, gain, bias, proj_weight):
    index = lax.axis_index("shard")
    group = lax.axis_index("groups")
    core, chip = index % CORES, index // CORES
    place = plan.position_of(chip)
    forward, backward = plan.ring()
    offset = chip * plan.chip_frames
    scale = lax.rsqrt(jnp.sum(lengths).astype(jnp.float32))
    pairs = plan.pairs
    far = jnp.asarray([d for pair in pairs for d in pair], jnp.int32)
    owned = CORES * plan.chip_at((place + far + plan.chips) % plan.chips) + core
    info = jnp.concatenate([jnp.stack([core, offset, group]), lengths, owned]).astype(jnp.int32)
    gain2, bias2 = gain.reshape(1, -1), bias.reshape(1, -1)
    taps = jnp.pad(kernel, ((0, plan.tap_rows - plan.taps), (0, 0)))
    consts = [jnp.asarray(c) for c in transforms(plan)]

    x_near, x_far = edge_call(plan, saved_input, grad_out)
    xa = lax.ppermute(x_near, "shard", plan.edges())
    xb = lax.ppermute(x_far, "shard", plan.edges_like())
    xp = lax.ppermute(saved_input, "shard", plan.partners())
    mgp = lax.ppermute(grad_out, "shard", plan.partners())

    halved = plan.weight_parts == 2
    piece = LANES // 2
    around = {}
    going = [proj_weight] * 2
    if halved:
        going = [lax.dynamic_slice_in_dim(proj_weight, group * piece, piece, 0)] * 2
    xa, xb, taps, info, scale = lax.optimization_barrier((xa, xb, taps, info, scale))

    def weight_round(step):
        going[0] = lax.ppermute(going[0], "shard", forward)
        around[-step] = going[0]
        if step < plan.rounds:
            going[1] = lax.ppermute(going[1], "shard", backward)
            around[step] = going[1]
        else:
            around[step] = around.pop(-step)

    convs, xs, products = [], [], []

    def conv_step(step, order):
        conv, x, *product = conv_call(
            plan, step, order, saved_input, xp, xa, xb, grad_out,
            mgp, taps, gain2, bias2, consts, jnp.bfloat16 if step == 0 else jnp.float32,
        )
        convs.append(conv)
        xs.append(x)
        products.append(product)

    def sum_round(step, send, *behind):
        received = (
            lax.ppermute(send[0], "shard", forward), lax.ppermute(send[1], "shard", backward)
        )
        kinds = (jnp.bfloat16, jnp.bfloat16 if step < plan.rounds - 1 else jnp.float32)
        own = lax.optimization_barrier((*products[step], *received, *behind))[:2]
        return [
            (product + value.astype(jnp.float32)).astype(kind)
            for product, value, kind in zip(own, received, kinds)
        ]

    def wait_for(value):
        going[:] = lax.optimization_barrier((*going, value))[:2]

    weight_round(1)
    conv_step(0, info)
    xc = lax.ppermute(after(xa, products[0][0]), "shard", plan.partners())
    wait_for(products[0][0])
    weight_round(2)
    conv_step(1, after(info, products[0][0]))
    wait_for(products[1][0])
    weight_round(3)
    conv_step(2, after(info, products[1][0]))
    wait_for(products[2][0])
    weight_round(4)
    send = sum_round(1, products[0], products[2][0])
    conv_step(3, after(info, products[2][0], *send))
    send = sum_round(2, send, products[3][0])

    arrays = [proj_weight]
    source = {0: [(0, None, 0, LANES)]}

    def keep(array):
        arrays.append(array)
        return len(arrays) - 1

    swap = [
        (g * plan.count + s, (1 - g) * plan.count + s) for g in range(2) for s in range(plan.count)
    ]
    for distances in ([1, -1], [2, -2], [3, -3, 4]):
        if not halved:
            for d in distances:
                source[d] = [(keep(around[d]), None, 0, LANES)]
            continue
        swapped = keep(
            lax.ppermute(
                jnp.concatenate([around[d] for d in distances], 0),
                ("groups", "shard"), swap,
            )
        )
        for i, d in enumerate(distances):
            source[d] = [(keep(around[d]), 0, 0, piece), (swapped, 1, i * piece, piece)]

    calls = [(3, 2), (1, 0)]
    pieces, stats = [], None
    for steps in calls:
        if steps == calls[-1]:
            send = sum_round(3, send, pieces[0])
        order = after(info, products[-1][0], *send)
        used = sorted({a[0] for step in steps for d in pairs[step] for a in source[d]})
        sources = [
            [
                (used.index(array), part, block, begin, rows)
                for block, d in enumerate(pairs[step])
                for array, part, begin, rows in source[d]
            ]
            for step in steps
        ]
        own, given, stat = back_call(
            plan, steps, order, (grad_out, mgp, xa, xc), sources, [arrays[i] for i in used],
            [convs[step] for step in steps], [xs[step] for step in steps],
            taps, gain2, bias2, consts, stats, calls[0],
        )
        stats = stat
        pieces += [own, lax.ppermute(given, "shard", plan.partners())]
    recv_f = after(lax.ppermute(send[0], "shard", forward), stats)
    proj_grad = (send[1] + recv_f.astype(jnp.float32)) * scale
    groups = [[CORES * p + c for p in range(plan.chips)] for c in range(CORES)]
    shares = lax.all_to_all(stats, "shard", 0, 0, axis_index_groups=groups)
    full = place_call(plan, calls, after(info, stats), pieces)
    summed = jnp.sum(after(shares, full, proj_grad), axis=0) * scale
    return (
        full, proj_grad, summed[: plan.taps], summed[plan.tap_rows : plan.tap_rows + 2]
    )


def shards(count, group_count, grad_out, saved_input, lengths, kernel, gain, bias, proj_weight):
    batches, frames, model_width = grad_out.shape
    plan = Plan(count, group_count, batches, frames, model_width, kernel.shape[0])
    args = (grad_out, saved_input, lengths, kernel, gain, bias, proj_weight)
    return ring_shards(plan, *args) if plan.usable() else plain_shards(*args)


def solution(mesh):
    placed = (
        P("groups", "shard", None),
        P("groups", "shard", None),
        P("groups"),
        P(),
        P(),
        P(),
        P("shard", None),
    )

    def body(*args):
        return shards(mesh.shape["shard"], mesh.shape["groups"], *args)

    return jax.shard_map(
        body,
        mesh=mesh,
        in_specs=placed,
        out_specs=(
            P("groups", "shard", None),
            P(("groups", "shard"), None),
            P("groups", "shard"),
            P("groups", "shard"),
        ),
        check_vma=False,
    )
```

```python
import functools

import jax
import jax.numpy as jnp
import numpy as np
from jax import lax
from jax.experimental import pallas as pl
from jax.experimental.pallas import tpu as pltpu
from jax.sharding import PartitionSpec as P


LANES = 128
CORES = 2
VMEM_LIMIT = 56 * 1024 * 1024
POINTS = 256


def cost(micros):
    return pl.CostEstimate(flops=0, transcendentals=0, bytes_accessed=int(micros * 3.6e6))


def extended(block, width):
    count = lax.axis_size("shard")
    forward = [(i, i + 1) for i in range(count - 1)]
    backward = [(target, source) for source, target in forward]
    low = lax.ppermute(block[:, block.shape[1] - width :], "shard", forward)
    high = lax.ppermute(block[:, :width], "shard", backward)
    return jnp.concatenate([low, block, high], axis=1)


def frame_mask(lengths, offset, count):
    position = offset + jnp.arange(count, dtype=jnp.int32)
    return (position[None, :] < lengths[:, None])[:, :, None]


def plain_shards(grad_out, saved_input, lengths, kernel, gain, bias, proj_weight):
    batches, frames, model_width = grad_out.shape
    tap_count = kernel.shape[0]
    half_span = (tap_count - 1) // 2
    offset = lax.axis_index("shard") * frames
    norm_scale = lax.rsqrt(jnp.sum(lengths).astype(jnp.float32))
    own_mask = frame_mask(lengths, offset, frames)
    masked_in = jnp.where(own_mask, saved_input, jnp.zeros_like(saved_input))
    masked_grad = jnp.where(own_mask, grad_out, jnp.zeros_like(grad_out))
    in_ext = extended(masked_in, half_span)
    conv = jnp.zeros(grad_out.shape, jnp.float32)
    for tap in range(tap_count):
        conv = conv + kernel[tap] * in_ext[:, tap : tap + frames].astype(jnp.float32)
    pre_act = gain * conv + bias
    gate_sig = jax.nn.sigmoid(pre_act)
    activated = (pre_act * gate_sig).astype(jnp.bfloat16)
    rows = masked_grad.reshape(batches * frames, model_width)
    weight = lax.all_gather(proj_weight, "shard", axis=0, tiled=True)
    act_grad = lax.dot_general(
        rows, weight, (((1,), (1,)), ((), ())), preferred_element_type=jnp.float32
    ).reshape(batches, frames, model_width)
    pre_grad = act_grad * gate_sig * (1.0 + pre_act * (1.0 - gate_sig))
    conv_grad = (pre_grad * gain).astype(jnp.bfloat16)
    grad_ext = extended(conv_grad, half_span)
    back_sum = jnp.zeros(grad_out.shape, jnp.float32)
    grad_float = conv_grad.astype(jnp.float32)
    tap_rows = []
    for tap in range(tap_count):
        begin = 2 * half_span - tap
        back_sum = back_sum + kernel[tap] * grad_ext[:, begin : begin + frames].astype(jnp.float32)
        tap_rows.append(
            jnp.sum(in_ext[:, tap : tap + frames].astype(jnp.float32) * grad_float, axis=(0, 1))
        )
    input_grad = jnp.where(own_mask, back_sum, 0.0).astype(jnp.bfloat16)
    tap_rows.append(jnp.sum(pre_grad * conv, axis=(0, 1)))
    tap_rows.append(jnp.sum(pre_grad, axis=(0, 1)))
    stats = jnp.stack(tap_rows, 0) * norm_scale
    summed = lax.psum_scatter(stats, "shard", scatter_dimension=1, tiled=True)
    product = lax.dot_general(
        activated.reshape(batches * frames, model_width),
        rows,
        (((0,), (0,)), ((), ())),
        preferred_element_type=jnp.float32,
    )
    proj_grad = lax.psum_scatter(product * norm_scale, "shard", scatter_dimension=0, tiled=True)
    return (input_grad, proj_grad, summed[:tap_count], summed[tap_count:])


class Plan:
    def __init__(self, count, groups, batches, frames, model_width, tap_count):
        self.count = count
        self.chips = count // CORES
        self.rounds = self.chips // 2
        self.batches = batches
        self.frames = frames
        self.chip_frames = CORES * frames
        self.width = model_width
        self.block = model_width // count
        self.taps = tap_count
        self.half = (tap_count - 1) // 2
        self.ghalo = -(-self.half // 16) * 16
        self.xhalo = 2 * self.ghalo
        self.ext = self.chip_frames + 2 * self.ghalo
        self.xext = self.chip_frames + 2 * self.xhalo
        self.tap_rows = -(-tap_count // 16) * 16
        self.stat_rows = self.tap_rows + 8
        self.weight_parts = 2 if groups == 2 else 1
        self.pairs = [(h, 1 - h) for h in range(self.rounds, 0, -1)]
        self.conv_windows = windows(self.ext, self.xhalo - self.ghalo - self.half + tap_count)
        self.back_windows = windows(self.chip_frames, self.ghalo + self.half + 1)

    def window_rows(self, found):
        return found[0] * (found[1] - 1) + POINTS

    def block_slot(self, step, side):
        return 3 + self.batches + 2 * step + side

    def usable(self):
        return (
            self.count % (2 * CORES) == 0
            and self.block == LANES
            and self.block * self.count == self.width
            and self.frames % 128 == 0
            and self.frames >= self.xhalo
            and self.taps % 2 == 1
            and 4 * self.ghalo <= POINTS // 2
            and self.window_rows(self.conv_windows) >= self.xext
            and self.window_rows(self.back_windows) >= self.ext
            and self.window_rows(self.conv_windows)
            >= self.xhalo + self.window_rows(self.back_windows) - self.back_windows[0]
            and self.chips == 8
            and self.batches == 2
        )

    def chip_at(self, position):
        half = self.chips // 2
        return jnp.where(position < half, 2 * position, 2 * (self.chips - 1 - position) + 1)

    def position_of(self, chip):
        return jnp.where(chip % 2 == 0, chip // 2, self.chips - 1 - chip // 2)

    def ring(self):
        half = self.chips // 2
        order = [2 * i for i in range(half)] + [2 * i + 1 for i in reversed(range(half))]
        forward = []
        for core in range(CORES):
            for i in range(self.chips):
                source, target = order[i], order[(i + 1) % self.chips]
                forward.append((CORES * source + core, CORES * target + core))
        return forward, [(t, s) for s, t in forward]

    def edges(self):
        pairs = []
        for chip in range(self.chips - 1):
            last, first = CORES * chip + 1, CORES * (chip + 1)
            pairs += [(last, first), (first, last)]
        return pairs

    def edges_like(self):
        pairs = []
        for chip in range(self.chips - 1):
            pairs.append((CORES * chip + 1, CORES * (chip + 1) + 1))
            pairs.append((CORES * (chip + 1), CORES * chip))
        return pairs

    def partners(self):
        return [(s, s ^ 1) for s in range(self.count)]


def sigmoid(value):
    return 0.5 * jnp.tanh(0.5 * value) + 0.5


def split(value):
    high = value.astype(jnp.bfloat16)
    return high, (value - high.astype(jnp.float32)).astype(jnp.bfloat16)


def split_matrix(matrix):
    high = matrix.astype(jnp.bfloat16)
    return high, (matrix - high.astype(np.float64)).astype(jnp.bfloat16)


def transforms(plan):
    time = np.arange(POINTS)
    theta = np.pi * (2 * np.arange(POINTS // 2) + 1) / POINTS
    angle = theta[:, None] * time[None, :]
    direct = np.concatenate([np.cos(angle), -np.sin(angle)], 0)
    inverse = direct.T * (2.0 / POINTS)

    def spectrum(lags):
        phase = theta[:, None] * lags[None, :]
        matrix = np.concatenate([np.cos(phase), np.sin(phase)], 0)
        return np.pad(matrix, ((0, 0), (0, plan.tap_rows - plan.taps)))

    taps = np.arange(plan.taps)
    back_lags = plan.ghalo + plan.half - taps
    lag_rows = np.pad(inverse[back_lags], ((0, plan.tap_rows - plan.taps), (0, 0)))
    half = lambda m: m.astype(jnp.bfloat16)
    conv_lags = plan.xhalo - plan.ghalo - plan.half + taps
    return (
        half(direct),
        half(inverse),
        np.stack(split_matrix(spectrum(conv_lags))),
        np.stack(split_matrix(spectrum(back_lags))),
        np.stack(split_matrix(lag_rows)),
        half(direct * (time < plan.back_windows[0])),
    )


def taps_spectrum(t_ref, k_ref):
    high, low = split(jnp.concatenate([k_ref[0][...], k_ref[1][...]], axis=1))
    dot = functools.partial(jnp.dot, preferred_element_type=jnp.float32)
    return dot(t_ref[0], high) + dot(t_ref[1], high) + dot(t_ref[0], low)


def to_spectrum(direct_ref, window):
    return jnp.dot(direct_ref[...], window, preferred_element_type=jnp.float32)


def from_spectrum(inverse_ref, rows, parts, slot):
    return jnp.dot(inverse_ref[:rows, :], parts[slot], preferred_element_type=jnp.float32)


def windows(rows_out, reach):
    count = -(-rows_out // ((POINTS - reach) // 16 * 16))
    return -(-rows_out // count // 16) * 16, count


STEP = 16
HALF = POINTS // 2


def spectral_product(spec, taps, parts, slot):
    for row in range(0, HALF, STEP):
        up, down = slice(row, row + STEP), slice(HALF + row, HALF + row + STEP)
        re, im, kr, ks = spec[slot, up, :], spec[slot, down, :], taps[up, :], taps[down, :]
        parts[slot, up, :] = (re * kr - im * ks).astype(jnp.bfloat16)
        parts[slot, down, :] = (re * ks + im * kr).astype(jnp.bfloat16)


def conv_body(plan, info, *refs):
    own_x, other_x, near_x, far_x, k_ref, gain_ref, bias_ref = (
        refs[2 * i : 2 * i + 2] for i in range(7)
    )
    direct, inverse, t_ref, own_g, other_g = refs[14:19]
    conv_ref, x_ref, out_f, out_b, spec, taps, parts, act, acc, grad, sem = refs[19:]
    each, count = plan.conv_windows
    f, xh, gh, cf = plan.frames, plan.xhalo, plan.ghalo, plan.chip_frames
    core, offset = info[0], info[1]

    copies = [
        pltpu.make_async_copy(
            ref.at[b], grad.at[b, pl.ds(pl.multiple_of(turned * f, f), f), :], sem.at[b, n]
        )
        for b in range(plan.batches)
        for n, (ref, turned) in enumerate(((own_g, core), (other_g, 1 - core)))
    ]
    for copy in copies:
        copy.start()
    taps[...] = taps_spectrum(t_ref, k_ref)

    def put(row, pair):
        for b in range(plan.batches):
            for part in range(0, pair[0].shape[1], STEP):
                position = lax.broadcasted_iota(jnp.int32, (STEP, LANES), 0) + (
                    offset - xh + row + part
                )
                keep = jnp.where(position < info[3 + b], 1.0, 0.0).astype(jnp.bfloat16)
                for side in range(2):
                    lanes = slice(side * LANES, (side + 1) * LANES)
                    x_ref[b, row + part : row + part + STEP, lanes] = (
                        pair[side][b, part : part + STEP, :] * keep
                    )

    @pl.when(core == 0)
    def _():
        put(0, near_x)
        put(xh, own_x)
        put(xh + f, other_x)
        put(xh + 2 * f, far_x)

    @pl.when(core != 0)
    def _():
        put(0, far_x)
        put(xh, other_x)
        put(xh + f, own_x)
        put(xh + 2 * f, near_x)

    x_ref[:, plan.xext :, :] = jnp.zeros(
        (plan.batches, x_ref.shape[1] - plan.xext, 2 * LANES), jnp.bfloat16
    )
    tiles = [slice(c, c + 2 * LANES) for c in range(0, plan.width, 2 * LANES)]

    def product(b, columns):
        return jnp.dot(act[b], grad[b, :, columns], preferred_element_type=jnp.float32)

    for b in range(plan.batches):
        if b == 1:
            for copy in copies:
                copy.wait()
            for columns in tiles:
                acc[:, columns] = product(0, columns)
        for j in range(count):
            spec[b * count + j] = to_spectrum(
                direct, x_ref[b, j * each : j * each + POINTS, :]
            )
        for j in range(count):
            slot = b * count + j
            spectral_product(spec, taps, parts, slot)
            rows = min(each, plan.ext - j * each)
            conv_ref[b, j * each : j * each + rows, :] = from_spectrum(
                inverse, rows, parts, slot
            )
        for i in range(cf // LANES):
            for side in range(2):
                lanes = slice(side * LANES, (side + 1) * LANES)
                begin = gh + i * LANES
                conv = conv_ref[b, begin : begin + LANES, lanes]
                pre = gain_ref[side][...] * conv + bias_ref[side][...]
                position = lax.broadcasted_iota(jnp.int32, (LANES, LANES), 0) + (
                    offset + i * LANES
                )
                value = jnp.where(position < info[3 + b], pre * sigmoid(pre), 0.0)
                act[b, lanes, i * LANES : (i + 1) * LANES] = value.T.astype(jnp.bfloat16)

    for columns in tiles:
        total = acc[:, columns] + product(1, columns)
        out_f[:, columns] = total[:LANES].astype(out_f.dtype)
        out_b[:, columns] = total[LANES:].astype(out_b.dtype)


def pair_specs(plan, step, shape, index):
    return [
        pl.BlockSpec(
            shape, lambda b, info, at=plan.block_slot(step, side): index(b, info[at])
        )
        for side in range(2)
    ]


def whole(array):
    return pl.BlockSpec(
        array.shape, lambda *_: (0,) * array.ndim, pipeline_mode=pl.Buffered(1)
    )


def conv_call(plan, step, info, x, xp, xa, xb, g, gp, kernel, gain, bias, consts, kind):
    bt = plan.batches
    flat = lambda b, block: (0, block)
    fixed = lambda b, info: (0, 0)
    direct, inverse, t_conv = consts[:3]
    wide = 2 * LANES
    slots = bt * plan.conv_windows[1]
    specs = functools.partial(pair_specs, plan, step)
    frames, halo = (bt, plan.frames, LANES), (bt, plan.xhalo, LANES)
    by_batch = lambda b, block: (0, 0, block)
    by_chip = lambda b, block: (0, 0, block // CORES)
    x_rows = plan.window_rows(plan.conv_windows)
    return pl.pallas_call(
        functools.partial(conv_body, plan),
        grid_spec=pltpu.PrefetchScalarGridSpec(
            num_scalar_prefetch=1,
            grid=(1,),
            in_specs=specs(frames, by_batch)
            + specs(frames, by_batch)
            + specs(halo, by_chip)
            + specs(halo, by_chip)
            + specs((plan.tap_rows, LANES), flat)
            + specs((1, LANES), flat)
            + specs((1, LANES), flat)
            + [whole(direct), whole(inverse), whole(t_conv)]
            + [pl.BlockSpec(memory_space=pl.ANY)] * 2,
            out_specs=[
                pl.BlockSpec((bt, plan.ext, wide), lambda b, info: (0, 0, 0)),
                pl.BlockSpec((bt, x_rows, wide), lambda b, info: (0, 0, 0)),
                pl.BlockSpec((LANES, plan.width), fixed),
                pl.BlockSpec((LANES, plan.width), fixed),
            ],
            scratch_shapes=[
                pltpu.VMEM((slots, POINTS, wide), jnp.float32),
                pltpu.VMEM((POINTS, wide), jnp.float32),
                pltpu.VMEM((slots, POINTS, wide), jnp.bfloat16),
                pltpu.VMEM((bt, wide, plan.chip_frames), jnp.bfloat16),
                pltpu.VMEM((wide, plan.width), jnp.float32),
                pltpu.VMEM((bt, plan.chip_frames, plan.width), jnp.bfloat16),
                pltpu.SemaphoreType.DMA((bt, 2)),
            ],
        ),
        out_shape=[
            jax.ShapeDtypeStruct((bt, plan.ext, wide), jnp.float32),
            jax.ShapeDtypeStruct((bt, x_rows, wide), jnp.bfloat16),
            jax.ShapeDtypeStruct((LANES, plan.width), kind),
            jax.ShapeDtypeStruct((LANES, plan.width), kind),
        ],
        compiler_params=pltpu.CompilerParams(vmem_limit_bytes=VMEM_LIMIT),
        cost_estimate=cost(6.0),
        name="conv",
    )(info, x, x, xp, xp, xa, xa, xb, xb, kernel, kernel, gain, gain, bias, bias,
      direct, inverse, t_conv, g, gp)


def back_body(plan, steps, earlier, sources, info, *refs):
    pairs = len(steps)
    g_refs = refs[:4]
    k_refs, gain_refs, bias_refs = (
        refs[4 + 2 * pairs * i : 4 + 2 * pairs * (i + 1)] for i in range(3)
    )
    refs = refs[4 + 6 * pairs :]
    conv_refs, x_refs, w_refs = refs[:pairs], refs[pairs : 2 * pairs], refs[2 * pairs : -28]
    (own_ref, send_ref, stat_ref, weight, mg, conv_buf, x_buf, ag_first, ag_second, gs, tail,
     spec, xspec, taps, cross, parts, os, flat, w_sem, c_sem, x_sem, g_sem) = refs[-22:]
    direct, segment, inverse, t_ref, lag_ref, before_ref = refs[-28:-22]
    core, offset, side_y = info[0], info[1], info[2]
    f, xh, gh, cf, ext = plan.frames, plan.xhalo, plan.ghalo, plan.chip_frames, plan.ext
    each, count = plan.back_windows
    turn = pl.program_id(0)

    def weight_copies(pair):
        made = []
        for n, (array, part, target, begin, rows) in enumerate(sources[pair]):
            first, into = begin, target * LANES
            if part is not None:
                into = pl.multiple_of(target * LANES + (side_y + part) % 2 * rows, rows)
            made.append(
                pltpu.make_async_copy(
                    w_refs[array].at[pl.ds(first, rows), :],
                    weight.at[pair, pl.ds(into, rows), :],
                    w_sem.at[pair, n],
                )
            )
        return made

    def frame_copies(pair):
        return [
            pltpu.make_async_copy(conv_refs[pair].at[i], conv_buf.at[pair, i], c_sem.at[pair, i])
            for i in range(plan.batches)
        ] + [
            pltpu.make_async_copy(x_refs[pair].at[i], x_buf.at[pair, i], x_sem.at[pair, i])
            for i in range(plan.batches)
        ]

    def grad_copies(b):
        own, other, near, far = g_refs
        moves = []
        for ref, turned in ((own, core), (other, 1 - core)):
            moves.append((ref.at[b], pl.multiple_of(gh + turned * f, gh), f, 0, plan.width))
        width = plan.width // CORES
        for ref, turned in ((near, core), (far, 1 - core)):
            for part in range(CORES):
                piece = ref.at[b, pl.ds(xh + part * gh, gh), :]
                moves.append((piece, pl.multiple_of(turned * (gh + cf), gh), gh, part * width, width))
        return [
            pltpu.make_async_copy(
                source, mg.at[b, pl.ds(row, rows), pl.ds(column, columns)], g_sem.at[b, n]
            )
            for n, (source, row, rows, column, columns) in enumerate(moves)
        ]

    def act_grad(pair, b):
        return lax.dot_general(
            mg[b], weight[pair], (((1,), (1,)), ((), ())), preferred_element_type=jnp.float32
        )

    @pl.when(turn == 0)
    def _():
        for copy in weight_copies(0) + grad_copies(0) + frame_copies(0) + grad_copies(1):
            copy.start()
        for pair in range(1, pairs):
            for copy in weight_copies(pair) + frame_copies(pair):
                copy.start()
        for b in range(plan.batches):
            gs[b, ext:, :] = jnp.zeros((gs.shape[1] - ext, 2 * LANES), jnp.bfloat16)
            tail[b] = jnp.zeros(tail.shape[1:], tail.dtype)
        for copy in weight_copies(0) + grad_copies(0):
            copy.wait()
        ag_first[...] = act_grad(0, 0)
        for copy in frame_copies(0) + grad_copies(1):
            copy.wait()

    for pair in range(pairs):

        @pl.when(turn == pair)
        def _():
            taps[...] = taps_spectrum(t_ref, k_refs[2 * pair : 2 * pair + 2])
            for row, pick in ((0, gain_refs), (8, bias_refs)):
                for side in range(2):
                    lanes = slice(side * LANES, (side + 1) * LANES)
                    flat[row : row + 8, lanes] = jnp.broadcast_to(
                        pick[2 * pair + side][...], (8, LANES)
                    )
            if pair > 0:
                for copy in frame_copies(pair):
                    copy.wait()
            if pair + 1 < pairs:
                for copy in weight_copies(pair + 1):
                    copy.wait()

    gain, bias = flat[:1, :], flat[8:9, :]
    last_rows = cf - (count - 1) * each
    fold = lambda v: jnp.sum(v.reshape(STEP // 8, 8, 2 * LANES), axis=0)
    gain_sum = jnp.zeros((8, 2 * LANES), jnp.float32)
    bias_sum = jnp.zeros((8, 2 * LANES), jnp.float32)
    for b in range(plan.batches):
        live = info[3 + b]
        here, ahead = (ag_first, ag_second) if b == 0 else (ag_second, ag_first)
        following = turn if b == 0 else jnp.minimum(turn + 1, pairs - 1)
        ahead[...] = act_grad(following, 1 - b)
        for j in range(count):
            begin = xh + j * each
            if j < count - 1:
                window = x_buf[turn, b, begin : begin + POINTS, :]
            else:
                tail[b, :last_rows, :] = x_buf[turn, b, begin : begin + last_rows, :]
                window = tail[b]
            xspec[b * count + j] = to_spectrum(segment, window)
        for row in range(0, ext, STEP):
            conv = conv_buf[turn, b, row : row + STEP, :]
            pre = gain * conv + bias
            sig = sigmoid(pre)
            value = here[row : row + STEP, :] * sig * (1.0 + pre * (1.0 - sig))
            position = lax.broadcasted_iota(jnp.int32, value.shape, 0) + (offset - gh + row)
            value = jnp.where(position < live, value, 0.0)
            gs[b, row : row + STEP, :] = (value * gain).astype(jnp.bfloat16)
            if gh <= row < gh + cf:
                gain_sum = gain_sum + fold(value * conv)
                bias_sum = bias_sum + fold(value)
        for j in range(count):
            spec[b * count + j] = to_spectrum(direct, gs[b, j * each : j * each + POINTS, :])
        for j in range(count):
            slot = b * count + j
            spectral_product(spec, taps, parts, slot)
            rows = min(each, cf - j * each)
            value = from_spectrum(inverse, rows, parts, slot)
            position = offset + j * each + lax.broadcasted_iota(jnp.int32, value.shape, 0)
            os[b, j * each : j * each + rows, :] = jnp.where(
                position < live, value, 0.0
            ).astype(jnp.bfloat16)

    for row in range(0, HALF, STEP):
        up, down = slice(row, row + STEP), slice(HALF + row, HALF + row + STEP)
        total_r = total_i = jnp.zeros((STEP, 2 * LANES), jnp.float32)
        for j in range(plan.batches * count):
            re, im, xr, xi = spec[j, up, :], spec[j, down, :], xspec[j, up, :], xspec[j, down, :]
            total_r = total_r + (re * xr + im * xi)
            total_i = total_i + (im * xr - re * xi)
        cross[up, :] = total_r
        cross[down, :] = total_i

    @pl.when(core == 0)
    def _():
        own_ref[0] = os[:, :f]
        send_ref[0] = os[:, f:]

    @pl.when(core != 0)
    def _():
        own_ref[0] = os[:, f:]
        send_ref[0] = os[:, :f]

    high, low = split(cross[...])
    dot = functools.partial(jnp.dot, preferred_element_type=jnp.float32)
    taps_total = dot(lag_ref[0], high) + dot(lag_ref[1], high) + dot(lag_ref[0], low)
    total = [jnp.sum(value, axis=0, keepdims=True) for value in (gain_sum, bias_sum)]
    pad = jnp.zeros((plan.stat_rows - plan.tap_rows - 2, 2 * LANES), jnp.float32)
    total = jnp.concatenate([taps_total] + total + [pad], axis=0)
    if earlier is None:
        stat_ref[0] = total
        return
    for side in range(2):
        lanes = slice(side * LANES, (side + 1) * LANES)
        chip = info[plan.block_slot(steps[0], side) - 2 * turn] // CORES
        stat_ref[chip] = total[:, lanes]
        for n, step in enumerate(earlier):
            chip = info[plan.block_slot(step, side)] // CORES
            stat_ref[chip] = before_ref[n, :, lanes]


def back_call(
    plan, steps, info, grads, sources, arrays, convs, xs, kernel, gain, bias, consts, before, earlier
):
    bt, pairs = plan.batches, len(steps)
    direct, inverse, _, t_back, lags, segment = consts
    wide = 2 * LANES
    slots = bt * plan.back_windows[1]
    any_space = pl.BlockSpec(memory_space=pl.ANY)

    def by_block(shape):
        return [
            pl.BlockSpec(
                shape, lambda p, info, at=plan.block_slot(step, side): (0, info[at]),
                pipeline_mode=pl.Buffered(1),
            )
            for step in steps for side in range(2)
        ]

    frames = (bt, plan.frames, wide)
    each = pl.BlockSpec((1,) + frames, lambda p, info: (p, 0, 0, 0))
    most = max(len(source) for source in sources)
    stat_shape = (pairs, plan.stat_rows, wide)
    stat_spec = pl.BlockSpec((1, plan.stat_rows, wide), lambda p, info: (p, 0, 0))
    if before is None:
        earlier, before = None, jnp.zeros((8, LANES), jnp.float32)
    else:
        stat_shape = (plan.chips, plan.stat_rows, LANES)
        stat_spec = pl.BlockSpec(stat_shape, lambda p, info: (0, 0, 0))
    return pl.pallas_call(
        functools.partial(back_body, plan, steps, earlier, sources),
        grid_spec=pltpu.PrefetchScalarGridSpec(
            num_scalar_prefetch=1,
            grid=(pairs,),
            in_specs=[any_space] * len(grads)
            + by_block((plan.tap_rows, LANES))
            + by_block((1, LANES))
            + by_block((1, LANES))
            + [any_space] * (2 * pairs + len(arrays))
            + [whole(c) for c in (direct, segment, inverse, t_back, lags, before)],
            out_specs=[
                each,
                each,
                stat_spec,
            ],
            scratch_shapes=[
                pltpu.VMEM((pairs, wide, plan.width), jnp.bfloat16),
                pltpu.VMEM((bt, plan.ext, plan.width), jnp.bfloat16),
                pltpu.VMEM((pairs, bt, plan.ext, wide), jnp.float32),
                pltpu.VMEM((pairs, bt, xs[0].shape[1], wide), jnp.bfloat16),
                pltpu.VMEM((plan.ext, wide), jnp.float32),
                pltpu.VMEM((plan.ext, wide), jnp.float32),
                pltpu.VMEM((bt, plan.window_rows(plan.back_windows), wide), jnp.bfloat16),
                pltpu.VMEM((bt, POINTS, wide), jnp.bfloat16),
                pltpu.VMEM((slots, POINTS, wide), jnp.float32),
                pltpu.VMEM((slots, POINTS, wide), jnp.float32),
                pltpu.VMEM((POINTS, wide), jnp.float32),
                pltpu.VMEM((POINTS, wide), jnp.float32),
                pltpu.VMEM((slots, POINTS, wide), jnp.bfloat16),
                pltpu.VMEM((bt, plan.chip_frames, wide), jnp.bfloat16),
                pltpu.VMEM((16, wide), jnp.float32),
                pltpu.SemaphoreType.DMA((pairs, most)),
                pltpu.SemaphoreType.DMA((pairs, bt)),
                pltpu.SemaphoreType.DMA((pairs, bt)),
                pltpu.SemaphoreType.DMA((bt, 2 + 2 * CORES)),
            ],
        ),
        out_shape=[
            jax.ShapeDtypeStruct((pairs,) + frames, jnp.bfloat16),
            jax.ShapeDtypeStruct((pairs,) + frames, jnp.bfloat16),
            jax.ShapeDtypeStruct(stat_shape, jnp.float32),
        ],
        compiler_params=pltpu.CompilerParams(vmem_limit_bytes=VMEM_LIMIT),
        cost_estimate=cost(6.0 * pairs),
        name="back",
    )(info, *grads, *[kernel] * 2 * pairs, *[gain] * 2 * pairs, *[bias] * 2 * pairs,
      *convs, *xs, *arrays, direct, segment, inverse, t_back, lags, before)


def place_body(plan, calls, info, *refs):
    out_ref = refs[-1]
    for i, ref in enumerate(refs[:-1]):
        for turn, step in enumerate(calls[i // 2]):
            for side in range(2):
                block = info[plan.block_slot(step, side)]
                if i % 2:
                    block = block + 1 - 2 * info[0]
                column = pl.multiple_of(block * LANES, LANES)
                lanes = slice(side * LANES, (side + 1) * LANES)
                out_ref[:, :, pl.ds(column, LANES)] = ref[turn, :, :, lanes]


def place_call(plan, calls, info, arrays):
    shape = (plan.batches, plan.frames, plan.width)
    return pl.pallas_call(
        functools.partial(place_body, plan, calls),
        grid_spec=pltpu.PrefetchScalarGridSpec(
            num_scalar_prefetch=1,
            grid=(1,),
            in_specs=[whole(array) for array in arrays],
            out_specs=pl.BlockSpec(shape, lambda g, info: (0, 0, 0)),
        ),
        out_shape=jax.ShapeDtypeStruct(shape, jnp.bfloat16),
        compiler_params=pltpu.CompilerParams(vmem_limit_bytes=VMEM_LIMIT),
        cost_estimate=cost(3.0),
        name="place",
    )(info, *arrays)


def edge_body(plan, x_first, x_last, g_first, g_last, near_ref, far_ref):
    core = lax.axis_index("shard") % CORES

    def take(owner, x_ref, grad_ref):
        for i in range(plan.chips):
            for out, parity in ((near_ref, 1 - owner), (far_ref, owner)):
                column = (CORES * i + parity) * LANES
                out[:, : plan.xhalo, i * LANES : (i + 1) * LANES] = x_ref[
                    :, :, column : column + LANES
                ]
        for part in range(CORES):
            row = plan.xhalo + part * plan.ghalo
            width = plan.width // CORES
            near_ref[:, row : row + plan.ghalo, :] = grad_ref[
                :, :, part * width : (part + 1) * width
            ]

    pl.when(core == 0)(lambda: take(0, x_first, g_first))
    pl.when(core != 0)(lambda: take(1, x_last, g_last))


def edge_call(plan, x, g):
    def spec(rows, first):
        shape = (plan.batches, rows, plan.width)
        block = 0 if first else plan.frames // rows - 1
        return pl.BlockSpec(shape, lambda i: (0, block, 0))

    xh, gh = plan.xhalo, plan.ghalo
    shapes = [
        (plan.batches, rows, plan.width // CORES) for rows in (xh + CORES * gh, xh)
    ]
    return pl.pallas_call(
        functools.partial(edge_body, plan),
        grid=(1,),
        in_specs=[spec(xh, True), spec(xh, False), spec(gh, True), spec(gh, False)],
        out_specs=[pl.BlockSpec(shape, lambda i: (0, 0, 0)) for shape in shapes],
        out_shape=[jax.ShapeDtypeStruct(shape, jnp.bfloat16) for shape in shapes],
        cost_estimate=cost(1.0),
        name="edge",
    )(x, x, g, g)


def after(value, *others):
    return lax.optimization_barrier((value, *others))[0]


def ring_shards(plan, grad_out, saved_input, lengths, kernel, gain, bias, proj_weight):
    index = lax.axis_index("shard")
    group = lax.axis_index("groups")
    core, chip = index % CORES, index // CORES
    place = plan.position_of(chip)
    forward, backward = plan.ring()
    offset = chip * plan.chip_frames
    scale = lax.rsqrt(jnp.sum(lengths).astype(jnp.float32))
    pairs = plan.pairs
    far = jnp.asarray([d for pair in pairs for d in pair], jnp.int32)
    owned = CORES * plan.chip_at((place + far + plan.chips) % plan.chips) + core
    info = jnp.concatenate([jnp.stack([core, offset, group]), lengths, owned]).astype(jnp.int32)
    gain2, bias2 = gain.reshape(1, -1), bias.reshape(1, -1)
    taps = jnp.pad(kernel, ((0, plan.tap_rows - plan.taps), (0, 0)))
    consts = [jnp.asarray(c) for c in transforms(plan)]

    x_near, x_far = edge_call(plan, saved_input, grad_out)
    xa = lax.ppermute(x_near, "shard", plan.edges())
    xb = lax.ppermute(x_far, "shard", plan.edges_like())
    xp = lax.ppermute(saved_input, "shard", plan.partners())
    mgp = lax.ppermute(grad_out, "shard", plan.partners())

    halved = plan.weight_parts == 2
    piece = LANES // 2
    around = {}
    going = [proj_weight] * 2
    if halved:
        going = [lax.dynamic_slice_in_dim(proj_weight, group * piece, piece, 0)] * 2
    xa, xb, taps, info, scale = lax.optimization_barrier((xa, xb, taps, info, scale))

    def weight_round(step):
        going[0] = lax.ppermute(going[0], "shard", forward)
        around[-step] = going[0]
        if step < plan.rounds:
            going[1] = lax.ppermute(going[1], "shard", backward)
            around[step] = going[1]
        else:
            around[step] = around.pop(-step)

    convs, xs, products = [], [], []

    def conv_step(step, order):
        conv, x, *product = conv_call(
            plan, step, order, saved_input, xp, xa, xb, grad_out,
            mgp, taps, gain2, bias2, consts, jnp.bfloat16 if step == 0 else jnp.float32,
        )
        convs.append(conv)
        xs.append(x)
        products.append(product)

    def sum_round(step, send, *behind):
        received = (
            lax.ppermute(send[0], "shard", forward), lax.ppermute(send[1], "shard", backward)
        )
        kinds = (jnp.bfloat16, jnp.bfloat16 if step < plan.rounds - 1 else jnp.float32)
        own = lax.optimization_barrier((*products[step], *received, *behind))[:2]
        return [
            (product + value.astype(jnp.float32)).astype(kind)
            for product, value, kind in zip(own, received, kinds)
        ]

    def wait_for(value):
        going[:] = lax.optimization_barrier((*going, value))[:2]

    weight_round(1)
    conv_step(0, info)
    xc = lax.ppermute(after(xa, products[0][0]), "shard", plan.partners())
    wait_for(products[0][0])
    weight_round(2)
    conv_step(1, after(info, products[0][0]))
    wait_for(products[1][0])
    weight_round(3)
    conv_step(2, after(info, products[1][0]))
    wait_for(products[2][0])
    weight_round(4)
    send = sum_round(1, products[0], products[2][0])
    conv_step(3, after(info, products[2][0], *send))

    arrays = [proj_weight]
    source = {0: [(0, None, 0, LANES)]}

    def keep(array):
        arrays.append(array)
        return len(arrays) - 1

    swap = [
        (g * plan.count + s, (1 - g) * plan.count + s) for g in range(2) for s in range(plan.count)
    ]
    for distances in ([1, -1], [2, -2], [3, -3, 4]):
        if not halved:
            for d in distances:
                source[d] = [(keep(around[d]), None, 0, LANES)]
            continue
        swapped = keep(
            lax.ppermute(
                jnp.concatenate([around[d] for d in distances], 0),
                ("groups", "shard"), swap,
            )
        )
        for i, d in enumerate(distances):
            source[d] = [(keep(around[d]), 0, 0, piece), (swapped, 1, i * piece, piece)]

    calls = [(3, 2), (1, 0)]
    pieces, stats = [], None
    for steps in calls:
        order = after(info, products[-1][0], *send)
        used = sorted({a[0] for step in steps for d in pairs[step] for a in source[d]})
        sources = [
            [
                (used.index(array), part, block, begin, rows)
                for block, d in enumerate(pairs[step])
                for array, part, begin, rows in source[d]
            ]
            for step in steps
        ]
        own, given, stat = back_call(
            plan, steps, order, (grad_out, mgp, xa, xc), sources, [arrays[i] for i in used],
            [convs[step] for step in steps], [xs[step] for step in steps],
            taps, gain2, bias2, consts, stats, calls[0],
        )
        stats = stat
        send = sum_round(2 if steps == calls[0] else 3, send, own)
        pieces += [own, lax.ppermute(given, "shard", plan.partners())]
    groups = [[CORES * p + c for p in range(plan.chips)] for c in range(CORES)]
    shares = lax.all_to_all(stats, "shard", 0, 0, axis_index_groups=groups)
    full = place_call(plan, calls, after(info, stats), pieces)
    summed = jnp.sum(after(shares, full), axis=0) * scale
    recv_f = after(lax.ppermute(send[0], "shard", forward), full, summed)
    proj_grad = (send[1] + recv_f.astype(jnp.float32)) * scale
    return (
        full, proj_grad, summed[: plan.taps], summed[plan.tap_rows : plan.tap_rows + 2]
    )


def shards(count, group_count, grad_out, saved_input, lengths, kernel, gain, bias, proj_weight):
    batches, frames, model_width = grad_out.shape
    plan = Plan(count, group_count, batches, frames, model_width, kernel.shape[0])
    args = (grad_out, saved_input, lengths, kernel, gain, bias, proj_weight)
    return ring_shards(plan, *args) if plan.usable() else plain_shards(*args)


def solution(mesh):
    placed = (
        P("groups", "shard", None),
        P("groups", "shard", None),
        P("groups"),
        P(),
        P(),
        P(),
        P("shard", None),
    )

    def body(*args):
        return shards(mesh.shape["shard"], mesh.shape["groups"], *args)

    return jax.shard_map(
        body,
        mesh=mesh,
        in_specs=placed,
        out_specs=(
            P("groups", "shard", None),
            P(("groups", "shard"), None),
            P("groups", "shard"),
            P("groups", "shard"),
        ),
        check_vma=False,
    )
```
